32 devices in a mesh: groups: 2 (over y), fsdp: 4 (over z), rep: 4 (over x, core).
Axes of the slice: x: 2, y: 2, z: 4, core: 2. Of those that a mesh axis runs over, the one named last changes fastest.
Arguments:
- images: bfloat16 [8, 16, 256, 320], P(('groups', 'rep'), 'fsdp'), parts along dimension 0, may hold values from -60 to 60
- gains: float32 [2, 320], replicated, may hold values from 0.5 to 1.5
- conv_weight: bfloat16 [2880, 320], P('fsdp'), may hold values from -0.109375 to 0.109375
- cotangent: bfloat16 [8, 8, 128, 320], P(('groups', 'rep'), 'fsdp'), parts along dimension 0, may hold values from -60 to 60
Outputs:
- output_maps: bfloat16 [8, 8, 128, 320], P(('groups', 'rep'), 'fsdp'), parts along dimension 0
- input_grad: bfloat16 [8, 16, 256, 320], P(('groups', 'rep'), 'fsdp'), parts along dimension 0
- weight_grad: float32 [5760, 320], P(('groups', 'fsdp')), parts along dimension 0
- gain_grad: float32 [4, 320], P('groups'), parts along dimension 0
The draws below stay inside these ranges and needn't reach their ends.
There are 2 independent parts, one for each index of `groups`. The reference program is written for one: setup_inputs(seed, part) draws one part's arguments, and reference() takes and returns one part's arrays. A program takes and returns all parts, laid end to end along the dimension named above; an argument that names none is the same for every part. Nothing has to cross between parts.
All inputs are finite; a program needn't handle non-finite values.
Results may differ from the reference program's by a relative error of at most 0.0095.
Values may be sent and summed in bfloat16 or wider, within the bound.
A program may use at most 64 MiB of HBM per device.

```python
import math
import jax
import jax.numpy as jnp
from jax import lax

W = 256
C = 320
CO = 320
GROUPS = 32
BATCH = 4
H = 16
HO = 8
WO = 128


def rough_field(key, batch, rows, cols, chans, offset):
    keys = jax.random.split(key, 4)
    position = jnp.arange(rows, dtype=jnp.float32) / rows
    row_scale = jnp.exp(position * math.log(3.0) + jax.random.uniform(keys[0], (rows,), jnp.float32, 0.0, math.log(3.3)))
    chan_scale = jnp.exp(jax.random.uniform(keys[1], (chans,), jnp.float32, math.log(0.5), math.log(2.0)))
    chan_mean = offset * jax.random.uniform(keys[2], (chans,), jnp.float32, -1.0, 1.0)
    noise = jax.random.normal(keys[3], (batch, rows, cols, chans), jnp.float32)
    field = (chan_mean + chan_scale * noise) * row_scale[None, :, None, None]
    return jnp.clip(field, -60.0, 60.0)


def draw_images(key, part):
    return rough_field(jax.random.fold_in(key, 11), BATCH, H, W, C, 1.0).astype(jnp.bfloat16)


def draw_cotangent(key, part):
    return rough_field(jax.random.fold_in(key, 23), BATCH, HO, WO, CO, 0.0).astype(jnp.bfloat16)


def block_scale(rng, dims, cuts, least, largest):
    loudness = 1.0
    for dim, shards_of in cuts:
        heights = jax.random.uniform(jax.random.fold_in(jax.random.fold_in(rng, 6), dim), (shards_of,), jnp.float32, least / len(cuts), largest / len(cuts))
        loudness = loudness * jnp.repeat(jnp.exp(heights), dims[dim] // shards_of).reshape((-1,) + (1,) * (len(dims) - 1 - dim))
    return loudness


def centred(key, shape, spread, limit, cuts=(), kind=jnp.bfloat16):
    drawn = jax.random.normal(key, shape, jnp.float32) * spread
    if len(cuts) > 0:
        drawn = block_scale(key, shape, cuts, -0.22, 0.18) * drawn
    return jnp.clip(drawn, min=-limit, max=limit).astype(kind)


def setup_inputs(seed: int = 0, part: int = 0) -> dict:
    key_list = jax.random.split(jax.random.key(seed), 5)
    part_keys = jax.random.split(jax.random.fold_in(key_list[4], part), 5)
    return {
        "images": draw_images(jax.random.fold_in(jax.random.fold_in(key_list[4], part), 71), part),
        "gains": jnp.clip(jax.random.uniform(key_list[1], (2, C), jnp.float32, 0.5, 1.5), 0.5, 1.5),
        "conv_weight": centred(key_list[2], (9 * C, CO), (9 * C) ** -0.5, 0.109375, ((0, 4),)),
        "cotangent": draw_cotangent(jax.random.fold_in(jax.random.fold_in(key_list[4], part), 71), part),
    }


def conv_full(act, kernel):
    return lax.conv_general_dilated(act, kernel, (2, 2), ((1, 1), (1, 1)), dimension_numbers=('NHWC', 'HWIO', 'NHWC'), precision=lax.Precision.HIGHEST)

def one_image(gains, kernel, pair):
    image, grad_out = pair
    x = image.astype(jnp.float32)[None]
    rows, cols, chans = (x.shape[1], x.shape[2], x.shape[3])
    per_group = chans // GROUPS
    count = rows * cols * per_group
    grouped = x.reshape(1, rows, cols, GROUPS, per_group)
    mean = lax.optimization_barrier(jnp.sum(grouped, axis=(1, 2, 4))) / count
    meansq = lax.optimization_barrier(jnp.sum(grouped * grouped, axis=(1, 2, 4))) / count
    rstd = 1.0 / jnp.sqrt(meansq - mean * mean + 1e-05)
    normed = ((grouped - mean[:, None, None, :, None]) * rstd[:, None, None, :, None]).reshape(x.shape)
    z_val = gains[0] * normed + gains[1]
    act = (z_val * jax.nn.sigmoid(z_val)).astype(jnp.bfloat16)
    result, pullback = jax.vjp(conv_full, act.astype(jnp.float32), kernel)
    act_grad, kernel_grad = pullback(grad_out.astype(jnp.float32)[None])
    sig = jax.nn.sigmoid(z_val)
    z_grad = act_grad * sig * (1.0 + z_val * (1.0 - sig))
    u_sum = lax.optimization_barrier(jnp.sum(z_grad * normed, axis=(1, 2)))
    v_sum = lax.optimization_barrier(jnp.sum(z_grad, axis=(1, 2)))
    su_val = lax.optimization_barrier(jnp.sum((gains[0] * u_sum).reshape(1, GROUPS, per_group), axis=-1))
    sv_val = lax.optimization_barrier(jnp.sum((gains[0] * v_sum).reshape(1, GROUPS, per_group), axis=-1))
    scaled = (gains[0] * z_grad).reshape(grouped.shape)
    normed_g = normed.reshape(grouped.shape)
    dx_val = rstd[:, None, None, :, None] * (scaled - sv_val[:, None, None, :, None] / count - normed_g * su_val[:, None, None, :, None] / count)
    input_grad = dx_val.reshape(x.shape)[0].astype(jnp.bfloat16)
    return (result[0].astype(jnp.bfloat16), input_grad, kernel_grad, jnp.stack([u_sum[0], v_sum[0]]))

def reference(images, gains, conv_weight, cotangent):
    chans = images.shape[3]
    outs_ch = conv_weight.shape[1]
    kernel = conv_weight.astype(jnp.float32).reshape(3, 3, chans, outs_ch)
    output_maps, input_grad, kernel_grads, gain_parts = lax.map(lambda pair: one_image(gains, kernel, pair), (images, cotangent))
    scale = 1.0 / jnp.sqrt(jnp.float32(BATCH * HO * WO))
    weight_grad = lax.optimization_barrier(jnp.sum(kernel_grads, axis=0)).reshape(9 * chans, outs_ch) * scale
    gain_grad = lax.optimization_barrier(jnp.sum(gain_parts, axis=0)) * scale
    return (output_maps, input_grad, weight_grad, gain_grad)
```

```python
import functools

import jax
import jax.numpy as jnp
from jax import lax
from jax.experimental import pallas as pl
from jax.experimental.pallas import tpu as pltpu
from jax.sharding import PartitionSpec as P

GROUPS = 32
MESH = pl.DeviceIdType.MESH


def passed_along(shard, axis, by):
    size = lax.axis_size(axis)
    pairs = [(i, i + by) for i in range(size) if 0 <= i + by < size]
    return lax.ppermute(shard, axis, pairs)


def spread_taps(first, middle, last, axis):
    length = first.shape[axis]
    widths_end = [(0, 0)] * first.ndim
    widths_end[axis] = (0, 1)
    widths_start = [(0, 0)] * first.ndim
    widths_start[axis] = (1, 0)
    even = jnp.pad(first, widths_end) + jnp.pad(last, widths_start)
    odd = jnp.pad(middle, widths_end)
    merged = jnp.stack([even, odd], axis=axis + 1)
    shape = list(even.shape)
    shape[axis] = 2 * (length + 1)
    merged = merged.reshape(shape)
    return lax.slice_in_dim(merged, 0, 2 * length + 1, axis=axis)


def shards(images, gains, conv_weight, cotangent):
    batch, rows, width, chans = images.shape
    outs_ch = conv_weight.shape[1]
    n_fsdp = lax.axis_size("fsdp")
    per_group = chans // GROUPS
    x_val = images.astype(jnp.float32)
    grouped = x_val.reshape(batch, rows, width, GROUPS, per_group)
    part_one = jnp.sum(grouped, axis=(1, 2, 4))
    part_two = jnp.sum(grouped * grouped, axis=(1, 2, 4))
    full_weight = lax.all_gather(conv_weight, "fsdp", axis=0, tiled=True)
    sum_one, sum_two = lax.psum((part_one, part_two), "fsdp")
    count = rows * n_fsdp * width * per_group
    mean = sum_one / count
    rstd = 1.0 / jnp.sqrt(sum_two / count - mean * mean + 1e-05)
    normed_g = (grouped - mean[:, None, None, :, None]) * rstd[:, None, None, :, None]
    normed = normed_g.reshape(x_val.shape)
    z_val = gains[0] * normed + gains[1]
    act = (z_val * jax.nn.sigmoid(z_val)).astype(jnp.bfloat16)
    above = passed_along(act[:, rows - 1 : rows], "fsdp", 1)
    padded = jnp.concatenate([above, act], axis=1)
    kernel = full_weight.reshape(3, 3, chans, outs_ch)
    result = lax.conv_general_dilated(
        padded,
        kernel,
        (2, 2),
        ((0, 0), (1, 0)),
        dimension_numbers=("NHWC", "HWIO", "NHWC"),
        preferred_element_type=jnp.float32,
    )
    output_maps = result.astype(jnp.bfloat16)
    patch_grad = jnp.einsum(
        "bijo,ko->bijk", cotangent, full_weight, preferred_element_type=jnp.float32
    )
    half_rows, half_cols = (cotangent.shape[1], cotangent.shape[2])
    taps = patch_grad.reshape(batch, half_rows, half_cols, 3, 3, chans)
    by_row = [
        spread_taps(
            taps[:, :, :, row_tap, 0], taps[:, :, :, row_tap, 1], taps[:, :, :, row_tap, 2], 2
        )
        for row_tap in range(3)
    ]
    grid = spread_taps(by_row[0], by_row[1], by_row[2], 1)[:, :, 1:]
    from_below = passed_along(grid[:, 0:1].astype(jnp.bfloat16), "fsdp", -1).astype(jnp.float32)
    filler = jnp.zeros((batch, rows - 1, width, chans), jnp.float32)
    act_grad = grid[:, 1:] + jnp.concatenate([filler, from_below], axis=1)
    padded_cols = jnp.pad(padded, ((0, 0), (0, 0), (1, 0), (0, 0)))
    blocks = []
    for row_tap in range(3):
        for col_tap in range(3):
            window = padded_cols[:, row_tap : row_tap + rows : 2, col_tap : col_tap + width : 2]
            blocks.append(
                jnp.einsum("bijc,bijo->co", window, cotangent, preferred_element_type=jnp.float32)
            )
    total_pixels = batch * lax.axis_size("rep") * half_rows * n_fsdp * half_cols
    scale = 1.0 / jnp.sqrt(jnp.float32(total_pixels))
    weight_term = jnp.concatenate(blocks, axis=0) * scale
    sig = jax.nn.sigmoid(z_val)
    z_grad = act_grad * sig * (1.0 + z_val * (1.0 - sig))
    u_part = jnp.sum(z_grad * normed, axis=(1, 2))
    v_part = jnp.sum(z_grad, axis=(1, 2))
    u_sum, v_sum = lax.psum((u_part, v_part), "fsdp")
    gain_term = jnp.stack([jnp.sum(u_sum, axis=0), jnp.sum(v_sum, axis=0)]) * scale
    su_val = jnp.sum((gains[0] * u_sum).reshape(batch, GROUPS, per_group), axis=-1)
    sv_val = jnp.sum((gains[0] * v_sum).reshape(batch, GROUPS, per_group), axis=-1)
    scaled = (gains[0] * z_grad).reshape(grouped.shape)
    dx_val = rstd[:, None, None, :, None] * (
        scaled
        - sv_val[:, None, None, :, None] / count
        - normed_g * su_val[:, None, None, :, None] / count
    )
    input_grad = dx_val.reshape(x_val.shape).astype(jnp.bfloat16)
    owned = lax.psum_scatter(weight_term, "fsdp", scatter_dimension=0, tiled=True)
    weight_grad, gain_grad = (
        lax.psum(owned.astype(jnp.bfloat16), "rep").astype(jnp.float32),
        lax.psum(gain_term.astype(jnp.bfloat16), "rep").astype(jnp.float32),
    )
    return (output_maps, input_grad, weight_grad, gain_grad)


HIGHEST = lax.Precision.HIGHEST


def dot(lhs, rhs, contract=((1,), (0,)), precision=None):
    return lax.dot_general(
        lhs, rhs, (contract, ((), ())), precision=precision, preferred_element_type=jnp.float32
    )


def fused(
    nz,
    x_hbm,
    g_hbm,
    w_hbm,
    ct_hbm,
    out_ref,
    dx_ref,
    wg_ref,
    gg_ref,
    xv,
    gv,
    ctl,
    split,
    same,
    p_out,
    p_in,
    norm,
    dsilu,
    zgrad,
    patches,
    taps,
    edge,
    wfull,
    stat,
    stat_in,
    part,
    core_in,
    half,
    x_in,
    quarter,
    z_in,
    comb,
    final,
    rep_in,
    uv,
    uv_in,
    uvt,
    uvt_in,
    loc_sem,
    halo_sem,
    stat_sem,
    w_send,
    w_recv,
    y_sem,
    c_sem,
    d_sem,
    core_sem,
    x_sem,
    z_sem,
    comb_sem,
    rep_sem,
    uv_sem,
    uvt_sem,
):
    f32, bf16 = jnp.float32, jnp.bfloat16
    rows, chans, width = x_hbm.shape[1:]
    cols = width // 2
    outs_ch, block = w_hbm.shape
    q_rows = outs_ch // 4
    h_rows = outs_ch // 2
    lanes = part.shape[3]
    sizes = [lanes, block - lanes]
    w_cut = [(0, -(-q_rows // 32) * 16)]
    w_cut.append((w_cut[0][1], q_rows - w_cut[0][1]))
    count = rows * nz * width * (chans // GROUPS)
    scale = 1.0 / jnp.sqrt(f32(4 * nz * ct_hbm.shape[1] * cols))
    z = lax.axis_index("fsdp")
    rep = lax.axis_index("rep")
    yi = lax.axis_index("groups")
    xi, ci = rep // 2, rep % 2
    mine = 2 * ci + xi
    peers_z = [lax.rem(z + d, nz) for d in range(1, nz)]
    reps = [(2 * xi + 1 - ci), (2 * (1 - xi) + ci), (2 * (1 - xi) + 1 - ci)]
    core_peer, x_peer = reps[0], reps[1]
    pair = z // 2
    partner = z + 1 - 2 * (z % 2)
    inner = jnp.logical_or(z == 1, z == 2)
    outer = jnp.logical_or(z == 0, z == 3)
    order = [3 * (1 - pair), 2 - pair, partner, z]
    others = [partner, 2 - pair, 3 * (1 - pair)]

    def aligned(value):
        return pl.multiple_of(value, 16)

    def remote(src, dst, send, recv, device):
        return pltpu.make_async_remote_copy(
            src_ref=src,
            dst_ref=dst,
            send_sem=send,
            recv_sem=recv,
            device_id=device,
            device_id_type=MESH,
        )

    barrier = pltpu.get_barrier_semaphore()
    for peer in peers_z:
        pl.semaphore_signal(barrier, inc=1, device_id={"fsdp": peer}, device_id_type=MESH)
    for peer in reps:
        pl.semaphore_signal(barrier, inc=1, device_id={"rep": peer}, device_id_type=MESH)
    pl.semaphore_signal(barrier, inc=1, device_id={"groups": 1 - yi}, device_id_type=MESH)

    x_local = [pltpu.make_async_copy(x_hbm.at[0, r], xv.at[r], loc_sem.at[r]) for r in range(rows)]
    g_local = pltpu.make_async_copy(g_hbm, gv, loc_sem.at[rows])
    w_local = pltpu.make_async_copy(w_hbm, wfull.at[z], loc_sem.at[rows + 1])
    c_local = [
        pltpu.make_async_copy(
            ct_hbm.at[0, i], ctl.at[k, :, pl.ds(i * cols, cols)], loc_sem.at[rows + 2 + n]
        )
        for n, (k, i) in enumerate([(1, 0), (1, 1), (0, 1)])
    ]
    for cp in x_local + c_local + [w_local, g_local]:
        cp.start()

    big_i = lax.broadcasted_iota(jnp.int32, (width, width), 0)
    big_j = lax.broadcasted_iota(jnp.int32, (width, width), 1)
    split[...] = jnp.where(
        jnp.where(big_j < cols, 2 * big_j, 2 * (big_j - cols) + 1) == big_i, 1.0, 0.0
    ).astype(bf16)
    inv = 1.0 / (chans // GROUPS)
    lane = lax.broadcasted_iota(jnp.int32, (chans, cols), 1)
    wide = same.shape[1] // 3
    ch_i = lax.broadcasted_iota(jnp.int32, (chans, wide), 0)
    ch_j = lax.broadcasted_iota(jnp.int32, (chans, wide), 1)
    grp_i = jnp.floor((ch_i.astype(f32) + 0.5) * inv)
    grp_j = jnp.floor((ch_j.astype(f32) + 0.5) * inv)
    same_one = jnp.where(jnp.where(ch_j < chans, grp_j, -1.0) == grp_i, 1.0, 0.0).astype(bf16)
    for k in range(3):
        same[:, k * wide : (k + 1) * wide] = same_one
    sums_i = lax.broadcasted_iota(jnp.int32, (8, width), 0)
    sums_j = lax.broadcasted_iota(jnp.int32, (8, width), 1)
    halves = jnp.where(jnp.where(sums_j < cols, 0, 4) == sums_i - lax.rem(sums_i, 4), 1.0, 0.0)
    halves = halves.astype(bf16)

    def three_terms(value):
        high = value.astype(bf16)
        rest = value - high.astype(f32)
        middle = rest.astype(bf16)
        low = (rest - middle.astype(f32)).astype(bf16)
        return high, middle, low

    def row_sums(first, second):
        both = jnp.concatenate([first, second], axis=1)
        terms = [dot(halves, term, ((1,), (1,))) for term in three_terms(both)]
        return terms[0] + (terms[1] + terms[2])

    def group_sums(total):
        pad = jnp.zeros((8, wide - chans), f32)
        terms = three_terms(jnp.concatenate([total, pad], axis=1))
        spread = jnp.concatenate(terms, axis=1).astype(f32)
        first = jnp.broadcast_to(spread[0:1], (cols, 3 * wide))
        second = jnp.broadcast_to(spread[4:5], (cols, 3 * wide))
        rhs = jnp.concatenate([first, second], axis=0).astype(bf16)
        sums = dot(same[...], rhs, ((1,), (1,)))
        return sums[:, :cols], sums[:, cols:]

    @pl.when(z == nz - 1)
    def _():
        ctl[0, :, :cols] = jnp.zeros((chans, cols), bf16)

    pl.semaphore_wait(barrier, nz - 1 + 3 + 1)

    halo_c = remote(
        ct_hbm.at[0, 0],
        ctl.at[0, :, pl.ds(0, cols)],
        halo_sem.at[0, 0],
        halo_sem.at[0, 1],
        {"fsdp": lax.rem(z + nz - 1, nz)},
    )
    p_copy = remote(
        p_out, p_in, halo_sem.at[1, 0], halo_sem.at[1, 1], {"fsdp": lax.rem(z + 1, nz)}
    )

    w_off = q_rows * (2 * ci + yi)

    def w_spot(q, y_from, c):
        start, size = w_cut[c]
        return wfull.at[q, pl.ds(aligned(q_rows * (2 * ci + y_from) + start), size)]

    def own_w(up, c):
        start, size = w_cut[c]
        to = lax.rem(z + (1 if up else nz - 1), nz)
        return remote(
            w_hbm.at[pl.ds(aligned(w_off + start), size)],
            w_spot(z, yi, c),
            w_send.at[1 if up else 0, c],
            w_recv.at[z, c],
            {"fsdp": to},
        )

    def when_up(act):
        pl.when(z < nz - 1)(act)

    def when_down(act):
        pl.when(z > 0)(act)

    when_down(lambda: halo_c.start())
    when_up(lambda: own_w(True, 0).start())

    sum_one = jnp.zeros((chans, cols), f32)
    sum_two = jnp.zeros((chans, cols), f32)
    for r in range(rows):
        x_local[r].wait()
        x_val = dot(xv[r], split[...])
        norm[r + 1] = x_val
        even, odd = x_val[:, :cols], x_val[:, cols:]
        sum_one = sum_one + (even + odd)
        sum_two = sum_two + (even * even + odd * odd)
    stat[...] = row_sums(sum_one, sum_two)

    stat_cp = [
        remote(stat, stat_in.at[d], stat_sem.at[d, 0], stat_sem.at[d, 1], {"fsdp": peers_z[d]})
        for d in range(nz - 1)
    ]
    for d in (1, 0, 2):
        stat_cp[d].start()

    eye_i = lax.broadcasted_iota(jnp.int32, (chans, chans), 0)
    eye_j = lax.broadcasted_iota(jnp.int32, (chans, chans), 1)
    eye = jnp.where(eye_i == eye_j, 1.0, 0.0)
    g_local.wait()
    gains = dot(eye, gv[...], ((1,), (1,)), HIGHEST)
    gain = jnp.broadcast_to(gains[:, 0:1], (chans, cols))
    shift = jnp.broadcast_to(gains[:, 1:2], (chans, cols))

    def block_taps(q):
        here = pl.ds(aligned(q * block), block)
        taps[here] = dot(wfull[q], ctl[1], ((0,), (0,)))

    for cp in c_local:
        cp.wait()
    w_local.wait()
    block_taps(z)

    for cp in stat_cp:
        cp.wait_recv()
    total = stat[...]
    for d in range(nz - 1):
        total = total + stat_in[d]
    when_up(lambda: own_w(True, 1).start())

    @pl.when(z > 0)
    def _():
        own_w(False, 0).start()
        own_w(False, 1).start()

    sum_one, sum_two = group_sums(total)
    mean = sum_one / count
    rstd = 1.0 / jnp.sqrt(sum_two / count - mean * mean + 1e-05)
    slope = gain * rstd

    def put(row_tap, col_tap, i, lo, value):
        start = (3 * row_tap + col_tap) * chans + lo
        patches[start : start + value.shape[0], i * cols : (i + 1) * cols] = value

    step = 64

    def activate(r, users):
        for lo in range(0, chans, step):
            part_of = slice(lo, lo + step)
            for odd in range(2):
                here = pl.ds(odd * cols, cols)
                x_val = norm[r, part_of, here]
                z_val = (x_val - mean[part_of]) * slope[part_of] + shift[part_of]
                sig = 0.5 * jnp.tanh(0.5 * z_val) + 0.5
                act = z_val * sig
                dsilu[r - 1, part_of, here] = sig
                rounded = act.astype(bf16)
                for t, i in users:
                    put(t, 1 + odd, i, lo, rounded)
                if odd == 1:
                    moved = pltpu.roll(act, 1, axis=1)
                    moved = jnp.where(lane[part_of] == 0, 0.0, moved).astype(bf16)
                    for t, i in users:
                        put(t, 0, i, lo, moved)

    activate(1, [(1, 0)])
    activate(3, [(1, 1)])
    activate(2, [(2, 0), (0, 1)])
    activate(4, [(2, 1), (0, 0)])

    when_up(lambda: halo_c.wait_recv())

    def w_arrive(j, c, role):
        @pl.when(role)
        def _():
            q = others[j]
            spot = w_spot(q, yi, c)
            remote(spot, spot, w_send.at[2 + j, c], w_recv.at[q, c], {"fsdp": partner}).wait_recv()
            if role is inner:
                to = 3 - z if j == 0 else partner
                remote(spot, spot, w_send.at[2 + j, c], w_recv.at[q, c], {"fsdp": to}).start()
            y_forward(j, c).start()
            c_forward(j, c).start()

    def y_forward(j, c):
        spot = w_spot(others[j], yi, c)
        return remote(spot, spot, y_sem.at[j, c, 0], y_sem.at[j, c, 1], {"groups": 1 - yi})

    def c_forward(j, c):
        spot = w_spot(others[j], yi, c)
        return remote(spot, spot, c_sem.at[j, c, 0], c_sem.at[j, c, 1], {"rep": core_peer})

    def d_forward(j, c):
        spot = w_spot(others[j], 1 - yi, c)
        return remote(spot, spot, d_sem.at[j, c, 0], d_sem.at[j, c, 1], {"rep": core_peer})

    def w_second(j, c):
        y_forward(j, c).wait_recv()
        d_forward(j, c).start()

    def w_taps(j):
        for c in range(2):
            c_forward(j, c).wait_recv()
            d_forward(j, c).wait_recv()
        block_taps(others[j])

    def core_copy(n, h):
        return remote(
            part.at[n, h, pl.ds(aligned(h_rows * (1 - ci)), h_rows)],
            core_in.at[n, h],
            core_sem.at[n, h, 0],
            core_sem.at[n, h, 1],
            {"rep": core_peer},
        )

    def x_copy(n, h):
        return remote(
            half.at[n, h, pl.ds(aligned(q_rows * (1 - xi)), q_rows)],
            x_in.at[n, h],
            x_sem.at[n, h, 0],
            x_sem.at[n, h, 1],
            {"rep": x_peer},
        )

    def z_copy(n, h):
        return remote(
            quarter.at[n, h],
            z_in.at[n, h],
            z_sem.at[n, h, 0],
            z_sem.at[n, h, 1],
            {"fsdp": partner},
        )

    def comb_copy(n, h):
        return remote(
            comb.at[n, h],
            z_in.at[3, h],
            comb_sem.at[n, h],
            z_sem.at[3, h, 1],
            {"fsdp": order[n]},
        )

    def weight_step(n, h):
        q, size = order[n], sizes[h]
        rhs = patches[pl.ds(aligned(q * block + h * lanes), size)]
        lhs = ctl[jnp.where(q == 0, 0, 1)]
        part[n, h, :, :size] = dot(lhs, rhs, ((1,), (1,))).astype(bf16)
        if h == 0 and n > 0:
            taken = 3 * chans - block

            @pl.when(q == 1)
            def _():
                rhs = patches[block : block + taken]
                part[n, h, :, :taken] = dot(ctl[0], rhs, ((1,), (1,))).astype(bf16)

        core_copy(n, h).start()

    def core_step(n, h):
        core_copy(n, h).wait_recv()
        mine_rows = part[n, h, pl.ds(aligned(h_rows * ci), h_rows)]
        half[n, h] = (mine_rows.astype(f32) + core_in[n, h].astype(f32)).astype(bf16)
        x_copy(n, h).start()

    def x_step(n, h):
        x_copy(n, h).wait_recv()
        mine_rows = half[n, h, pl.ds(aligned(q_rows * xi), q_rows)]
        quarter[n, h] = (mine_rows.astype(f32) + x_in[n, h].astype(f32)).astype(bf16)
        if n == 2:
            z_copy(n, h).start()
        elif n < 2:
            pl.when(outer)(lambda: z_copy(n, h).start())

    def comb_step(n, h):
        @pl.when(inner)
        def _():
            z_copy(n, h).wait_recv()
            value = quarter[n, h].astype(f32) + z_in[n, h].astype(f32)
            comb[n, h] = value.astype(bf16)
            comb_copy(n, h).start()

    def rep_copy(m, h):
        src = final.at[h] if m < 2 else rep_in.at[1, h]
        to = core_peer if m == 2 else reps[m]
        return remote(
            src, rep_in.at[m, h], rep_sem.at[m, h, 0], rep_sem.at[m, h, 1], {"rep": to}
        )

    def place(ref, k, h):
        rows_k = pl.ds(aligned(q_rows * k), q_rows)
        wg_ref[rows_k, h * lanes : h * lanes + sizes[h]] = ref[:, : sizes[h]].astype(f32)

    def final_step(h):
        z_copy(2, h).wait_recv()
        comb_copy(1, h).wait_recv()
        value = quarter[3, h].astype(f32) + z_in[2, h].astype(f32) + z_in[3, h].astype(f32)
        final[h] = (value * scale).astype(bf16)
        rep_copy(1, h).start()
        rep_copy(0, h).start()

    def relay_step(h):
        rep_copy(1, h).wait_recv()
        rep_copy(2, h).start()

    def prepare():
        for r in range(rows):
            for odd in range(2):
                here = pl.ds(odd * cols, cols)
                normed = (norm[r + 1, :, here] - mean) * rstd
                z_val = gain * normed + shift
                sig = dsilu[r, :, here]
                norm[r + 1, :, here] = normed
                dsilu[r, :, here] = sig * (1.0 + z_val * (1.0 - sig))

    w_lane = lax.broadcasted_iota(jnp.int32, (outs_ch, block), 1)
    top = 3 * chans - block
    upto, since = -(-top // 128) * 128, top // 128 * 128

    def top_maps():
        first = jnp.where(w_lane[:, :upto] < top, wfull[1, :, :upto].astype(f32), 0.0).astype(bf16)
        value = dot(wfull[0], patches[:block]) + dot(first, patches[block : block + upto])
        p_out[...] = value[:, :cols].astype(bf16)
        when_up(lambda: p_copy.start())
        return value[:, cols:]

    def low_maps(above):
        rest = wfull[1, :, since:].astype(f32)
        rest = jnp.where(w_lane[:, since:] < top, 0.0, rest).astype(bf16)
        value = dot(rest, patches[block + since : 2 * block])
        for q in range(2, nz):
            value = value + dot(wfull[q], patches[q * block : (q + 1) * block])
        out_ref[0, 1] = (value[:, cols:] + above).astype(bf16)
        return value[:, :cols]

    def join_maps(value):
        @pl.when(z == 0)
        def _():
            p_in[...] = jnp.zeros(p_in.shape, bf16)

        when_down(lambda: p_copy.wait_recv())
        out_ref[0, 0] = (value + p_in[...].astype(f32)).astype(bf16)

    def edge_taps():
        below = ctl[0, :, :cols]
        done = 0
        q = 0
        while done < 3 * chans:
            take = min(block, 3 * chans - done)
            edge[done : done + take] = dot(wfull[q, :, :take], below, ((0,), (0,)))
            done += take
            q += 1

    def tap_at(row_tap, col_tap, i):
        tap = 3 * row_tap + col_tap
        here = slice(tap * chans, (tap + 1) * chans)
        if i == 2:
            return edge[here]
        return taps[here, i * cols : (i + 1) * cols]

    uv_cp = [
        remote(uv, uv_in.at[d], uv_sem.at[d, 0], uv_sem.at[d, 1], {"fsdp": peers_z[d]})
        for d in range(nz - 1)
    ]

    def channel_sums():
        u_sum = jnp.zeros((chans, cols), f32)
        v_sum = jnp.zeros((chans, cols), f32)
        for r in range(rows):
            pairs = [(t, i) for i in range(3) for t in range(3) if 2 * i + t == r + 1]
            for odd in range(2):
                here = pl.ds(odd * cols, cols)
                grad = sum(tap_at(t, 1 + odd, i) for t, i in pairs)
                if odd == 1:
                    left = sum(tap_at(t, 0, i) for t, i in pairs)
                    moved = pltpu.roll(left, cols - 1, axis=1)
                    grad = grad + jnp.where(lane == cols - 1, 0.0, moved)
                value = grad * dsilu[r, :, here]
                zgrad[r, :, here] = value
                u_sum = u_sum + value * norm[r + 1, :, here]
                v_sum = v_sum + value
        uv[...] = row_sums(u_sum, v_sum)
        for d in (1, 0, 2):
            uv_cp[d].start()

    uvt_cp = [
        remote(uvt, uvt_in.at[m], uvt_sem.at[m, 0], uvt_sem.at[m, 1], {"rep": reps[m]})
        for m in range(3)
    ]

    def input_grads():
        for cp in uv_cp:
            cp.wait_recv()
        total = uv[...]
        for d in range(nz - 1):
            total = total + uv_in[d]
        uvt[...] = total
        for cp in uvt_cp:
            cp.start()
        su_val, sv_val = group_sums(gv[0:1] * total)
        su_val, sv_val = su_val / count, sv_val / count
        merge = jnp.where(
            jnp.where(big_i < cols, 2 * big_i, 2 * (big_i - cols) + 1) == big_j, 1.0, 0.0
        ).astype(bf16)
        for r in range(rows):
            for odd in range(2):
                here = pl.ds(odd * cols, cols)
                value = rstd * (gain * zgrad[r, :, here] - sv_val - norm[r + 1, :, here] * su_val)
                patches[r * chans : (r + 1) * chans, here] = value.astype(bf16)
            dx_ref[0, r] = dot(patches[r * chans : (r + 1) * chans], merge).astype(bf16)

    weight_step(0, 0)
    weight_step(0, 1)
    weight_step(1, 0)
    weight_step(1, 1)
    core_step(0, 0)
    w_arrive(0, 0, inner)
    w_arrive(1, 0, inner)
    w_arrive(0, 0, outer)
    weight_step(2, 0)
    core_step(0, 1)
    weight_step(2, 1)
    core_step(1, 0)
    w_arrive(0, 1, inner)
    w_arrive(1, 1, inner)
    w_arrive(0, 1, outer)
    weight_step(3, 0)
    core_step(1, 1)
    weight_step(3, 1)
    core_step(2, 0)
    core_step(2, 1)
    core_step(3, 0)
    core_step(3, 1)
    prepare()
    x_step(0, 0)
    w_arrive(2, 0, inner)
    w_arrive(1, 0, outer)
    w_second(0, 0)
    w_second(0, 1)
    x_step(0, 1)
    w_arrive(2, 1, inner)
    w_arrive(1, 1, outer)
    w_taps(0)
    comb_step(0, 0)
    x_step(1, 0)
    w_second(1, 0)
    w_second(1, 1)
    w_arrive(2, 0, outer)
    comb_step(0, 1)
    x_step(1, 1)
    w_taps(1)
    w_arrive(2, 1, outer)
    comb_step(1, 0)
    x_step(2, 0)
    w_second(2, 0)
    comb_step(1, 1)
    x_step(2, 1)
    w_second(2, 1)
    w_taps(2)
    x_step(3, 0)
    edge_taps()
    final_step(0)
    channel_sums()
    x_step(3, 1)
    final_step(1)
    above = top_maps()
    low = low_maps(above)
    relay_step(0)
    relay_step(1)
    input_grads()
    join_maps(low)

    owners = [2 * (1 - ci) + xi, 2 * ci + 1 - xi, 2 * (1 - ci) + 1 - xi]
    for h in range(2):
        place(final.at[h], mine, h)
        for m in (1, 0, 2):
            if m != 1:
                rep_copy(m, h).wait_recv()
            place(rep_in.at[m, h], owners[m], h)
    for cp in uvt_cp:
        cp.wait_recv()
    total = uvt[...] + uvt_in[0] + uvt_in[1] + uvt_in[2]
    gg_ref[0:1] = total[0:1] * scale
    gg_ref[1:2] = total[4:5] * scale

    @pl.when(z < nz - 1)
    def _():
        p_copy.wait_send()
        own_w(True, 0).wait_send()
        own_w(True, 1).wait_send()

    @pl.when(z > 0)
    def _():
        halo_c.wait_send()
        own_w(False, 0).wait_send()
        own_w(False, 1).wait_send()

    for cp in stat_cp + uv_cp + uvt_cp:
        cp.wait_send()
    for h in range(2):
        for j in range(3):
            y_forward(j, h).wait_send()
            c_forward(j, h).wait_send()
            d_forward(j, h).wait_send()
            rep_copy(j, h).wait_send()
        for n in range(4):
            core_copy(n, h).wait_send()
            x_copy(n, h).wait_send()
        z_copy(2, h).wait_send()

    @pl.when(inner)
    def _():
        for h in range(2):
            for j in range(3):
                spot = w_spot(others[j], yi, h)
                to = 3 - z if j == 0 else partner
                remote(
                    spot, spot, w_send.at[2 + j, h], w_recv.at[others[j], h], {"fsdp": to}
                ).wait_send()
            for n in range(2):
                comb_copy(n, h).wait_send()

    @pl.when(outer)
    def _():
        for h in range(2):
            for n in range(2):
                z_copy(n, h).wait_send()


def write_out(*refs):
    n = len(refs) // 2
    sems = refs[-1]
    copies = [pltpu.make_async_copy(refs[i], refs[n + i], sems.at[i]) for i in range(n)]
    for cp in copies:
        cp.start()
    for cp in copies:
        cp.wait()


def in_hbm(value):
    return pltpu.with_memory_space_constraint(value, pltpu.HBM)


def fused_shards(images, gains, conv_weight, cotangent):
    batch, rows, width, chans = images.shape
    block, outs_ch = conv_weight.shape
    nz = lax.axis_size("fsdp")
    fits = (batch, rows, cotangent.shape[1]) == (1, 4, 2) and chans % 64 == 0 and width == 256
    if not fits or block % 16 or outs_ch % 64 or nz * block != 9 * chans:
        return shards(images, gains, conv_weight, cotangent)
    if not block < 3 * chans < 2 * block or 3 * chans - block > 384:
        return shards(images, gains, conv_weight, cotangent)
    cols = width // 2
    q_rows = outs_ch // 4
    lanes = -(-block // 256) * 128
    wide = -(-chans // 128) * 128
    f32, bf16 = jnp.float32, jnp.bfloat16
    vmem = pltpu.VMEM
    dma = pltpu.SemaphoreType.DMA
    shapes = (
        jax.ShapeDtypeStruct((batch, rows // 2, outs_ch, cols), bf16),
        jax.ShapeDtypeStruct((batch, rows, chans, width), bf16),
        jax.ShapeDtypeStruct((outs_ch, block), f32),
        jax.ShapeDtypeStruct(gains.shape, f32),
    )
    results = pl.pallas_call(
        functools.partial(fused, nz),
        out_shape=tuple(vmem(shape.shape, shape.dtype) for shape in shapes),
        in_specs=[pl.BlockSpec(memory_space=pltpu.HBM)] * 4,
        out_specs=[pl.BlockSpec(memory_space=vmem)] * 4,
        scratch_shapes=[
            vmem((rows, chans, width), bf16),
            vmem(gains.shape, f32),
            vmem((2, outs_ch, width), bf16),
            vmem((width, width), bf16),
            vmem((chans, 3 * wide), bf16),
            vmem((outs_ch, cols), bf16),
            vmem((outs_ch, cols), bf16),
            vmem((rows + 1, chans, width), f32),
            vmem((rows, chans, width), f32),
            vmem((rows, chans, width), f32),
            vmem((nz * block, width), bf16),
            vmem((nz * block, width), f32),
            vmem((3 * chans, cols), f32),
            vmem((nz, outs_ch, block), bf16),
            vmem((8, chans), f32),
            vmem((nz - 1, 8, chans), f32),
            vmem((nz, 2, outs_ch, lanes), bf16),
            vmem((nz, 2, 2 * q_rows, lanes), bf16),
            vmem((nz, 2, 2 * q_rows, lanes), bf16),
            vmem((nz, 2, q_rows, lanes), bf16),
            vmem((nz, 2, q_rows, lanes), bf16),
            vmem((4, 2, q_rows, lanes), bf16),
            vmem((2, 2, q_rows, lanes), bf16),
            vmem((2, q_rows, lanes), bf16),
            vmem((3, 2, q_rows, lanes), bf16),
            vmem((8, chans), f32),
            vmem((nz - 1, 8, chans), f32),
            vmem((8, chans), f32),
            vmem((3, 8, chans), f32),
            dma((rows + 5,)),
            dma((2, 2)),
            dma((nz - 1, 2)),
            dma((5, 2)),
            dma((nz, 2)),
            dma((3, 2, 2)),
            dma((3, 2, 2)),
            dma((3, 2, 2)),
            dma((nz, 2, 2)),
            dma((nz, 2, 2)),
            dma((4, 2, 2)),
            dma((2, 2)),
            dma((3, 2, 2)),
            dma((nz - 1, 2)),
            dma((3, 2)),
        ],
        compiler_params=pltpu.CompilerParams(
            collective_id=0, has_side_effects=True, vmem_limit_bytes=48 * 1024 * 1024
        ),
    )(
        in_hbm(jnp.swapaxes(images, 2, 3)),
        in_hbm(gains),
        in_hbm(conv_weight.T),
        in_hbm(jnp.swapaxes(cotangent, 2, 3)),
    )
    output_maps, input_grad, weight_grad, gain_grad = pl.pallas_call(
        write_out,
        out_shape=shapes,
        in_specs=[pl.BlockSpec(memory_space=vmem)] * 4,
        out_specs=[pl.BlockSpec(memory_space=pltpu.HBM)] * 4,
        scratch_shapes=[dma((4,))],
        compiler_params=pltpu.CompilerParams(vmem_limit_bytes=1024 * 1024),
    )(*(pltpu.with_memory_space_constraint(value, vmem) for value in results))
    return (
        jnp.swapaxes(output_maps, 2, 3),
        jnp.swapaxes(input_grad, 2, 3),
        weight_grad.T,
        gain_grad,
    )


def solution(mesh):
    in_specs = (
        P(("groups", "rep"), "fsdp", None, None),
        P(),
        P("fsdp", None),
        P(("groups", "rep"), "fsdp", None, None),
    )
    out_specs = (
        P(("groups", "rep"), "fsdp", None, None),
        P(("groups", "rep"), "fsdp", None, None),
        P(("groups", "fsdp"), None),
        P("groups", None),
    )
    small = mesh.shape["groups"] == 2 and mesh.shape["rep"] == 4 and mesh.shape["fsdp"] == 4
    body = fused_shards if small else shards
    return jax.shard_map(body, mesh=mesh, in_specs=in_specs, out_specs=out_specs, check_vma=False)
```

```python
import functools

import jax
import jax.numpy as jnp
from jax import lax
from jax.experimental import pallas as pl
from jax.experimental.pallas import tpu as pltpu
from jax.sharding import PartitionSpec as P

GROUPS = 32
MESH = pl.DeviceIdType.MESH


def passed_along(shard, axis, by):
    size = lax.axis_size(axis)
    pairs = [(i, i + by) for i in range(size) if 0 <= i + by < size]
    return lax.ppermute(shard, axis, pairs)


def spread_taps(first, middle, last, axis):
    length = first.shape[axis]
    widths_end = [(0, 0)] * first.ndim
    widths_end[axis] = (0, 1)
    widths_start = [(0, 0)] * first.ndim
    widths_start[axis] = (1, 0)
    even = jnp.pad(first, widths_end) + jnp.pad(last, widths_start)
    odd = jnp.pad(middle, widths_end)
    merged = jnp.stack([even, odd], axis=axis + 1)
    shape = list(even.shape)
    shape[axis] = 2 * (length + 1)
    merged = merged.reshape(shape)
    return lax.slice_in_dim(merged, 0, 2 * length + 1, axis=axis)


def shards(images, gains, conv_weight, cotangent):
    batch, rows, width, chans = images.shape
    outs_ch = conv_weight.shape[1]
    n_fsdp = lax.axis_size("fsdp")
    per_group = chans // GROUPS
    x_val = images.astype(jnp.float32)
    grouped = x_val.reshape(batch, rows, width, GROUPS, per_group)
    part_one = jnp.sum(grouped, axis=(1, 2, 4))
    part_two = jnp.sum(grouped * grouped, axis=(1, 2, 4))
    full_weight = lax.all_gather(conv_weight, "fsdp", axis=0, tiled=True)
    sum_one, sum_two = lax.psum((part_one, part_two), "fsdp")
    count = rows * n_fsdp * width * per_group
    mean = sum_one / count
    rstd = 1.0 / jnp.sqrt(sum_two / count - mean * mean + 1e-05)
    normed_g = (grouped - mean[:, None, None, :, None]) * rstd[:, None, None, :, None]
    normed = normed_g.reshape(x_val.shape)
    z_val = gains[0] * normed + gains[1]
    act = (z_val * jax.nn.sigmoid(z_val)).astype(jnp.bfloat16)
    above = passed_along(act[:, rows - 1 : rows], "fsdp", 1)
    padded = jnp.concatenate([above, act], axis=1)
    kernel = full_weight.reshape(3, 3, chans, outs_ch)
    result = lax.conv_general_dilated(
        padded,
        kernel,
        (2, 2),
        ((0, 0), (1, 0)),
        dimension_numbers=("NHWC", "HWIO", "NHWC"),
        preferred_element_type=jnp.float32,
    )
    output_maps = result.astype(jnp.bfloat16)
    patch_grad = jnp.einsum(
        "bijo,ko->bijk", cotangent, full_weight, preferred_element_type=jnp.float32
    )
    half_rows, half_cols = (cotangent.shape[1], cotangent.shape[2])
    taps = patch_grad.reshape(batch, half_rows, half_cols, 3, 3, chans)
    by_row = [
        spread_taps(
            taps[:, :, :, row_tap, 0], taps[:, :, :, row_tap, 1], taps[:, :, :, row_tap, 2], 2
        )
        for row_tap in range(3)
    ]
    grid = spread_taps(by_row[0], by_row[1], by_row[2], 1)[:, :, 1:]
    from_below = passed_along(grid[:, 0:1].astype(jnp.bfloat16), "fsdp", -1).astype(jnp.float32)
    filler = jnp.zeros((batch, rows - 1, width, chans), jnp.float32)
    act_grad = grid[:, 1:] + jnp.concatenate([filler, from_below], axis=1)
    padded_cols = jnp.pad(padded, ((0, 0), (0, 0), (1, 0), (0, 0)))
    blocks = []
    for row_tap in range(3):
        for col_tap in range(3):
            window = padded_cols[:, row_tap : row_tap + rows : 2, col_tap : col_tap + width : 2]
            blocks.append(
                jnp.einsum("bijc,bijo->co", window, cotangent, preferred_element_type=jnp.float32)
            )
    total_pixels = batch * lax.axis_size("rep") * half_rows * n_fsdp * half_cols
    scale = 1.0 / jnp.sqrt(jnp.float32(total_pixels))
    weight_term = jnp.concatenate(blocks, axis=0) * scale
    sig = jax.nn.sigmoid(z_val)
    z_grad = act_grad * sig * (1.0 + z_val * (1.0 - sig))
    u_part = jnp.sum(z_grad * normed, axis=(1, 2))
    v_part = jnp.sum(z_grad, axis=(1, 2))
    u_sum, v_sum = lax.psum((u_part, v_part), "fsdp")
    gain_term = jnp.stack([jnp.sum(u_sum, axis=0), jnp.sum(v_sum, axis=0)]) * scale
    su_val = jnp.sum((gains[0] * u_sum).reshape(batch, GROUPS, per_group), axis=-1)
    sv_val = jnp.sum((gains[0] * v_sum).reshape(batch, GROUPS, per_group), axis=-1)
    scaled = (gains[0] * z_grad).reshape(grouped.shape)
    dx_val = rstd[:, None, None, :, None] * (
        scaled
        - sv_val[:, None, None, :, None] / count
        - normed_g * su_val[:, None, None, :, None] / count
    )
    input_grad = dx_val.reshape(x_val.shape).astype(jnp.bfloat16)
    owned = lax.psum_scatter(weight_term, "fsdp", scatter_dimension=0, tiled=True)
    weight_grad, gain_grad = (
        lax.psum(owned.astype(jnp.bfloat16), "rep").astype(jnp.float32),
        lax.psum(gain_term.astype(jnp.bfloat16), "rep").astype(jnp.float32),
    )
    return (output_maps, input_grad, weight_grad, gain_grad)


HIGHEST = lax.Precision.HIGHEST


def dot(lhs, rhs, contract=((1,), (0,)), precision=None):
    return lax.dot_general(
        lhs, rhs, (contract, ((), ())), precision=precision, preferred_element_type=jnp.float32
    )


def fused(
    nz,
    x_hbm,
    g_hbm,
    w_hbm,
    ct_hbm,
    out_ref,
    dx_ref,
    wg_ref,
    gg_ref,
    xv,
    gv,
    ctl,
    split,
    same,
    p_out,
    p_in,
    norm,
    dsilu,
    zgrad,
    patches,
    taps,
    edge,
    wfull,
    stat,
    stat_in,
    part,
    core_in,
    half,
    x_in,
    quarter,
    z_in,
    comb,
    final,
    rep_in,
    uv,
    uv_in,
    uvt,
    uvt_in,
    loc_sem,
    halo_sem,
    stat_sem,
    w_send,
    w_recv,
    y_sem,
    c_sem,
    d_sem,
    core_sem,
    x_sem,
    z_sem,
    comb_sem,
    rep_sem,
    uv_sem,
    uvt_sem,
):
    f32, bf16 = jnp.float32, jnp.bfloat16
    rows, chans, width = x_hbm.shape[1:]
    cols = width // 2
    outs_ch, block = w_hbm.shape
    q_rows = outs_ch // 4
    h_rows = outs_ch // 2
    lanes = part.shape[3]
    sizes = [lanes, block - lanes]
    w_cut = [(0, -(-q_rows // 32) * 16)]
    w_cut.append((w_cut[0][1], q_rows - w_cut[0][1]))
    count = rows * nz * width * (chans // GROUPS)
    scale = 1.0 / jnp.sqrt(f32(4 * nz * ct_hbm.shape[1] * cols))
    z = lax.axis_index("fsdp")
    rep = lax.axis_index("rep")
    yi = lax.axis_index("groups")
    xi, ci = rep // 2, rep % 2
    mine = 2 * ci + xi
    peers_z = [lax.rem(z + d, nz) for d in range(1, nz)]
    reps = [(2 * xi + 1 - ci), (2 * (1 - xi) + ci), (2 * (1 - xi) + 1 - ci)]
    core_peer, x_peer = reps[0], reps[1]
    pair = z // 2
    partner = z + 1 - 2 * (z % 2)
    inner = jnp.logical_or(z == 1, z == 2)
    outer = jnp.logical_or(z == 0, z == 3)
    order = [3 * (1 - pair), 2 - pair, partner, z]
    others = [partner, 2 - pair, 3 * (1 - pair)]

    def aligned(value):
        return pl.multiple_of(value, 16)

    def remote(src, dst, send, recv, device):
        return pltpu.make_async_remote_copy(
            src_ref=src,
            dst_ref=dst,
            send_sem=send,
            recv_sem=recv,
            device_id=device,
            device_id_type=MESH,
        )

    barrier = pltpu.get_barrier_semaphore()
    for peer in peers_z:
        pl.semaphore_signal(barrier, inc=1, device_id={"fsdp": peer}, device_id_type=MESH)
    for peer in reps:
        pl.semaphore_signal(barrier, inc=1, device_id={"rep": peer}, device_id_type=MESH)
    pl.semaphore_signal(barrier, inc=1, device_id={"groups": 1 - yi}, device_id_type=MESH)

    x_local = [pltpu.make_async_copy(x_hbm.at[0, r], xv.at[r], loc_sem.at[r]) for r in range(rows)]
    g_local = pltpu.make_async_copy(g_hbm, gv, loc_sem.at[rows])
    w_local = pltpu.make_async_copy(w_hbm, wfull.at[z], loc_sem.at[rows + 1])
    c_local = [
        pltpu.make_async_copy(
            ct_hbm.at[0, i], ctl.at[k, :, pl.ds(i * cols, cols)], loc_sem.at[rows + 2 + n]
        )
        for n, (k, i) in enumerate([(1, 0), (1, 1), (0, 1)])
    ]
    for cp in x_local + c_local + [w_local, g_local]:
        cp.start()

    big_i = lax.broadcasted_iota(jnp.int32, (width, width), 0)
    big_j = lax.broadcasted_iota(jnp.int32, (width, width), 1)
    inv = 1.0 / (chans // GROUPS)
    lane = lax.broadcasted_iota(jnp.int32, (chans, cols), 1)
    wide = same.shape[1] // 3
    ch_i = lax.broadcasted_iota(jnp.int32, (chans, wide), 0)
    ch_j = lax.broadcasted_iota(jnp.int32, (chans, wide), 1)
    grp_i = jnp.floor((ch_i.astype(f32) + 0.5) * inv)
    grp_j = jnp.floor((ch_j.astype(f32) + 0.5) * inv)
    same_one = jnp.where(jnp.where(ch_j < chans, grp_j, -1.0) == grp_i, 1.0, 0.0).astype(bf16)
    sums_i = lax.broadcasted_iota(jnp.int32, (8, width), 0)
    sums_j = lax.broadcasted_iota(jnp.int32, (8, width), 1)
    halves = jnp.where(jnp.where(sums_j < cols, 0, 4) == sums_i - lax.rem(sums_i, 4), 1.0, 0.0)
    halves = halves.astype(bf16)

    def three_terms(value):
        high = value.astype(bf16)
        rest = value - high.astype(f32)
        middle = rest.astype(bf16)
        low = (rest - middle.astype(f32)).astype(bf16)
        return high, middle, low

    def row_sums(first, second):
        both = jnp.concatenate([first, second], axis=1)
        terms = [dot(halves, term, ((1,), (1,))) for term in three_terms(both)]
        return terms[0] + (terms[1] + terms[2])

    def group_sums(total):
        pad = jnp.zeros((8, wide - chans), f32)
        terms = three_terms(jnp.concatenate([total, pad], axis=1))
        spread = jnp.concatenate(terms, axis=1).astype(f32)
        first = jnp.broadcast_to(spread[0:1], (cols, 3 * wide))
        second = jnp.broadcast_to(spread[4:5], (cols, 3 * wide))
        rhs = jnp.concatenate([first, second], axis=0).astype(bf16)
        sums = dot(same[...], rhs, ((1,), (1,)))
        return sums[:, :cols], sums[:, cols:]

    @pl.when(z == nz - 1)
    def _():
        ctl[0, :, :cols] = jnp.zeros((chans, cols), bf16)

    halo_c = remote(
        ctl.at[1, :, pl.ds(0, cols)],
        ctl.at[0, :, pl.ds(0, cols)],
        halo_sem.at[0, 0],
        halo_sem.at[0, 1],
        {"fsdp": lax.rem(z + nz - 1, nz)},
    )
    p_copy = remote(
        p_out, p_in, halo_sem.at[1, 0], halo_sem.at[1, 1], {"fsdp": lax.rem(z + 1, nz)}
    )

    def w_spot(q, y_from, c):
        start, size = w_cut[c]
        return wfull.at[q, pl.ds(aligned(q_rows * (2 * ci + y_from) + start), size)]

    def own_w(up, c):
        start, size = w_cut[c]
        to = lax.rem(z + (1 if up else nz - 1), nz)
        return remote(
            w_spot(z, yi, c),
            w_spot(z, yi, c),
            w_send.at[1 if up else 0, c],
            w_recv.at[z, c],
            {"fsdp": to},
        )

    def when_up(act):
        pl.when(z < nz - 1)(act)

    def when_down(act):
        pl.when(z > 0)(act)

    sum_one = jnp.zeros((chans, cols), f32)
    sum_two = jnp.zeros((chans, cols), f32)
    for r in range(rows):
        x_local[r].wait()
        even, odd = xv[r, :, :cols].astype(f32), xv[r, :, cols:].astype(f32)
        sum_one = sum_one + (even + odd)
        sum_two = sum_two + (even * even + odd * odd)
    stat[...] = row_sums(sum_one, sum_two)

    stat_cp = [
        remote(stat, stat_in.at[d], stat_sem.at[d, 0], stat_sem.at[d, 1], {"fsdp": peers_z[d]})
        for d in range(nz - 1)
    ]
    pl.semaphore_wait(barrier, nz - 1 + 3 + 1)
    for d in (1, 0, 2):
        stat_cp[d].start()
    split[...] = jnp.where(
        jnp.where(big_j < cols, 2 * big_j, 2 * (big_j - cols) + 1) == big_i, 1.0, 0.0
    ).astype(bf16)
    for k in range(3):
        same[:, k * wide : (k + 1) * wide] = same_one
    for r in range(rows):
        norm[r + 1] = dot(xv[r], split[...])
    eye_i = lax.broadcasted_iota(jnp.int32, (chans, chans), 0)
    eye_j = lax.broadcasted_iota(jnp.int32, (chans, chans), 1)
    eye = jnp.where(eye_i == eye_j, 1.0, 0.0)
    g_local.wait()
    gains = dot(eye, gv[...], ((1,), (1,)), HIGHEST)
    gain = jnp.broadcast_to(gains[:, 0:1], (chans, cols))
    shift = jnp.broadcast_to(gains[:, 1:2], (chans, cols))

    for cp in c_local:
        cp.wait()
    w_local.wait()

    @pl.when(z == nz - 1)
    def _():
        halo_c.start()
        own_w(False, 0).start()
        own_w(False, 1).start()

    def block_taps(q):
        here = pl.ds(aligned(q * block), block)
        taps[here] = dot(wfull[q], ctl[1], ((0,), (0,)))

    block_taps(z)

    for cp in stat_cp:
        cp.wait_recv()
    total = stat[...]
    for d in range(nz - 1):
        total = total + stat_in[d]
    @pl.when(z == 0)
    def _():
        own_w(True, 0).start()
        own_w(True, 1).start()

    @pl.when(inner)
    def _():
        for c in range(2):
            own_w(True, c).start()
            own_w(False, c).start()
        halo_c.start()

    sum_one, sum_two = group_sums(total)
    mean = sum_one / count
    rstd = 1.0 / jnp.sqrt(sum_two / count - mean * mean + 1e-05)
    slope = gain * rstd

    def put(row_tap, col_tap, i, lo, value):
        start = (3 * row_tap + col_tap) * chans + lo
        patches[start : start + value.shape[0], i * cols : (i + 1) * cols] = value

    step = 64

    def activate(r, users):
        for lo in range(0, chans, step):
            part_of = slice(lo, lo + step)
            for odd in range(2):
                here = pl.ds(odd * cols, cols)
                x_val = norm[r, part_of, here]
                z_val = (x_val - mean[part_of]) * slope[part_of] + shift[part_of]
                sig = 0.5 * jnp.tanh(0.5 * z_val) + 0.5
                act = z_val * sig
                dsilu[r - 1, part_of, here] = sig
                rounded = act.astype(bf16)
                for t, i in users:
                    put(t, 1 + odd, i, lo, rounded)
                if odd == 1:
                    moved = pltpu.roll(act, 1, axis=1)
                    moved = jnp.where(lane[part_of] == 0, 0.0, moved).astype(bf16)
                    for t, i in users:
                        put(t, 0, i, lo, moved)

    activate(1, [(1, 0)])
    activate(3, [(1, 1)])
    activate(2, [(2, 0), (0, 1)])
    activate(4, [(2, 1), (0, 0)])

    pl.when(z == nz - 2)(lambda: halo_c.wait_recv())

    def w_arrive(j, c, role):
        @pl.when(role)
        def _():
            q = others[j]
            spot = w_spot(q, yi, c)
            remote(spot, spot, w_send.at[2 + j, c], w_recv.at[q, c], {"fsdp": partner}).wait_recv()
            if role is inner:
                to = 3 - z if j == 0 else partner
                remote(spot, spot, w_send.at[2 + j, c], w_recv.at[q, c], {"fsdp": to}).start()
            y_forward(j, c).start()
            c_forward(j, c).start()

    def y_forward(j, c):
        spot = w_spot(others[j], yi, c)
        return remote(spot, spot, y_sem.at[j, c, 0], y_sem.at[j, c, 1], {"groups": 1 - yi})

    def c_forward(j, c):
        spot = w_spot(others[j], yi, c)
        return remote(spot, spot, c_sem.at[j, c, 0], c_sem.at[j, c, 1], {"rep": core_peer})

    def d_forward(j, c):
        spot = w_spot(others[j], 1 - yi, c)
        return remote(spot, spot, d_sem.at[j, c, 0], d_sem.at[j, c, 1], {"rep": core_peer})

    def w_second(j, c):
        y_forward(j, c).wait_recv()
        d_forward(j, c).start()

    def w_taps(j):
        for c in range(2):
            c_forward(j, c).wait_recv()
            d_forward(j, c).wait_recv()
        block_taps(others[j])

    def core_copy(n, h):
        return remote(
            part.at[n, h, pl.ds(aligned(h_rows * (1 - ci)), h_rows)],
            core_in.at[n, h],
            core_sem.at[n, h, 0],
            core_sem.at[n, h, 1],
            {"rep": core_peer},
        )

    def x_copy(n, h):
        return remote(
            half.at[n, h, pl.ds(aligned(q_rows * (1 - xi)), q_rows)],
            x_in.at[n, h],
            x_sem.at[n, h, 0],
            x_sem.at[n, h, 1],
            {"rep": x_peer},
        )

    def z_copy(n, h):
        return remote(
            quarter.at[n, h],
            z_in.at[n, h],
            z_sem.at[n, h, 0],
            z_sem.at[n, h, 1],
            {"fsdp": partner},
        )

    def comb_copy(n, h):
        slot = 4 - n
        return remote(
            comb.at[n, h],
            z_in.at[slot, h],
            comb_sem.at[n, h],
            z_sem.at[slot, h, 1],
            {"fsdp": 3 - z},
        )

    def join_copy(h):
        return remote(
            comb.at[2, h],
            z_in.at[2, h],
            z_sem.at[2, h, 0],
            z_sem.at[2, h, 1],
            {"fsdp": partner},
        )

    def weight_step(n, h):
        q, size = order[n], sizes[h]
        rhs = patches[pl.ds(aligned(q * block + h * lanes), size)]
        lhs = ctl[jnp.where(q == 0, 0, 1)]
        part[n, h, :, :size] = dot(lhs, rhs, ((1,), (1,))).astype(bf16)
        if h == 0 and n > 0:
            taken = 3 * chans - block

            @pl.when(q == 1)
            def _():
                rhs = patches[block : block + taken]
                part[n, h, :, :taken] = dot(ctl[0], rhs, ((1,), (1,))).astype(bf16)

        core_copy(n, h).start()

    def core_step(n, h):
        core_copy(n, h).wait_recv()
        mine_rows = part[n, h, pl.ds(aligned(h_rows * ci), h_rows)]
        half[n, h] = (mine_rows.astype(f32) + core_in[n, h].astype(f32)).astype(bf16)
        x_copy(n, h).start()

    def x_step(n, h):
        x_copy(n, h).wait_recv()
        mine_rows = half[n, h, pl.ds(aligned(q_rows * xi), q_rows)]
        quarter[n, h] = (mine_rows.astype(f32) + x_in[n, h].astype(f32)).astype(bf16)
        if n < 3:
            pl.when(outer)(lambda: z_copy(n, h).start())

    def comb_step(n, h):
        @pl.when(inner)
        def _():
            z_copy(n, h).wait_recv()
            value = quarter[n, h].astype(f32) + z_in[n, h].astype(f32)
            comb[n, h] = value.astype(bf16)
            comb_copy(n, h).start()

    def join_step(h):
        @pl.when(inner)
        def _():
            comb_copy(0, h).wait_recv()
            value = quarter[2, h].astype(f32) + z_in[4, h].astype(f32)
            comb[2, h] = value.astype(bf16)
            join_copy(h).start()

    def rep_copy(m, h):
        src = final.at[h] if m < 2 else rep_in.at[1, h]
        to = core_peer if m == 2 else reps[m]
        return remote(
            src, rep_in.at[m, h], rep_sem.at[m, h, 0], rep_sem.at[m, h, 1], {"rep": to}
        )

    def place(ref, k, h):
        rows_k = pl.ds(aligned(q_rows * k), q_rows)
        wg_ref[rows_k, h * lanes : h * lanes + sizes[h]] = ref[:, : sizes[h]].astype(f32)

    def final_step(h):
        z_copy(2, h).wait_recv()
        pl.when(inner)(lambda: comb_copy(1, h).wait_recv())
        value = quarter[3, h].astype(f32) + z_in[2, h].astype(f32)
        value = value + jnp.where(inner, z_in[3, h].astype(f32), 0.0)
        final[h] = (value * scale).astype(bf16)
        rep_copy(1, h).start()
        rep_copy(0, h).start()

    def relay_step(h):
        rep_copy(1, h).wait_recv()
        rep_copy(2, h).start()

    def prepare():
        for r in range(rows):
            for odd in range(2):
                here = pl.ds(odd * cols, cols)
                normed = (norm[r + 1, :, here] - mean) * rstd
                z_val = gain * normed + shift
                sig = dsilu[r, :, here]
                norm[r + 1, :, here] = normed
                dsilu[r, :, here] = sig * (1.0 + z_val * (1.0 - sig))

    w_lane = lax.broadcasted_iota(jnp.int32, (outs_ch, block), 1)
    top = 3 * chans - block
    upto, since = -(-top // 128) * 128, top // 128 * 128

    def top_maps():
        first = jnp.where(w_lane[:, :upto] < top, wfull[1, :, :upto].astype(f32), 0.0).astype(bf16)
        value = dot(wfull[0], patches[:block]) + dot(first, patches[block : block + upto])
        p_out[...] = value[:, :cols].astype(bf16)
        when_up(lambda: p_copy.start())
        return value[:, cols:]

    def low_maps(above):
        rest = wfull[1, :, since:].astype(f32)
        rest = jnp.where(w_lane[:, since:] < top, 0.0, rest).astype(bf16)
        value = dot(rest, patches[block + since : 2 * block])
        for q in range(2, nz):
            value = value + dot(wfull[q], patches[q * block : (q + 1) * block])
        out_ref[0, 1] = (value[:, cols:] + above).astype(bf16)
        return value[:, :cols]

    def join_maps(value):
        @pl.when(z == 0)
        def _():
            p_in[...] = jnp.zeros(p_in.shape, bf16)

        when_down(lambda: p_copy.wait_recv())
        out_ref[0, 0] = (value + p_in[...].astype(f32)).astype(bf16)

    def edge_taps():
        below = ctl[0, :, :cols]
        done = 0
        q = 0
        while done < 3 * chans:
            take = min(block, 3 * chans - done)
            edge[done : done + take] = dot(wfull[q, :, :take], below, ((0,), (0,)))
            done += take
            q += 1

    def tap_at(row_tap, col_tap, i):
        tap = 3 * row_tap + col_tap
        here = slice(tap * chans, (tap + 1) * chans)
        if i == 2:
            return edge[here]
        return taps[here, i * cols : (i + 1) * cols]

    uv_cp = [
        remote(uv, uv_in.at[d], uv_sem.at[d, 0], uv_sem.at[d, 1], {"fsdp": peers_z[d]})
        for d in range(nz - 1)
    ]

    def channel_sums():
        u_sum = jnp.zeros((chans, cols), f32)
        v_sum = jnp.zeros((chans, cols), f32)
        for r in range(rows):
            pairs = [(t, i) for i in range(3) for t in range(3) if 2 * i + t == r + 1]
            for odd in range(2):
                here = pl.ds(odd * cols, cols)
                grad = sum(tap_at(t, 1 + odd, i) for t, i in pairs)
                if odd == 1:
                    left = sum(tap_at(t, 0, i) for t, i in pairs)
                    moved = pltpu.roll(left, cols - 1, axis=1)
                    grad = grad + jnp.where(lane == cols - 1, 0.0, moved)
                value = grad * dsilu[r, :, here]
                zgrad[r, :, here] = value
                u_sum = u_sum + value * norm[r + 1, :, here]
                v_sum = v_sum + value
        uv[...] = row_sums(u_sum, v_sum)
        for d in (1, 0, 2):
            uv_cp[d].start()

    uvt_cp = [
        remote(uvt, uvt_in.at[m], uvt_sem.at[m, 0], uvt_sem.at[m, 1], {"rep": reps[m]})
        for m in range(3)
    ]

    def input_grads():
        for cp in uv_cp:
            cp.wait_recv()
        total = uv[...]
        for d in range(nz - 1):
            total = total + uv_in[d]
        uvt[...] = total
        for cp in uvt_cp:
            cp.start()
        su_val, sv_val = group_sums(gv[0:1] * total)
        su_val, sv_val = su_val / count, sv_val / count
        merge = jnp.where(
            jnp.where(big_i < cols, 2 * big_i, 2 * (big_i - cols) + 1) == big_j, 1.0, 0.0
        ).astype(bf16)
        for r in range(rows):
            for odd in range(2):
                here = pl.ds(odd * cols, cols)
                value = rstd * (gain * zgrad[r, :, here] - sv_val - norm[r + 1, :, here] * su_val)
                patches[r * chans : (r + 1) * chans, here] = value.astype(bf16)
            dx_ref[0, r] = dot(patches[r * chans : (r + 1) * chans], merge).astype(bf16)

    def halo_wait():
        pl.when(z < nz - 2)(lambda: halo_c.wait_recv())

    def drain():
        @pl.when(z < nz - 1)
        def _():
            own_w(True, 0).wait_send()
            own_w(True, 1).wait_send()

        @pl.when(z > 0)
        def _():
            halo_c.wait_send()
            own_w(False, 0).wait_send()
            own_w(False, 1).wait_send()

        for cp in stat_cp:
            cp.wait_send()
        for h in range(2):
            for j in range(3):
                y_forward(j, h).wait_send()
                c_forward(j, h).wait_send()
                d_forward(j, h).wait_send()
            for n in range(4):
                core_copy(n, h).wait_send()
                x_copy(n, h).wait_send()
        @pl.when(inner)
        def _():
            for h in range(2):
                for j in range(3):
                    spot = w_spot(others[j], yi, h)
                    to = 3 - z if j == 0 else partner
                    remote(
                        spot, spot, w_send.at[2 + j, h], w_recv.at[others[j], h], {"fsdp": to}
                    ).wait_send()
                for n in range(2):
                    comb_copy(n, h).wait_send()
                join_copy(h).wait_send()

        @pl.when(outer)
        def _():
            for h in range(2):
                for n in range(3):
                    z_copy(n, h).wait_send()

    weight_step(0, 0)
    weight_step(0, 1)
    weight_step(1, 0)
    core_step(0, 0)
    weight_step(1, 1)
    core_step(0, 1)
    w_arrive(0, 0, inner)
    w_arrive(1, 0, inner)
    w_arrive(0, 0, outer)
    core_step(1, 0)
    w_arrive(0, 1, inner)
    w_arrive(1, 1, inner)
    w_arrive(0, 1, outer)
    core_step(1, 1)
    prepare()
    halo_wait()
    weight_step(2, 0)
    weight_step(2, 1)
    weight_step(3, 0)
    core_step(2, 0)
    weight_step(3, 1)
    core_step(2, 1)
    x_step(0, 0)
    core_step(3, 0)
    w_arrive(2, 0, inner)
    w_arrive(1, 0, outer)
    x_step(0, 1)
    core_step(3, 1)
    w_arrive(2, 1, inner)
    w_arrive(1, 1, outer)
    w_second(0, 0)
    w_second(0, 1)
    x_step(1, 0)
    comb_step(0, 0)
    w_taps(0)
    x_step(1, 1)
    comb_step(0, 1)
    w_second(1, 0)
    w_arrive(2, 0, outer)
    w_second(1, 1)
    w_arrive(2, 1, outer)
    x_step(2, 0)
    comb_step(1, 0)
    join_step(0)
    w_taps(1)
    x_step(2, 1)
    comb_step(1, 1)
    join_step(1)
    w_second(2, 0)
    x_step(3, 0)
    w_second(2, 1)
    x_step(3, 1)
    w_taps(2)
    above = top_maps()
    final_step(0)
    edge_taps()
    channel_sums()
    final_step(1)
    low = low_maps(above)
    drain()
    input_grads()
    relay_step(0)
    relay_step(1)
    join_maps(low)

    owners = [2 * (1 - ci) + xi, 2 * ci + 1 - xi, 2 * (1 - ci) + 1 - xi]
    for h in range(2):
        place(final.at[h], mine, h)
        for m in (1, 0, 2):
            if m != 1:
                rep_copy(m, h).wait_recv()
            place(rep_in.at[m, h], owners[m], h)
    for cp in uvt_cp:
        cp.wait_recv()
    total = uvt[...] + uvt_in[0] + uvt_in[1] + uvt_in[2]
    gg_ref[0:1] = total[0:1] * scale
    gg_ref[1:2] = total[4:5] * scale

    when_up(lambda: p_copy.wait_send())
    for cp in uv_cp + uvt_cp:
        cp.wait_send()
    for h in range(2):
        for m in range(3):
            rep_copy(m, h).wait_send()


def write_out(*refs):
    n = len(refs) // 2
    sems = refs[-1]
    copies = [pltpu.make_async_copy(refs[i], refs[n + i], sems.at[i]) for i in range(n)]
    for cp in copies:
        cp.start()
    for cp in copies:
        cp.wait()


def in_hbm(value):
    return pltpu.with_memory_space_constraint(value, pltpu.HBM)


def fused_shards(images, gains, conv_weight, cotangent):
    batch, rows, width, chans = images.shape
    block, outs_ch = conv_weight.shape
    nz = lax.axis_size("fsdp")
    fits = (batch, rows, cotangent.shape[1]) == (1, 4, 2) and chans % 64 == 0 and width == 256
    if not fits or block % 16 or outs_ch % 64 or nz * block != 9 * chans:
        return shards(images, gains, conv_weight, cotangent)
    if not block < 3 * chans < 2 * block or 3 * chans - block > 384:
        return shards(images, gains, conv_weight, cotangent)
    cols = width // 2
    q_rows = outs_ch // 4
    lanes = -(-block // 256) * 128
    wide = -(-chans // 128) * 128
    f32, bf16 = jnp.float32, jnp.bfloat16
    vmem = pltpu.VMEM
    dma = pltpu.SemaphoreType.DMA
    shapes = (
        jax.ShapeDtypeStruct((batch, rows // 2, outs_ch, cols), bf16),
        jax.ShapeDtypeStruct((batch, rows, chans, width), bf16),
        jax.ShapeDtypeStruct((outs_ch, block), f32),
        jax.ShapeDtypeStruct(gains.shape, f32),
    )
    results = pl.pallas_call(
        functools.partial(fused, nz),
        out_shape=tuple(vmem(shape.shape, shape.dtype) for shape in shapes),
        in_specs=[pl.BlockSpec(memory_space=pltpu.HBM)] * 4,
        out_specs=[pl.BlockSpec(memory_space=vmem)] * 4,
        scratch_shapes=[
            vmem((rows, chans, width), bf16),
            vmem(gains.shape, f32),
            vmem((2, outs_ch, width), bf16),
            vmem((width, width), bf16),
            vmem((chans, 3 * wide), bf16),
            vmem((outs_ch, cols), bf16),
            vmem((outs_ch, cols), bf16),
            vmem((rows + 1, chans, width), f32),
            vmem((rows, chans, width), f32),
            vmem((rows, chans, width), f32),
            vmem((nz * block, width), bf16),
            vmem((nz * block, width), f32),
            vmem((3 * chans, cols), f32),
            vmem((nz, outs_ch, block), bf16),
            vmem((8, chans), f32),
            vmem((nz - 1, 8, chans), f32),
            vmem((nz, 2, outs_ch, lanes), bf16),
            vmem((nz, 2, 2 * q_rows, lanes), bf16),
            vmem((nz, 2, 2 * q_rows, lanes), bf16),
            vmem((nz, 2, q_rows, lanes), bf16),
            vmem((nz, 2, q_rows, lanes), bf16),
            vmem((5, 2, q_rows, lanes), bf16),
            vmem((3, 2, q_rows, lanes), bf16),
            vmem((2, q_rows, lanes), bf16),
            vmem((3, 2, q_rows, lanes), bf16),
            vmem((8, chans), f32),
            vmem((nz - 1, 8, chans), f32),
            vmem((8, chans), f32),
            vmem((3, 8, chans), f32),
            dma((rows + 5,)),
            dma((2, 2)),
            dma((nz - 1, 2)),
            dma((5, 2)),
            dma((nz, 2)),
            dma((3, 2, 2)),
            dma((3, 2, 2)),
            dma((3, 2, 2)),
            dma((nz, 2, 2)),
            dma((nz, 2, 2)),
            dma((5, 2, 2)),
            dma((2, 2)),
            dma((3, 2, 2)),
            dma((nz - 1, 2)),
            dma((3, 2)),
        ],
        compiler_params=pltpu.CompilerParams(
            collective_id=0, has_side_effects=True, vmem_limit_bytes=48 * 1024 * 1024
        ),
    )(
        in_hbm(jnp.swapaxes(images, 2, 3)),
        in_hbm(gains),
        in_hbm(conv_weight.T),
        in_hbm(jnp.swapaxes(cotangent, 2, 3)),
    )
    output_maps, input_grad, weight_grad, gain_grad = pl.pallas_call(
        write_out,
        out_shape=shapes,
        in_specs=[pl.BlockSpec(memory_space=vmem)] * 4,
        out_specs=[pl.BlockSpec(memory_space=pltpu.HBM)] * 4,
        scratch_shapes=[dma((4,))],
        compiler_params=pltpu.CompilerParams(vmem_limit_bytes=1024 * 1024),
    )(*(pltpu.with_memory_space_constraint(value, vmem) for value in results))
    return (
        jnp.swapaxes(output_maps, 2, 3),
        jnp.swapaxes(input_grad, 2, 3),
        weight_grad.T,
        gain_grad,
    )


def solution(mesh):
    in_specs = (
        P(("groups", "rep"), "fsdp", None, None),
        P(),
        P("fsdp", None),
        P(("groups", "rep"), "fsdp", None, None),
    )
    out_specs = (
        P(("groups", "rep"), "fsdp", None, None),
        P(("groups", "rep"), "fsdp", None, None),
        P(("groups", "fsdp"), None),
        P("groups", None),
    )
    small = mesh.shape["groups"] == 2 and mesh.shape["rep"] == 4 and mesh.shape["fsdp"] == 4
    body = fused_shards if small else shards
    return jax.shard_map(body, mesh=mesh, in_specs=in_specs, out_specs=out_specs, check_vma=False)
```

```python
import functools

import jax
import jax.numpy as jnp
from jax import lax
from jax.experimental import pallas as pl
from jax.experimental.pallas import tpu as pltpu
from jax.sharding import PartitionSpec as P

GROUPS = 32
MESH = pl.DeviceIdType.MESH


def passed_along(shard, axis, by):
    size = lax.axis_size(axis)
    pairs = [(i, i + by) for i in range(size) if 0 <= i + by < size]
    return lax.ppermute(shard, axis, pairs)


def spread_taps(first, middle, last, axis):
    length = first.shape[axis]
    widths_end = [(0, 0)] * first.ndim
    widths_end[axis] = (0, 1)
    widths_start = [(0, 0)] * first.ndim
    widths_start[axis] = (1, 0)
    even = jnp.pad(first, widths_end) + jnp.pad(last, widths_start)
    odd = jnp.pad(middle, widths_end)
    merged = jnp.stack([even, odd], axis=axis + 1)
    shape = list(even.shape)
    shape[axis] = 2 * (length + 1)
    merged = merged.reshape(shape)
    return lax.slice_in_dim(merged, 0, 2 * length + 1, axis=axis)


def shards(images, gains, conv_weight, cotangent):
    batch, rows, width, chans = images.shape
    outs_ch = conv_weight.shape[1]
    n_fsdp = lax.axis_size("fsdp")
    per_group = chans // GROUPS
    x_val = images.astype(jnp.float32)
    grouped = x_val.reshape(batch, rows, width, GROUPS, per_group)
    part_one = jnp.sum(grouped, axis=(1, 2, 4))
    part_two = jnp.sum(grouped * grouped, axis=(1, 2, 4))
    full_weight = lax.all_gather(conv_weight, "fsdp", axis=0, tiled=True)
    sum_one, sum_two = lax.psum((part_one, part_two), "fsdp")
    count = rows * n_fsdp * width * per_group
    mean = sum_one / count
    rstd = 1.0 / jnp.sqrt(sum_two / count - mean * mean + 1e-05)
    normed_g = (grouped - mean[:, None, None, :, None]) * rstd[:, None, None, :, None]
    normed = normed_g.reshape(x_val.shape)
    z_val = gains[0] * normed + gains[1]
    act = (z_val * jax.nn.sigmoid(z_val)).astype(jnp.bfloat16)
    above = passed_along(act[:, rows - 1 : rows], "fsdp", 1)
    padded = jnp.concatenate([above, act], axis=1)
    kernel = full_weight.reshape(3, 3, chans, outs_ch)
    result = lax.conv_general_dilated(
        padded,
        kernel,
        (2, 2),
        ((0, 0), (1, 0)),
        dimension_numbers=("NHWC", "HWIO", "NHWC"),
        preferred_element_type=jnp.float32,
    )
    output_maps = result.astype(jnp.bfloat16)
    patch_grad = jnp.einsum(
        "bijo,ko->bijk", cotangent, full_weight, preferred_element_type=jnp.float32
    )
    half_rows, half_cols = (cotangent.shape[1], cotangent.shape[2])
    taps = patch_grad.reshape(batch, half_rows, half_cols, 3, 3, chans)
    by_row = [
        spread_taps(
            taps[:, :, :, row_tap, 0], taps[:, :, :, row_tap, 1], taps[:, :, :, row_tap, 2], 2
        )
        for row_tap in range(3)
    ]
    grid = spread_taps(by_row[0], by_row[1], by_row[2], 1)[:, :, 1:]
    from_below = passed_along(grid[:, 0:1].astype(jnp.bfloat16), "fsdp", -1).astype(jnp.float32)
    filler = jnp.zeros((batch, rows - 1, width, chans), jnp.float32)
    act_grad = grid[:, 1:] + jnp.concatenate([filler, from_below], axis=1)
    padded_cols = jnp.pad(padded, ((0, 0), (0, 0), (1, 0), (0, 0)))
    blocks = []
    for row_tap in range(3):
        for col_tap in range(3):
            window = padded_cols[:, row_tap : row_tap + rows : 2, col_tap : col_tap + width : 2]
            blocks.append(
                jnp.einsum("bijc,bijo->co", window, cotangent, preferred_element_type=jnp.float32)
            )
    total_pixels = batch * lax.axis_size("rep") * half_rows * n_fsdp * half_cols
    scale = 1.0 / jnp.sqrt(jnp.float32(total_pixels))
    weight_term = jnp.concatenate(blocks, axis=0) * scale
    sig = jax.nn.sigmoid(z_val)
    z_grad = act_grad * sig * (1.0 + z_val * (1.0 - sig))
    u_part = jnp.sum(z_grad * normed, axis=(1, 2))
    v_part = jnp.sum(z_grad, axis=(1, 2))
    u_sum, v_sum = lax.psum((u_part, v_part), "fsdp")
    gain_term = jnp.stack([jnp.sum(u_sum, axis=0), jnp.sum(v_sum, axis=0)]) * scale
    su_val = jnp.sum((gains[0] * u_sum).reshape(batch, GROUPS, per_group), axis=-1)
    sv_val = jnp.sum((gains[0] * v_sum).reshape(batch, GROUPS, per_group), axis=-1)
    scaled = (gains[0] * z_grad).reshape(grouped.shape)
    dx_val = rstd[:, None, None, :, None] * (
        scaled
        - sv_val[:, None, None, :, None] / count
        - normed_g * su_val[:, None, None, :, None] / count
    )
    input_grad = dx_val.reshape(x_val.shape).astype(jnp.bfloat16)
    owned = lax.psum_scatter(weight_term, "fsdp", scatter_dimension=0, tiled=True)
    weight_grad, gain_grad = (
        lax.psum(owned.astype(jnp.bfloat16), "rep").astype(jnp.float32),
        lax.psum(gain_term.astype(jnp.bfloat16), "rep").astype(jnp.float32),
    )
    return (output_maps, input_grad, weight_grad, gain_grad)


HIGHEST = lax.Precision.HIGHEST


def dot(lhs, rhs, contract=((1,), (0,)), precision=None):
    return lax.dot_general(
        lhs, rhs, (contract, ((), ())), precision=precision, preferred_element_type=jnp.float32
    )


def fused(
    nz,
    x_hbm,
    g_hbm,
    w_hbm,
    ct_hbm,
    out_ref,
    dx_ref,
    wg_ref,
    gg_ref,
    xv,
    gv,
    ctl,
    split,
    same,
    p_out,
    p_in,
    norm,
    dsilu,
    zgrad,
    patches,
    taps,
    edge,
    wfull,
    stat,
    stat_in,
    part,
    core_in,
    half,
    x_in,
    quarter,
    z_in,
    comb,
    final,
    rep_in,
    uv,
    uv_in,
    uvt,
    uvt_in,
    loc_sem,
    halo_sem,
    stat_send,
    stat_recv,
    send_sem,
    w_recv,
    y_recv,
    cd_recv,
    core_recv,
    x_recv,
    z_recv,
    rep_recv,
    uv_recv,
):
    f32, bf16 = jnp.float32, jnp.bfloat16
    rows, chans, width = x_hbm.shape[1:]
    cols = width // 2
    outs_ch, block = w_hbm.shape
    q_rows = outs_ch // 4
    h_rows = outs_ch // 2
    lanes = part.shape[3]
    sizes = [lanes, block - lanes]
    w_cut = [(0, -(-q_rows // 32) * 16)]
    w_cut.append((w_cut[0][1], q_rows - w_cut[0][1]))
    count = rows * nz * width * (chans // GROUPS)
    scale = 1.0 / jnp.sqrt(f32(4 * nz * ct_hbm.shape[1] * cols))
    z = lax.axis_index("fsdp")
    rep = lax.axis_index("rep")
    yi = lax.axis_index("groups")
    xi, ci = rep // 2, rep % 2
    mine = 2 * ci + xi
    peers_z = [lax.rem(z + d, nz) for d in range(1, nz)]
    reps = [(2 * xi + 1 - ci), (2 * (1 - xi) + ci), (2 * (1 - xi) + 1 - ci)]
    core_peer, x_peer = reps[0], reps[1]
    pair = z // 2
    partner = z + 1 - 2 * (z % 2)
    inner = jnp.logical_or(z == 1, z == 2)
    outer = jnp.logical_or(z == 0, z == 3)
    order = [3 * (1 - pair), 2 - pair, partner, z]
    others = [partner, 2 - pair, 3 * (1 - pair)]

    def aligned(value):
        return pl.multiple_of(value, 16)

    def remote(src, dst, send, recv, device):
        return pltpu.make_async_remote_copy(
            src_ref=src,
            dst_ref=dst,
            send_sem=send,
            recv_sem=recv,
            device_id=device,
            device_id_type=MESH,
        )

    def done(ref, sem):
        pltpu.make_async_copy(ref, ref, sem).wait()

    barrier = pltpu.get_barrier_semaphore()
    for near in (partner, 3 - z):
        wanted = inner if near is not partner else z >= 0

        @pl.when(wanted)
        def _():
            pl.semaphore_signal(barrier, inc=1, device_id={"fsdp": near}, device_id_type=MESH)

    @pl.when(z == 0)
    def _():
        pl.semaphore_signal(barrier, inc=1, device_id={"fsdp": 2}, device_id_type=MESH)

    for peer in reps:
        pl.semaphore_signal(barrier, inc=1, device_id={"rep": peer}, device_id_type=MESH)
    pl.semaphore_signal(barrier, inc=1, device_id={"groups": 1 - yi}, device_id_type=MESH)

    x_local = [pltpu.make_async_copy(x_hbm.at[0, r], xv.at[r], loc_sem.at[r]) for r in range(rows)]
    g_local = pltpu.make_async_copy(g_hbm, gv, loc_sem.at[rows])
    w_local = pltpu.make_async_copy(w_hbm, wfull.at[z], loc_sem.at[rows + 1])
    c_local = [
        pltpu.make_async_copy(
            ct_hbm.at[0, i], ctl.at[k, :, pl.ds(i * cols, cols)], loc_sem.at[rows + 2 + n]
        )
        for n, k, i in ((0, 1, 0), (0, 1, 1), (1, 0, 1))
    ]
    for cp in x_local + c_local + [w_local, g_local]:
        cp.start()

    big_i = lax.broadcasted_iota(jnp.int32, (width, width), 0)
    big_j = lax.broadcasted_iota(jnp.int32, (width, width), 1)
    inv = 1.0 / (chans // GROUPS)
    lane = lax.broadcasted_iota(jnp.int32, (chans, cols), 1)
    wide = same.shape[1] // 3
    ch_i = lax.broadcasted_iota(jnp.int32, (chans, wide), 0)
    ch_j = lax.broadcasted_iota(jnp.int32, (chans, wide), 1)
    grp_i = jnp.floor((ch_i.astype(f32) + 0.5) * inv)
    grp_j = jnp.floor((ch_j.astype(f32) + 0.5) * inv)
    same_one = jnp.where(jnp.where(ch_j < chans, grp_j, -1.0) == grp_i, 1.0, 0.0).astype(bf16)
    sums_i = lax.broadcasted_iota(jnp.int32, (8, width), 0)
    sums_j = lax.broadcasted_iota(jnp.int32, (8, width), 1)
    halves = jnp.where(jnp.where(sums_j < cols, 0, 4) == sums_i - lax.rem(sums_i, 4), 1.0, 0.0)
    halves = halves.astype(bf16)

    def three_terms(value):
        high = value.astype(bf16)
        rest = value - high.astype(f32)
        middle = rest.astype(bf16)
        low = (rest - middle.astype(f32)).astype(bf16)
        return high, middle, low

    def row_sums(first, second):
        both = jnp.concatenate([first, second], axis=1)
        terms = [dot(halves, term, ((1,), (1,))) for term in three_terms(both)]
        return terms[0] + (terms[1] + terms[2])

    def group_sums(total):
        pad = jnp.zeros((8, wide - chans), f32)
        terms = three_terms(jnp.concatenate([total, pad], axis=1))
        spread = jnp.concatenate(terms, axis=1).astype(f32)
        first = jnp.broadcast_to(spread[0:1], (cols, 3 * wide))
        second = jnp.broadcast_to(spread[4:5], (cols, 3 * wide))
        rhs = jnp.concatenate([first, second], axis=0).astype(bf16)
        sums = dot(same[...], rhs, ((1,), (1,)))
        return sums[:, :cols], sums[:, cols:]

    @pl.when(z == nz - 1)
    def _():
        ctl[0, :, :cols] = jnp.zeros((chans, cols), bf16)

    halo_c = remote(
        ctl.at[1, :, pl.ds(0, cols)],
        ctl.at[0, :, pl.ds(0, cols)],
        halo_sem.at[0, 0],
        halo_sem.at[0, 1],
        {"fsdp": lax.rem(z + nz - 1, nz)},
    )
    p_copy = remote(
        p_out, p_in, halo_sem.at[1, 0], halo_sem.at[1, 1], {"fsdp": lax.rem(z + 1, nz)}
    )

    def w_spot(q, y_from, c):
        start, size = w_cut[c]
        return wfull.at[q, pl.ds(aligned(q_rows * (2 * ci + y_from) + start), size)]

    def own_w(up, c):
        start, size = w_cut[c]
        to = lax.rem(z + (1 if up else nz - 1), nz)
        return remote(
            w_spot(z, yi, c),
            w_spot(z, yi, c),
            send_sem.at[0],
            w_recv.at[z, c],
            {"fsdp": to},
        )

    def when_up(act):
        pl.when(z < nz - 1)(act)

    def when_down(act):
        pl.when(z > 0)(act)

    sum_one = jnp.zeros((chans, cols), f32)
    sum_two = jnp.zeros((chans, cols), f32)
    for r in range(rows):
        x_local[r].wait()
        even, odd = xv[r, :, :cols].astype(f32), xv[r, :, cols:].astype(f32)
        sum_one = sum_one + (even + odd)
        sum_two = sum_two + (even * even + odd * odd)
    stat[0] = row_sums(sum_one, sum_two)

    pl.semaphore_wait(barrier, 4 + jnp.where(z == 2, 3, jnp.where(z == 1, 2, 1)))

    def stat_copy(k, src, slot, to):
        return remote(
            stat.at[src], stat_in.at[slot], stat_send.at[k], stat_recv.at[slot], {"fsdp": to}
        )

    def stat_wait(slot):
        stat_copy(0, 0, slot, partner).wait_recv()

    @pl.when(z != 2)
    def _():
        stat_copy(0, 0, 0, partner).start()

    @pl.when(z == 1)
    def _():
        stat_wait(0)
        stat[1] = stat[0] + stat_in[0]
        stat_copy(1, 1, 1, 2).start()

    split[...] = jnp.where(
        jnp.where(big_j < cols, 2 * big_j, 2 * (big_j - cols) + 1) == big_i, 1.0, 0.0
    ).astype(bf16)
    for k in range(3):
        same[:, k * wide : (k + 1) * wide] = same_one
    for r in range(rows):
        norm[r + 1] = dot(xv[r], split[...])
    eye_i = lax.broadcasted_iota(jnp.int32, (chans, chans), 0)
    eye_j = lax.broadcasted_iota(jnp.int32, (chans, chans), 1)
    eye = jnp.where(eye_i == eye_j, 1.0, 0.0)
    g_local.wait()
    gains = dot(eye, gv[...], ((1,), (1,)), HIGHEST)
    gain = jnp.broadcast_to(gains[:, 0:1], (chans, cols))
    shift = jnp.broadcast_to(gains[:, 1:2], (chans, cols))

    done(ctl.at[1], loc_sem.at[rows + 2])
    c_local[2].wait()
    w_local.wait()

    @pl.when(z == 0)
    def _():
        own_w(True, 0).start()
        own_w(True, 1).start()

    @pl.when(z == 1)
    def _():
        own_w(True, 0).start()
        own_w(True, 1).start()

    @pl.when(z == 2)
    def _():
        stat_wait(0)
        stat[1] = stat[0] + stat_in[0]
        stat_copy(1, 1, 1, 1).start()
        stat_copy(2, 1, 1, 0).start()
        stat_wait(1)
        stat[2] = stat[1] + stat_in[1]
        stat_copy(0, 2, 1, 3).start()
        for c in range(2):
            own_w(True, c).start()
            own_w(False, c).start()
        halo_c.start()

    @pl.when(z == 3)
    def _():
        halo_c.start()
        own_w(False, 0).start()
        own_w(False, 1).start()
        stat_wait(1)
        stat[2] = stat_in[1]

    @pl.when(z == 1)
    def _():
        stat_wait(1)
        stat[2] = stat[1] + stat_in[1]
        own_w(False, 0).start()
        own_w(False, 1).start()
        halo_c.start()

    @pl.when(z == 0)
    def _():
        stat_wait(0)
        stat_wait(1)
        stat[2] = stat[0] + stat_in[0] + stat_in[1]

    def block_taps(q):
        here = pl.ds(aligned(q * block), block)
        taps[here] = dot(wfull[q], ctl[1], ((0,), (0,)))

    total = stat[2]
    sum_one, sum_two = group_sums(total)
    mean = sum_one / count
    rstd = 1.0 / jnp.sqrt(sum_two / count - mean * mean + 1e-05)
    slope = gain * rstd

    def put(row_tap, col_tap, i, lo, value):
        start = (3 * row_tap + col_tap) * chans + lo
        patches[start : start + value.shape[0], i * cols : (i + 1) * cols] = value

    step = 64

    def activate(r, users):
        for lo in range(0, chans, step):
            part_of = slice(lo, lo + step)
            for odd in range(2):
                here = pl.ds(odd * cols, cols)
                x_val = norm[r, part_of, here]
                z_val = (x_val - mean[part_of]) * slope[part_of] + shift[part_of]
                sig = 0.5 * jnp.tanh(0.5 * z_val) + 0.5
                act = z_val * sig
                dsilu[r - 1, part_of, here] = sig
                rounded = act.astype(bf16)
                for t, i in users:
                    put(t, 1 + odd, i, lo, rounded)
                if odd == 1:
                    moved = pltpu.roll(act, 1, axis=1)
                    moved = jnp.where(lane[part_of] == 0, 0.0, moved).astype(bf16)
                    for t, i in users:
                        put(t, 0, i, lo, moved)

    activate(1, [(1, 0)])
    activate(3, [(1, 1)])
    activate(2, [(2, 0), (0, 1)])
    activate(4, [(2, 1), (0, 0)])

    pl.when(z == nz - 2)(lambda: halo_c.wait_recv())

    def w_arrive(j, c, role):
        @pl.when(role)
        def _():
            q = others[j]
            spot = w_spot(q, yi, c)
            remote(spot, spot, send_sem.at[1], w_recv.at[q, c], {"fsdp": partner}).wait_recv()
            if role is inner:
                to = 3 - z if j == 0 else partner
                remote(spot, spot, send_sem.at[1], w_recv.at[q, c], {"fsdp": to}).start()
            y_forward(j, c).start()
            c_forward(j, c).start()

    def y_forward(j, c):
        spot = w_spot(others[j], yi, c)
        return remote(spot, spot, send_sem.at[2], y_recv.at[j, c], {"groups": 1 - yi})

    def c_forward(j, c):
        spot = w_spot(others[j], yi, c)
        return remote(spot, spot, send_sem.at[3], cd_recv.at[j], {"rep": core_peer})

    def d_forward(j, c):
        spot = w_spot(others[j], 1 - yi, c)
        return remote(spot, spot, send_sem.at[4], cd_recv.at[j], {"rep": core_peer})

    def w_second(j, c):
        y_forward(j, c).wait_recv()
        d_forward(j, c).start()

    def w_taps(j):
        rows_in = pl.ds(aligned(h_rows * (1 - ci)), h_rows)
        done(wfull.at[others[j], rows_in], cd_recv.at[j])
        block_taps(others[j])

    def core_copy(n, h):
        return remote(
            part.at[n, h, pl.ds(aligned(h_rows * (1 - ci)), h_rows)],
            core_in.at[n, h],
            send_sem.at[5],
            core_recv.at[n, h],
            {"rep": core_peer},
        )

    def x_copy(n, h):
        return remote(
            half.at[n, h, pl.ds(aligned(q_rows * (1 - xi)), q_rows)],
            x_in.at[n, h],
            send_sem.at[6],
            x_recv.at[n, h],
            {"rep": x_peer},
        )

    def z_copy(n, h):
        return remote(
            quarter.at[n, h],
            z_in.at[n, h],
            send_sem.at[7],
            z_recv.at[n, h],
            {"fsdp": partner},
        )

    def comb_copy(n, h):
        slot = 4 - n
        return remote(
            comb.at[n, h],
            z_in.at[slot, h],
            send_sem.at[7],
            z_recv.at[slot, h],
            {"fsdp": 3 - z},
        )

    def join_copy(h):
        return remote(
            comb.at[2, h],
            z_in.at[2, h],
            send_sem.at[7],
            z_recv.at[2, h],
            {"fsdp": partner},
        )

    def weight_step(n, h):
        q, size = order[n], sizes[h]
        rhs = patches[pl.ds(aligned(q * block + h * lanes), size)]
        lhs = ctl[jnp.where(q == 0, 0, 1)]
        part[n, h, :, :size] = dot(lhs, rhs, ((1,), (1,))).astype(bf16)
        if h == 0 and n > 0:
            taken = 3 * chans - block

            @pl.when(q == 1)
            def _():
                rhs = patches[block : block + taken]
                part[n, h, :, :taken] = dot(ctl[0], rhs, ((1,), (1,))).astype(bf16)

        core_copy(n, h).start()

    def core_step(n, h):
        core_copy(n, h).wait_recv()
        mine_rows = part[n, h, pl.ds(aligned(h_rows * ci), h_rows)]
        half[n, h] = (mine_rows.astype(f32) + core_in[n, h].astype(f32)).astype(bf16)
        x_copy(n, h).start()

    def x_step(n, h):
        x_copy(n, h).wait_recv()
        mine_rows = half[n, h, pl.ds(aligned(q_rows * xi), q_rows)]
        quarter[n, h] = (mine_rows.astype(f32) + x_in[n, h].astype(f32)).astype(bf16)
        if n < 3:
            pl.when(outer)(lambda: z_copy(n, h).start())

    def comb_step(n, h):
        @pl.when(inner)
        def _():
            z_copy(n, h).wait_recv()
            value = quarter[n, h].astype(f32) + z_in[n, h].astype(f32)
            comb[n, h] = value.astype(bf16)
            comb_copy(n, h).start()

    def join_step(h):
        @pl.when(inner)
        def _():
            comb_copy(0, h).wait_recv()
            value = quarter[2, h].astype(f32) + z_in[4, h].astype(f32)
            comb[2, h] = value.astype(bf16)
            join_copy(h).start()

    def rep_copy(m, h):
        slot = (0, 2, 1)[m]
        src = final.at[h] if m < 2 else rep_in.at[h, 2]
        to = core_peer if m == 2 else reps[m]
        recv = rep_recv.at[1 if m == 1 else 0, h]
        return remote(src, rep_in.at[h, slot], send_sem.at[8], recv, {"rep": to})

    def place(ref, k, h):
        rows_k = pl.ds(aligned(q_rows * k), q_rows)
        wg_ref[rows_k, h * lanes : h * lanes + sizes[h]] = ref[:, : sizes[h]].astype(f32)

    def final_step(h):
        z_copy(2, h).wait_recv()
        pl.when(inner)(lambda: comb_copy(1, h).wait_recv())
        value = quarter[3, h].astype(f32) + z_in[2, h].astype(f32)
        value = value + jnp.where(inner, z_in[3, h].astype(f32), 0.0)
        final[h] = (value * scale).astype(bf16)
        rep_copy(1, h).start()
        rep_copy(0, h).start()

    def relay_step(h):
        rep_copy(1, h).wait_recv()
        rep_copy(2, h).start()

    def prepare():
        for r in range(rows):
            for odd in range(2):
                here = pl.ds(odd * cols, cols)
                normed = (norm[r + 1, :, here] - mean) * rstd
                z_val = gain * normed + shift
                sig = dsilu[r, :, here]
                norm[r + 1, :, here] = normed
                dsilu[r, :, here] = sig * (1.0 + z_val * (1.0 - sig))

    w_lane = lax.broadcasted_iota(jnp.int32, (outs_ch, block), 1)
    top = 3 * chans - block
    upto, since = -(-top // 128) * 128, top // 128 * 128

    def top_maps():
        first = jnp.where(w_lane[:, :upto] < top, wfull[1, :, :upto].astype(f32), 0.0).astype(bf16)
        value = dot(wfull[0], patches[:block]) + dot(first, patches[block : block + upto])
        p_out[...] = value[:, :cols].astype(bf16)
        when_up(lambda: p_copy.start())
        return value[:, cols:]

    def low_maps(above):
        rest = wfull[1, :, since:].astype(f32)
        rest = jnp.where(w_lane[:, since:] < top, 0.0, rest).astype(bf16)
        value = dot(rest, patches[block + since : 2 * block])
        for q in range(2, nz):
            value = value + dot(wfull[q], patches[q * block : (q + 1) * block])
        out_ref[0, 1] = (value[:, cols:] + above).astype(bf16)
        return value[:, :cols]

    def join_maps(value):
        @pl.when(z == 0)
        def _():
            p_in[...] = jnp.zeros(p_in.shape, bf16)

        when_down(lambda: p_copy.wait_recv())
        out_ref[0, 0] = (value + p_in[...].astype(f32)).astype(bf16)

    def edge_taps():
        below = ctl[0, :, :cols]
        done = 0
        q = 0
        while done < 3 * chans:
            take = min(block, 3 * chans - done)
            edge[done : done + take] = dot(wfull[q, :, :take], below, ((0,), (0,)))
            done += take
            q += 1

    def tap_at(row_tap, col_tap, i):
        tap = 3 * row_tap + col_tap
        here = slice(tap * chans, (tap + 1) * chans)
        if i == 2:
            return edge[here]
        return taps[here, i * cols : (i + 1) * cols]

    uv_cp = [
        remote(uv, uv_in.at[d], send_sem.at[9], uv_recv.at[0], {"fsdp": peers_z[d]})
        for d in range(nz - 1)
    ]

    def channel_sums():
        u_sum = jnp.zeros((chans, cols), f32)
        v_sum = jnp.zeros((chans, cols), f32)
        for r in range(rows):
            pairs = [(t, i) for i in range(3) for t in range(3) if 2 * i + t == r + 1]
            for odd in range(2):
                here = pl.ds(odd * cols, cols)
                grad = sum(tap_at(t, 1 + odd, i) for t, i in pairs)
                if odd == 1:
                    left = sum(tap_at(t, 0, i) for t, i in pairs)
                    moved = pltpu.roll(left, cols - 1, axis=1)
                    grad = grad + jnp.where(lane == cols - 1, 0.0, moved)
                value = grad * dsilu[r, :, here]
                zgrad[r, :, here] = value
                u_sum = u_sum + value * norm[r + 1, :, here]
                v_sum = v_sum + value
        uv[...] = row_sums(u_sum, v_sum)
        for d in (1, 0, 2):
            uv_cp[d].start()

    uvt_cp = [
        remote(uvt, uvt_in.at[m], send_sem.at[10], uv_recv.at[1], {"rep": reps[m]})
        for m in range(3)
    ]

    def input_grads():
        done(uv_in, uv_recv.at[0])
        total = uv[...]
        for d in range(nz - 1):
            total = total + uv_in[d]
        uvt[...] = total
        for cp in uvt_cp:
            cp.start()
        su_val, sv_val = group_sums(gv[0:1] * total)
        su_val, sv_val = su_val / count, sv_val / count
        merge = jnp.where(
            jnp.where(big_i < cols, 2 * big_i, 2 * (big_i - cols) + 1) == big_j, 1.0, 0.0
        ).astype(bf16)
        for r in range(rows):
            for odd in range(2):
                here = pl.ds(odd * cols, cols)
                value = rstd * (gain * zgrad[r, :, here] - sv_val - norm[r + 1, :, here] * su_val)
                patches[r * chans : (r + 1) * chans, here] = value.astype(bf16)
            dx_ref[0, r] = dot(patches[r * chans : (r + 1) * chans], merge).astype(bf16)

    def halo_wait():
        pl.when(z < nz - 2)(lambda: halo_c.wait_recv())

    def drain():
        own = wfull.at[0, pl.ds(0, q_rows)]
        three = wfull.at[0, pl.ds(0, 3 * q_rows)]

        @pl.when(z != 2)
        def _():
            stat_copy(0, 0, 0, partner).wait_send()

        @pl.when(z == 1)
        def _():
            stat_copy(1, 1, 1, 2).wait_send()

        @pl.when(z == 2)
        def _():
            for k in range(3):
                stat_copy(k, 1, 1, 1).wait_send()

        when_down(lambda: halo_c.wait_send())
        pl.when(outer)(lambda: done(own, send_sem.at[0]))

        @pl.when(inner)
        def _():
            done(wfull.at[0, pl.ds(0, 2 * q_rows)], send_sem.at[0])
            done(three, send_sem.at[1])

        for k in (2, 3, 4):
            done(three, send_sem.at[k])
        done(half, send_sem.at[5])
        done(quarter, send_sem.at[6])
        done(comb, send_sem.at[7])

    weight_step(0, 0)
    weight_step(0, 1)
    weight_step(1, 0)
    block_taps(z)
    core_step(0, 0)
    weight_step(1, 1)
    core_step(0, 1)
    w_arrive(0, 0, inner)
    w_arrive(1, 0, inner)
    w_arrive(0, 0, outer)
    core_step(1, 0)
    w_arrive(0, 1, inner)
    w_arrive(1, 1, inner)
    w_arrive(0, 1, outer)
    core_step(1, 1)
    prepare()
    halo_wait()
    weight_step(2, 0)
    weight_step(2, 1)
    weight_step(3, 0)
    core_step(2, 0)
    weight_step(3, 1)
    core_step(2, 1)
    x_step(0, 0)
    core_step(3, 0)
    w_arrive(2, 0, inner)
    w_arrive(1, 0, outer)
    x_step(0, 1)
    core_step(3, 1)
    w_arrive(2, 1, inner)
    w_arrive(1, 1, outer)
    w_second(0, 0)
    w_second(0, 1)
    x_step(1, 0)
    comb_step(0, 0)
    w_taps(0)
    x_step(1, 1)
    comb_step(0, 1)
    w_second(1, 0)
    w_arrive(2, 0, outer)
    w_second(1, 1)
    w_arrive(2, 1, outer)
    x_step(2, 0)
    comb_step(1, 0)
    join_step(0)
    w_taps(1)
    x_step(2, 1)
    comb_step(1, 1)
    join_step(1)
    w_second(2, 0)
    x_step(3, 0)
    w_second(2, 1)
    x_step(3, 1)
    w_taps(2)
    above = top_maps()
    final_step(0)
    edge_taps()
    channel_sums()
    final_step(1)
    low = low_maps(above)
    drain()
    input_grads()
    relay_step(0)
    relay_step(1)
    join_maps(low)

    owners = [2 * (1 - ci) + xi, 2 * (1 - ci) + 1 - xi, 2 * ci + 1 - xi]
    for h in range(2):
        place(final.at[h], mine, h)
        place(rep_in.at[h, 2], owners[2], h)
    done(uvt_in, uv_recv.at[1])
    total = uvt[...] + uvt_in[0] + uvt_in[1] + uvt_in[2]
    gg_ref[0:1] = total[0:1] * scale
    gg_ref[1:2] = total[4:5] * scale
    for h in range(2):
        done(rep_in.at[h, pl.ds(0, 2)], rep_recv.at[0, h])
        for m in range(2):
            place(rep_in.at[h, m], owners[m], h)

    when_up(lambda: p_copy.wait_send())
    done(uv_in, send_sem.at[9])
    done(uvt_in, send_sem.at[10])
    done(rep_in, send_sem.at[8])


def write_out(*refs):
    n = len(refs) // 2
    sems = refs[-1]
    copies = [pltpu.make_async_copy(refs[i], refs[n + i], sems.at[i]) for i in range(n)]
    for cp in copies:
        cp.start()
    for cp in copies:
        cp.wait()


def in_hbm(value):
    return pltpu.with_memory_space_constraint(value, pltpu.HBM)


def fused_shards(images, gains, conv_weight, cotangent):
    batch, rows, width, chans = images.shape
    block, outs_ch = conv_weight.shape
    nz = lax.axis_size("fsdp")
    fits = (batch, rows, cotangent.shape[1]) == (1, 4, 2) and chans % 64 == 0 and width == 256
    if not fits or block % 16 or outs_ch % 64 or nz * block != 9 * chans:
        return shards(images, gains, conv_weight, cotangent)
    if not block < 3 * chans < 2 * block or 3 * chans - block > 384:
        return shards(images, gains, conv_weight, cotangent)
    cols = width // 2
    q_rows = outs_ch // 4
    lanes = -(-block // 256) * 128
    wide = -(-chans // 128) * 128
    f32, bf16 = jnp.float32, jnp.bfloat16
    vmem = pltpu.VMEM
    dma = pltpu.SemaphoreType.DMA
    shapes = (
        jax.ShapeDtypeStruct((batch, rows // 2, outs_ch, cols), bf16),
        jax.ShapeDtypeStruct((batch, rows, chans, width), bf16),
        jax.ShapeDtypeStruct((outs_ch, block), f32),
        jax.ShapeDtypeStruct(gains.shape, f32),
    )
    results = pl.pallas_call(
        functools.partial(fused, nz),
        out_shape=tuple(vmem(shape.shape, shape.dtype) for shape in shapes),
        in_specs=[pl.BlockSpec(memory_space=pltpu.HBM)] * 4,
        out_specs=[pl.BlockSpec(memory_space=vmem)] * 4,
        scratch_shapes=[
            vmem((rows, chans, width), bf16),
            vmem(gains.shape, f32),
            vmem((2, outs_ch, width), bf16),
            vmem((width, width), bf16),
            vmem((chans, 3 * wide), bf16),
            vmem((outs_ch, cols), bf16),
            vmem((outs_ch, cols), bf16),
            vmem((rows + 1, chans, width), f32),
            vmem((rows, chans, width), f32),
            vmem((rows, chans, width), f32),
            vmem((nz * block, width), bf16),
            vmem((nz * block, width), f32),
            vmem((3 * chans, cols), f32),
            vmem((nz, outs_ch, block), bf16),
            vmem((3, 8, chans), f32),
            vmem((2, 8, chans), f32),
            vmem((nz, 2, outs_ch, lanes), bf16),
            vmem((nz, 2, 2 * q_rows, lanes), bf16),
            vmem((nz, 2, 2 * q_rows, lanes), bf16),
            vmem((nz, 2, q_rows, lanes), bf16),
            vmem((nz, 2, q_rows, lanes), bf16),
            vmem((5, 2, q_rows, lanes), bf16),
            vmem((3, 2, q_rows, lanes), bf16),
            vmem((2, q_rows, lanes), bf16),
            vmem((2, 3, q_rows, lanes), bf16),
            vmem((8, chans), f32),
            vmem((nz - 1, 8, chans), f32),
            vmem((8, chans), f32),
            vmem((3, 8, chans), f32),
            dma((rows + 4,)),
            dma((2, 2)),
            dma((3,)),
            dma((2,)),
            dma((11,)),
            dma((nz, 2)),
            dma((3, 2)),
            dma((3,)),
            dma((nz, 2)),
            dma((nz, 2)),
            dma((5, 2)),
            dma((2, 2)),
            dma((2,)),
        ],
        compiler_params=pltpu.CompilerParams(
            collective_id=0, has_side_effects=True, vmem_limit_bytes=48 * 1024 * 1024
        ),
    )(
        in_hbm(jnp.swapaxes(images, 2, 3)),
        in_hbm(gains),
        in_hbm(conv_weight.T),
        in_hbm(jnp.swapaxes(cotangent, 2, 3)),
    )
    output_maps, input_grad, weight_grad, gain_grad = pl.pallas_call(
        write_out,
        out_shape=shapes,
        in_specs=[pl.BlockSpec(memory_space=vmem)] * 4,
        out_specs=[pl.BlockSpec(memory_space=pltpu.HBM)] * 4,
        scratch_shapes=[dma((4,))],
        compiler_params=pltpu.CompilerParams(vmem_limit_bytes=1024 * 1024),
    )(*(pltpu.with_memory_space_constraint(value, vmem) for value in results))
    return (
        jnp.swapaxes(output_maps, 2, 3),
        jnp.swapaxes(input_grad, 2, 3),
        weight_grad.T,
        gain_grad,
    )


def solution(mesh):
    in_specs = (
        P(("groups", "rep"), "fsdp", None, None),
        P(),
        P("fsdp", None),
        P(("groups", "rep"), "fsdp", None, None),
    )
    out_specs = (
        P(("groups", "rep"), "fsdp", None, None),
        P(("groups", "rep"), "fsdp", None, None),
        P(("groups", "fsdp"), None),
        P("groups", None),
    )
    small = mesh.shape["groups"] == 2 and mesh.shape["rep"] == 4 and mesh.shape["fsdp"] == 4
    body = fused_shards if small else shards
    return jax.shard_map(body, mesh=mesh, in_specs=in_specs, out_specs=out_specs, check_vma=False)
```

```python
import functools

import jax
import jax.numpy as jnp
from jax import lax
from jax.experimental import pallas as pl
from jax.experimental.pallas import tpu as pltpu
from jax.sharding import PartitionSpec as P

GROUPS = 32
MESH = pl.DeviceIdType.MESH


def passed_along(shard, axis, by):
    size = lax.axis_size(axis)
    pairs = [(i, i + by) for i in range(size) if 0 <= i + by < size]
    return lax.ppermute(shard, axis, pairs)


def spread_taps(first, middle, last, axis):
    length = first.shape[axis]
    widths_end = [(0, 0)] * first.ndim
    widths_end[axis] = (0, 1)
    widths_start = [(0, 0)] * first.ndim
    widths_start[axis] = (1, 0)
    even = jnp.pad(first, widths_end) + jnp.pad(last, widths_start)
    odd = jnp.pad(middle, widths_end)
    merged = jnp.stack([even, odd], axis=axis + 1)
    shape = list(even.shape)
    shape[axis] = 2 * (length + 1)
    merged = merged.reshape(shape)
    return lax.slice_in_dim(merged, 0, 2 * length + 1, axis=axis)


def shards(images, gains, conv_weight, cotangent):
    batch, rows, width, chans = images.shape
    outs_ch = conv_weight.shape[1]
    n_fsdp = lax.axis_size("fsdp")
    per_group = chans // GROUPS
    x_val = images.astype(jnp.float32)
    grouped = x_val.reshape(batch, rows, width, GROUPS, per_group)
    part_one = jnp.sum(grouped, axis=(1, 2, 4))
    part_two = jnp.sum(grouped * grouped, axis=(1, 2, 4))
    full_weight = lax.all_gather(conv_weight, "fsdp", axis=0, tiled=True)
    sum_one, sum_two = lax.psum((part_one, part_two), "fsdp")
    count = rows * n_fsdp * width * per_group
    mean = sum_one / count
    rstd = 1.0 / jnp.sqrt(sum_two / count - mean * mean + 1e-05)
    normed_g = (grouped - mean[:, None, None, :, None]) * rstd[:, None, None, :, None]
    normed = normed_g.reshape(x_val.shape)
    z_val = gains[0] * normed + gains[1]
    act = (z_val * jax.nn.sigmoid(z_val)).astype(jnp.bfloat16)
    above = passed_along(act[:, rows - 1 : rows], "fsdp", 1)
    padded = jnp.concatenate([above, act], axis=1)
    kernel = full_weight.reshape(3, 3, chans, outs_ch)
    result = lax.conv_general_dilated(
        padded,
        kernel,
        (2, 2),
        ((0, 0), (1, 0)),
        dimension_numbers=("NHWC", "HWIO", "NHWC"),
        preferred_element_type=jnp.float32,
    )
    output_maps = result.astype(jnp.bfloat16)
    patch_grad = jnp.einsum(
        "bijo,ko->bijk", cotangent, full_weight, preferred_element_type=jnp.float32
    )
    half_rows, half_cols = (cotangent.shape[1], cotangent.shape[2])
    taps = patch_grad.reshape(batch, half_rows, half_cols, 3, 3, chans)
    by_row = [
        spread_taps(
            taps[:, :, :, row_tap, 0], taps[:, :, :, row_tap, 1], taps[:, :, :, row_tap, 2], 2
        )
        for row_tap in range(3)
    ]
    grid = spread_taps(by_row[0], by_row[1], by_row[2], 1)[:, :, 1:]
    from_below = passed_along(grid[:, 0:1].astype(jnp.bfloat16), "fsdp", -1).astype(jnp.float32)
    filler = jnp.zeros((batch, rows - 1, width, chans), jnp.float32)
    act_grad = grid[:, 1:] + jnp.concatenate([filler, from_below], axis=1)
    padded_cols = jnp.pad(padded, ((0, 0), (0, 0), (1, 0), (0, 0)))
    blocks = []
    for row_tap in range(3):
        for col_tap in range(3):
            window = padded_cols[:, row_tap : row_tap + rows : 2, col_tap : col_tap + width : 2]
            blocks.append(
                jnp.einsum("bijc,bijo->co", window, cotangent, preferred_element_type=jnp.float32)
            )
    total_pixels = batch * lax.axis_size("rep") * half_rows * n_fsdp * half_cols
    scale = 1.0 / jnp.sqrt(jnp.float32(total_pixels))
    weight_term = jnp.concatenate(blocks, axis=0) * scale
    sig = jax.nn.sigmoid(z_val)
    z_grad = act_grad * sig * (1.0 + z_val * (1.0 - sig))
    u_part = jnp.sum(z_grad * normed, axis=(1, 2))
    v_part = jnp.sum(z_grad, axis=(1, 2))
    u_sum, v_sum = lax.psum((u_part, v_part), "fsdp")
    gain_term = jnp.stack([jnp.sum(u_sum, axis=0), jnp.sum(v_sum, axis=0)]) * scale
    su_val = jnp.sum((gains[0] * u_sum).reshape(batch, GROUPS, per_group), axis=-1)
    sv_val = jnp.sum((gains[0] * v_sum).reshape(batch, GROUPS, per_group), axis=-1)
    scaled = (gains[0] * z_grad).reshape(grouped.shape)
    dx_val = rstd[:, None, None, :, None] * (
        scaled
        - sv_val[:, None, None, :, None] / count
        - normed_g * su_val[:, None, None, :, None] / count
    )
    input_grad = dx_val.reshape(x_val.shape).astype(jnp.bfloat16)
    owned = lax.psum_scatter(weight_term, "fsdp", scatter_dimension=0, tiled=True)
    weight_grad, gain_grad = (
        lax.psum(owned.astype(jnp.bfloat16), "rep").astype(jnp.float32),
        lax.psum(gain_term.astype(jnp.bfloat16), "rep").astype(jnp.float32),
    )
    return (output_maps, input_grad, weight_grad, gain_grad)


HIGHEST = lax.Precision.HIGHEST


def dot(lhs, rhs, contract=((1,), (0,)), precision=None):
    return lax.dot_general(
        lhs, rhs, (contract, ((), ())), precision=precision, preferred_element_type=jnp.float32
    )


def fused(
    nz,
    x_hbm,
    g_hbm,
    w_hbm,
    ct_hbm,
    out_ref,
    dx_ref,
    wg_ref,
    gg_ref,
    xv,
    gv,
    ctl,
    split,
    same,
    p_out,
    p_in,
    norm,
    dsilu,
    zgrad,
    patches,
    taps,
    edge,
    wfull,
    stat,
    stat_in,
    part,
    core_in,
    half,
    x_in,
    quarter,
    z_in,
    comb,
    final,
    rep_in,
    uv,
    uv_in,
    uvt,
    uvt_in,
    loc_sem,
    halo_sem,
    send_sem,
    w_recv,
    y_recv,
    cd_recv,
    core_recv,
    x_recv,
    z_recv,
    rep_recv,
    uv_recv,
):
    f32, bf16 = jnp.float32, jnp.bfloat16
    rows, chans, width = x_hbm.shape[1:]
    cols = width // 2
    outs_ch, block = w_hbm.shape
    q_rows = outs_ch // 4
    h_rows = outs_ch // 2
    lanes = part.shape[3]
    sizes = [lanes, block - lanes]
    w_cut = [(0, -(-q_rows // 32) * 16)]
    w_cut.append((w_cut[0][1], q_rows - w_cut[0][1]))
    count = rows * nz * width * (chans // GROUPS)
    scale = 1.0 / jnp.sqrt(f32(4 * nz * ct_hbm.shape[1] * cols))
    z = lax.axis_index("fsdp")
    rep = lax.axis_index("rep")
    yi = lax.axis_index("groups")
    xi, ci = rep // 2, rep % 2
    mine = 2 * ci + xi
    peers_z = [lax.rem(z + d, nz) for d in range(1, nz)]
    reps = [(2 * xi + 1 - ci), (2 * (1 - xi) + ci), (2 * (1 - xi) + 1 - ci)]
    core_peer, x_peer = reps[0], reps[1]
    pair = z // 2
    partner = z + 1 - 2 * (z % 2)
    inner = jnp.logical_or(z == 1, z == 2)
    outer = jnp.logical_or(z == 0, z == 3)
    order = [3 * (1 - pair), 2 - pair, partner, z]
    near_far = [partner, 2 - pair, 3 * (1 - pair)]
    one_order = [near_far[2], near_far[0], near_far[1]]
    two_order = [near_far[2], near_far[1], near_far[0]]
    others = [
        jnp.where(z == 1, one_order[k], jnp.where(z == 2, two_order[k], near_far[k]))
        for k in range(3)
    ]

    def aligned(value):
        return pl.multiple_of(value, 16)

    def remote(src, dst, send, recv, device):
        return pltpu.make_async_remote_copy(
            src_ref=src,
            dst_ref=dst,
            send_sem=send,
            recv_sem=recv,
            device_id=device,
            device_id_type=MESH,
        )

    def done(ref, sem):
        pltpu.make_async_copy(ref, ref, sem).wait()

    barrier = pltpu.get_barrier_semaphore()
    for peer in peers_z:
        pl.semaphore_signal(barrier, inc=1, device_id={"fsdp": peer}, device_id_type=MESH)
    for peer in reps:
        pl.semaphore_signal(barrier, inc=1, device_id={"rep": peer}, device_id_type=MESH)
    pl.semaphore_signal(barrier, inc=1, device_id={"groups": 1 - yi}, device_id_type=MESH)

    x_local = [pltpu.make_async_copy(x_hbm.at[0, r], xv.at[r], loc_sem.at[r]) for r in range(rows)]
    g_local = pltpu.make_async_copy(g_hbm, gv, loc_sem.at[rows])
    w_local = pltpu.make_async_copy(w_hbm, wfull.at[z], loc_sem.at[rows + 1])
    c_local = [
        pltpu.make_async_copy(
            ct_hbm.at[0, i], ctl.at[k, :, pl.ds(i * cols, cols)], loc_sem.at[rows + 2 + n]
        )
        for n, k, i in ((0, 1, 0), (0, 1, 1), (1, 0, 1))
    ]
    for cp in x_local + c_local + [w_local, g_local]:
        cp.start()

    big_i = lax.broadcasted_iota(jnp.int32, (width, width), 0)
    big_j = lax.broadcasted_iota(jnp.int32, (width, width), 1)
    inv = 1.0 / (chans // GROUPS)
    lane = lax.broadcasted_iota(jnp.int32, (chans, cols), 1)
    wide = same.shape[1] // 3
    ch_i = lax.broadcasted_iota(jnp.int32, (chans, wide), 0)
    ch_j = lax.broadcasted_iota(jnp.int32, (chans, wide), 1)
    grp_i = jnp.floor((ch_i.astype(f32) + 0.5) * inv)
    grp_j = jnp.floor((ch_j.astype(f32) + 0.5) * inv)
    same_one = jnp.where(jnp.where(ch_j < chans, grp_j, -1.0) == grp_i, 1.0, 0.0).astype(bf16)
    sums_i = lax.broadcasted_iota(jnp.int32, (8, width), 0)
    sums_j = lax.broadcasted_iota(jnp.int32, (8, width), 1)
    halves = jnp.where(jnp.where(sums_j < cols, 0, 4) == sums_i - lax.rem(sums_i, 4), 1.0, 0.0)
    halves = halves.astype(bf16)

    def three_terms(value):
        high = value.astype(bf16)
        rest = value - high.astype(f32)
        middle = rest.astype(bf16)
        low = (rest - middle.astype(f32)).astype(bf16)
        return high, middle, low

    def row_sums(first, second):
        both = jnp.concatenate([first, second], axis=1)
        terms = [dot(halves, term, ((1,), (1,))) for term in three_terms(both)]
        return terms[0] + (terms[1] + terms[2])

    def group_sums(total):
        pad = jnp.zeros((8, wide - chans), f32)
        terms = three_terms(jnp.concatenate([total, pad], axis=1))
        sums = dot(same[...], jnp.concatenate(terms, axis=1), ((1,), (1,)))
        first = jnp.broadcast_to(sums[:, 0:1], (chans, cols))
        second = jnp.broadcast_to(sums[:, 4:5], (chans, cols))
        return first, second

    @pl.when(z == nz - 1)
    def _():
        ctl[0, :, :cols] = jnp.zeros((chans, cols), bf16)

    halo_c = remote(
        ctl.at[1, :, pl.ds(0, cols)],
        ctl.at[0, :, pl.ds(0, cols)],
        halo_sem.at[0, 0],
        halo_sem.at[0, 1],
        {"fsdp": lax.rem(z + nz - 1, nz)},
    )
    p_copy = remote(
        p_out, p_in, halo_sem.at[1, 0], halo_sem.at[1, 1], {"fsdp": lax.rem(z + 1, nz)}
    )

    def w_spot(q, y_from, c):
        start, size = w_cut[c]
        return wfull.at[q, pl.ds(aligned(q_rows * (2 * ci + y_from) + start), size)]

    def own_w(to, c):
        spot = w_spot(z, yi, c)
        return remote(spot, spot, send_sem.at[0], w_recv.at[z, c], {"fsdp": to})

    def when_up(act):
        pl.when(z < nz - 1)(act)

    def when_down(act):
        pl.when(z > 0)(act)

    sum_one = jnp.zeros((chans, cols), f32)
    sum_two = jnp.zeros((chans, cols), f32)
    for r in range(rows):
        x_local[r].wait()
        even, odd = xv[r, :, :cols].astype(f32), xv[r, :, cols:].astype(f32)
        sum_one = sum_one + (even + odd)
        sum_two = sum_two + (even * even + odd * odd)
    stat[...] = row_sums(sum_one, sum_two)

    stat_cp = [
        remote(stat, stat_in.at[d], send_sem.at[11], uv_recv.at[2], {"fsdp": peers_z[d]})
        for d in range(nz - 1)
    ]
    pl.semaphore_wait(barrier, nz - 1 + 3 + 1)
    for d in (1, 0, 2):
        stat_cp[d].start()

    split[...] = jnp.where(
        jnp.where(big_j < cols, 2 * big_j, 2 * (big_j - cols) + 1) == big_i, 1.0, 0.0
    ).astype(bf16)
    for k in range(3):
        same[:, k * wide : (k + 1) * wide] = same_one
    done(ctl.at[1], loc_sem.at[rows + 2])
    c_local[2].wait()
    w_local.wait()

    @pl.when(z == nz - 1)
    def _():
        halo_c.start()
        for to in (1, 2):
            for c in range(2):
                own_w(to, c).start()

    for r in range(rows):
        norm[r + 1] = dot(xv[r], split[...])
    eye_i = lax.broadcasted_iota(jnp.int32, (chans, chans), 0)
    eye_j = lax.broadcasted_iota(jnp.int32, (chans, chans), 1)
    eye = jnp.where(eye_i == eye_j, 1.0, 0.0)
    g_local.wait()
    gains = dot(eye, gv[...], ((1,), (1,)), HIGHEST)
    gain = jnp.broadcast_to(gains[:, 0:1], (chans, cols))
    shift = jnp.broadcast_to(gains[:, 1:2], (chans, cols))

    done(stat_in, uv_recv.at[2])

    @pl.when(z == 0)
    def _():
        for to in (2, 1):
            for c in range(2):
                own_w(to, c).start()

    @pl.when(inner)
    def _():
        halo_c.start()
        for to in (3 * (1 - pair), partner, 3 - z):
            for c in range(2):
                own_w(to, c).start()

    def block_taps(q):
        here = pl.ds(aligned(q * block), block)
        taps[here] = dot(wfull[q], ctl[1], ((0,), (0,)))

    total = stat[...]
    for d in range(nz - 1):
        total = total + stat_in[d]
    sum_one, sum_two = group_sums(total)
    mean = sum_one / count
    rstd = 1.0 / jnp.sqrt(sum_two / count - mean * mean + 1e-05)
    slope = gain * rstd

    def put(row_tap, col_tap, i, lo, value):
        start = (3 * row_tap + col_tap) * chans + lo
        patches[start : start + value.shape[0], i * cols : (i + 1) * cols] = value

    step = 64

    def activate(r, users):
        for lo in range(0, chans, step):
            part_of = slice(lo, lo + step)
            for odd in range(2):
                here = pl.ds(odd * cols, cols)
                x_val = norm[r, part_of, here]
                z_val = (x_val - mean[part_of]) * slope[part_of] + shift[part_of]
                sig = 0.5 * jnp.tanh(0.5 * z_val) + 0.5
                act = z_val * sig
                dsilu[r - 1, part_of, here] = sig
                rounded = act.astype(bf16)
                for t, i in users:
                    put(t, 1 + odd, i, lo, rounded)
                if odd == 1:
                    moved = pltpu.roll(act, 1, axis=1)
                    moved = jnp.where(lane[part_of] == 0, 0.0, moved).astype(bf16)
                    for t, i in users:
                        put(t, 0, i, lo, moved)

    activate(1, [(1, 0)])
    activate(3, [(1, 1)])
    activate(2, [(2, 0), (0, 1)])
    activate(4, [(2, 1), (0, 0)])

    pl.when(z == nz - 2)(lambda: halo_c.wait_recv())

    def relay_w(c):
        spot = w_spot(others[0], yi, c)
        return remote(spot, spot, send_sem.at[1], w_recv.at[others[0], c], {"fsdp": partner})

    def w_arrive(j, c):
        q = others[j]
        spot = w_spot(q, yi, c)
        remote(spot, spot, send_sem.at[1], w_recv.at[q, c], {"fsdp": partner}).wait_recv()
        if j == 0:
            pl.when(inner)(lambda: relay_w(c).start())
        y_forward(j, c).start()
        c_forward(j, c).start()

    def y_forward(j, c):
        spot = w_spot(others[j], yi, c)
        return remote(spot, spot, send_sem.at[2], y_recv.at[j, c], {"groups": 1 - yi})

    def c_forward(j, c):
        spot = w_spot(others[j], yi, c)
        return remote(spot, spot, send_sem.at[3], cd_recv.at[j], {"rep": core_peer})

    def d_forward(j, c):
        spot = w_spot(others[j], 1 - yi, c)
        return remote(spot, spot, send_sem.at[4], cd_recv.at[j], {"rep": core_peer})

    def w_second(j, c):
        y_forward(j, c).wait_recv()
        d_forward(j, c).start()

    def w_taps(j):
        rows_in = pl.ds(aligned(h_rows * (1 - ci)), h_rows)
        done(wfull.at[others[j], rows_in], cd_recv.at[j])
        block_taps(others[j])

    def core_copy(n, h):
        return remote(
            part.at[n, h, pl.ds(aligned(h_rows * (1 - ci)), h_rows)],
            core_in.at[n, h],
            send_sem.at[5],
            core_recv.at[n, h],
            {"rep": core_peer},
        )

    def x_copy(n, h):
        return remote(
            half.at[n, h, pl.ds(aligned(q_rows * (1 - xi)), q_rows)],
            x_in.at[n, h],
            send_sem.at[6],
            x_recv.at[n, h],
            {"rep": x_peer},
        )

    def z_copy(n, h):
        return remote(
            quarter.at[n, h],
            z_in.at[n, h],
            send_sem.at[7],
            z_recv.at[n, h],
            {"fsdp": partner},
        )

    def comb_copy(n, h):
        return remote(
            comb.at[n, h],
            z_in.at[3, h],
            send_sem.at[7],
            z_recv.at[3, h],
            {"fsdp": order[n]},
        )

    def weight_step(n, h):
        q, size = order[n], sizes[h]
        rhs = patches[pl.ds(aligned(q * block + h * lanes), size)]
        lhs = ctl[jnp.where(q == 0, 0, 1)]
        part[n, h, :, :size] = dot(lhs, rhs, ((1,), (1,))).astype(bf16)
        if h == 0 and n > 0:
            taken = 3 * chans - block

            @pl.when(q == 1)
            def _():
                rhs = patches[block : block + taken]
                part[n, h, :, :taken] = dot(ctl[0], rhs, ((1,), (1,))).astype(bf16)

        core_copy(n, h).start()

    def core_step(n, h):
        core_copy(n, h).wait_recv()
        mine_rows = part[n, h, pl.ds(aligned(h_rows * ci), h_rows)]
        half[n, h] = (mine_rows.astype(f32) + core_in[n, h].astype(f32)).astype(bf16)
        x_copy(n, h).start()

    def x_step(n, h):
        x_copy(n, h).wait_recv()
        mine_rows = half[n, h, pl.ds(aligned(q_rows * xi), q_rows)]
        quarter[n, h] = (mine_rows.astype(f32) + x_in[n, h].astype(f32)).astype(bf16)
        if n == 2:
            z_copy(n, h).start()
        elif n < 2:
            pl.when(outer)(lambda: z_copy(n, h).start())

    def comb_step(n, h):
        @pl.when(inner)
        def _():
            z_copy(n, h).wait_recv()
            value = quarter[n, h].astype(f32) + z_in[n, h].astype(f32)
            comb[n, h] = value.astype(bf16)
            comb_copy(n, h).start()

    def rep_copy(m, h):
        slot = (0, 2, 1)[m]
        src = final.at[h] if m < 2 else rep_in.at[h, 2]
        to = core_peer if m == 2 else reps[m]
        recv = rep_recv.at[1 if m == 1 else 0, h]
        return remote(src, rep_in.at[h, slot], send_sem.at[8], recv, {"rep": to})

    def place(ref, k, h):
        rows_k = pl.ds(aligned(q_rows * k), q_rows)
        wg_ref[rows_k, h * lanes : h * lanes + sizes[h]] = ref[:, : sizes[h]].astype(f32)

    def final_step(h):
        z_copy(2, h).wait_recv()
        comb_copy(1, h).wait_recv()
        value = quarter[3, h].astype(f32) + z_in[2, h].astype(f32) + z_in[3, h].astype(f32)
        final[h] = (value * scale).astype(bf16)
        rep_copy(1, h).start()
        rep_copy(0, h).start()

    def relay_step(h):
        rep_copy(1, h).wait_recv()
        rep_copy(2, h).start()

    def prepare():
        for r in range(rows):
            for odd in range(2):
                here = pl.ds(odd * cols, cols)
                normed = (norm[r + 1, :, here] - mean) * rstd
                z_val = gain * normed + shift
                sig = dsilu[r, :, here]
                norm[r + 1, :, here] = normed
                dsilu[r, :, here] = sig * (1.0 + z_val * (1.0 - sig))

    w_lane = lax.broadcasted_iota(jnp.int32, (outs_ch, block), 1)
    top = 3 * chans - block
    upto, since = -(-top // 128) * 128, top // 128 * 128

    def top_maps():
        first = jnp.where(w_lane[:, :upto] < top, wfull[1, :, :upto].astype(f32), 0.0).astype(bf16)
        value = dot(wfull[0], patches[:block]) + dot(first, patches[block : block + upto])
        p_out[...] = value[:, :cols].astype(bf16)
        when_up(lambda: p_copy.start())
        return value[:, cols:]

    def low_maps(above):
        rest = wfull[1, :, since:].astype(f32)
        rest = jnp.where(w_lane[:, since:] < top, 0.0, rest).astype(bf16)
        value = dot(rest, patches[block + since : 2 * block])
        for q in range(2, nz):
            value = value + dot(wfull[q], patches[q * block : (q + 1) * block])
        out_ref[0, 1] = (value[:, cols:] + above).astype(bf16)
        return value[:, :cols]

    def join_maps(value):
        @pl.when(z == 0)
        def _():
            p_in[...] = jnp.zeros(p_in.shape, bf16)

        when_down(lambda: p_copy.wait_recv())
        out_ref[0, 0] = (value + p_in[...].astype(f32)).astype(bf16)

    def edge_taps():
        @pl.when(z < nz - 1)
        def _():
            below = ctl[0, :, :cols]
            edge[:block] = dot(wfull[0], below, ((0,), (0,)))
            edge[block:] = dot(wfull[1, :, :top], below, ((0,), (0,)))

        @pl.when(z == nz - 1)
        def _():
            edge[...] = jnp.zeros(edge.shape, f32)

    def tap_at(row_tap, col_tap, i):
        tap = 3 * row_tap + col_tap
        here = slice(tap * chans, (tap + 1) * chans)
        if i == 2:
            return edge[here]
        return taps[here, i * cols : (i + 1) * cols]

    uv_cp = [
        remote(uv, uv_in.at[d], send_sem.at[9], uv_recv.at[0], {"fsdp": peers_z[d]})
        for d in range(nz - 1)
    ]

    def channel_sums():
        u_sum = jnp.zeros((chans, cols), f32)
        v_sum = jnp.zeros((chans, cols), f32)
        for r in range(rows):
            pairs = [(t, i) for i in range(3) for t in range(3) if 2 * i + t == r + 1]
            for odd in range(2):
                here = pl.ds(odd * cols, cols)
                grad = sum(tap_at(t, 1 + odd, i) for t, i in pairs)
                if odd == 1:
                    left = sum(tap_at(t, 0, i) for t, i in pairs)
                    moved = pltpu.roll(left, cols - 1, axis=1)
                    grad = grad + jnp.where(lane == cols - 1, 0.0, moved)
                value = grad * dsilu[r, :, here]
                zgrad[r, :, here] = value
                u_sum = u_sum + value * norm[r + 1, :, here]
                v_sum = v_sum + value
        uv[...] = row_sums(u_sum, v_sum)
        for d in (1, 0, 2):
            uv_cp[d].start()

    uvt_cp = [
        remote(uvt, uvt_in.at[m], send_sem.at[10], uv_recv.at[1], {"rep": reps[m]})
        for m in range(3)
    ]

    def input_grads():
        done(uv_in, uv_recv.at[0])
        total = uv[...]
        for d in range(nz - 1):
            total = total + uv_in[d]
        uvt[...] = total
        for cp in uvt_cp:
            cp.start()
        su_val, sv_val = group_sums(gv[0:1] * total)
        su_val, sv_val = su_val / count, sv_val / count
        merge = jnp.where(
            jnp.where(big_i < cols, 2 * big_i, 2 * (big_i - cols) + 1) == big_j, 1.0, 0.0
        ).astype(bf16)
        def grad_row(r):
            for odd in range(2):
                here = pl.ds(odd * cols, cols)
                value = rstd * (gain * zgrad[r, :, here] - sv_val - norm[r + 1, :, here] * su_val)
                patches[r * chans : (r + 1) * chans, here] = value.astype(bf16)
            dx_ref[0, r] = dot(patches[r * chans : (r + 1) * chans], merge).astype(bf16)

        half_done = rows // 2
        for r in range(half_done):
            grad_row(r)
        relay_step(0)
        for r in range(half_done, rows):
            grad_row(r)
        relay_step(1)

    def halo_wait():
        pl.when(z < nz - 2)(lambda: halo_c.wait_recv())

    def drain():
        own = wfull.at[0, pl.ds(0, q_rows)]
        three = wfull.at[0, pl.ds(0, 3 * q_rows)]

        done(stat_in, send_sem.at[11])
        when_down(lambda: halo_c.wait_send())
        pl.when(outer)(lambda: done(wfull.at[0, pl.ds(0, 2 * q_rows)], send_sem.at[0]))

        @pl.when(inner)
        def _():
            done(three, send_sem.at[0])
            done(own, send_sem.at[1])

        for k in (2, 3, 4):
            done(three, send_sem.at[k])
        done(half, send_sem.at[5])
        done(quarter, send_sem.at[6])
        done(comb, send_sem.at[7])

    weight_step(0, 0)
    weight_step(0, 1)
    weight_step(1, 0)
    weight_step(1, 1)
    block_taps(z)
    core_step(0, 0)
    core_step(0, 1)
    core_step(1, 0)
    core_step(1, 1)
    w_arrive(0, 0)
    w_arrive(0, 1)
    halo_wait()
    weight_step(2, 0)
    weight_step(2, 1)
    weight_step(3, 0)
    x_step(0, 0)
    core_step(2, 0)
    w_arrive(1, 0)
    core_step(2, 1)
    weight_step(3, 1)
    x_step(0, 1)
    w_arrive(1, 1)
    core_step(3, 0)
    core_step(3, 1)
    w_second(0, 0)
    w_second(0, 1)
    x_step(1, 0)
    w_arrive(2, 0)
    w_arrive(2, 1)
    comb_step(0, 0)
    x_step(1, 1)
    w_second(1, 0)
    comb_step(0, 1)
    w_taps(0)
    w_second(1, 1)
    x_step(2, 0)
    comb_step(1, 0)
    x_step(2, 1)
    w_second(2, 0)
    w_taps(1)
    comb_step(1, 1)
    w_second(2, 1)
    edge_taps()
    x_step(3, 0)
    prepare()
    w_taps(2)
    x_step(3, 1)
    final_step(0)
    channel_sums()
    final_step(1)
    above = top_maps()
    low = low_maps(above)
    drain()
    input_grads()
    join_maps(low)

    owners = [2 * (1 - ci) + xi, 2 * (1 - ci) + 1 - xi, 2 * ci + 1 - xi]
    for h in range(2):
        place(final.at[h], mine, h)
        place(rep_in.at[h, 2], owners[2], h)
    done(uvt_in, uv_recv.at[1])
    total = uvt[...] + uvt_in[0] + uvt_in[1] + uvt_in[2]
    gg_ref[0:1] = total[0:1] * scale
    gg_ref[1:2] = total[4:5] * scale
    for h in range(2):
        done(rep_in.at[h, pl.ds(0, 2)], rep_recv.at[0, h])
        for m in range(2):
            place(rep_in.at[h, m], owners[m], h)

    when_up(lambda: p_copy.wait_send())
    done(uv_in, send_sem.at[9])
    done(uvt_in, send_sem.at[10])
    done(rep_in, send_sem.at[8])


def write_out(*refs):
    n = len(refs) // 2
    sems = refs[-1]
    copies = [pltpu.make_async_copy(refs[i], refs[n + i], sems.at[i]) for i in range(n)]
    for cp in copies:
        cp.start()
    for cp in copies:
        cp.wait()


def in_hbm(value):
    return pltpu.with_memory_space_constraint(value, pltpu.HBM)


def fused_shards(images, gains, conv_weight, cotangent):
    batch, rows, width, chans = images.shape
    block, outs_ch = conv_weight.shape
    nz = lax.axis_size("fsdp")
    fits = (batch, rows, cotangent.shape[1]) == (1, 4, 2) and chans % 64 == 0 and width == 256
    if not fits or block % 16 or outs_ch % 64 or nz * block != 9 * chans:
        return shards(images, gains, conv_weight, cotangent)
    if not block < 3 * chans < 2 * block or 3 * chans - block > 384:
        return shards(images, gains, conv_weight, cotangent)
    cols = width // 2
    q_rows = outs_ch // 4
    lanes = -(-block // 256) * 128
    wide = -(-chans // 128) * 128
    f32, bf16 = jnp.float32, jnp.bfloat16
    vmem = pltpu.VMEM
    dma = pltpu.SemaphoreType.DMA
    shapes = (
        jax.ShapeDtypeStruct((batch, rows // 2, outs_ch, cols), bf16),
        jax.ShapeDtypeStruct((batch, rows, chans, width), bf16),
        jax.ShapeDtypeStruct((outs_ch, block), f32),
        jax.ShapeDtypeStruct(gains.shape, f32),
    )
    results = pl.pallas_call(
        functools.partial(fused, nz),
        out_shape=tuple(vmem(shape.shape, shape.dtype) for shape in shapes),
        in_specs=[pl.BlockSpec(memory_space=pltpu.HBM)] * 4,
        out_specs=[pl.BlockSpec(memory_space=vmem)] * 4,
        scratch_shapes=[
            vmem((rows, chans, width), bf16),
            vmem(gains.shape, f32),
            vmem((2, outs_ch, width), bf16),
            vmem((width, width), bf16),
            vmem((chans, 3 * wide), bf16),
            vmem((outs_ch, cols), bf16),
            vmem((outs_ch, cols), bf16),
            vmem((rows + 1, chans, width), f32),
            vmem((rows, chans, width), f32),
            vmem((rows, chans, width), f32),
            vmem((nz * block, width), bf16),
            vmem((nz * block, width), f32),
            vmem((3 * chans, cols), f32),
            vmem((nz, outs_ch, block), bf16),
            vmem((8, chans), f32),
            vmem((nz - 1, 8, chans), f32),
            vmem((nz, 2, outs_ch, lanes), bf16),
            vmem((nz, 2, 2 * q_rows, lanes), bf16),
            vmem((nz, 2, 2 * q_rows, lanes), bf16),
            vmem((nz, 2, q_rows, lanes), bf16),
            vmem((nz, 2, q_rows, lanes), bf16),
            vmem((4, 2, q_rows, lanes), bf16),
            vmem((3, 2, q_rows, lanes), bf16),
            vmem((2, q_rows, lanes), bf16),
            vmem((2, 3, q_rows, lanes), bf16),
            vmem((8, chans), f32),
            vmem((nz - 1, 8, chans), f32),
            vmem((8, chans), f32),
            vmem((3, 8, chans), f32),
            dma((rows + 4,)),
            dma((2, 2)),
            dma((12,)),
            dma((nz, 2)),
            dma((3, 2)),
            dma((3,)),
            dma((nz, 2)),
            dma((nz, 2)),
            dma((4, 2)),
            dma((2, 2)),
            dma((3,)),
        ],
        compiler_params=pltpu.CompilerParams(
            collective_id=0, has_side_effects=True, vmem_limit_bytes=48 * 1024 * 1024
        ),
    )(
        in_hbm(jnp.swapaxes(images, 2, 3)),
        in_hbm(gains),
        in_hbm(conv_weight.T),
        in_hbm(jnp.swapaxes(cotangent, 2, 3)),
    )
    output_maps, input_grad, weight_grad, gain_grad = pl.pallas_call(
        write_out,
        out_shape=shapes,
        in_specs=[pl.BlockSpec(memory_space=vmem)] * 4,
        out_specs=[pl.BlockSpec(memory_space=pltpu.HBM)] * 4,
        scratch_shapes=[dma((4,))],
        compiler_params=pltpu.CompilerParams(vmem_limit_bytes=1024 * 1024),
    )(*(pltpu.with_memory_space_constraint(value, vmem) for value in results))
    return (
        jnp.swapaxes(output_maps, 2, 3),
        jnp.swapaxes(input_grad, 2, 3),
        weight_grad.T,
        gain_grad,
    )


def solution(mesh):
    in_specs = (
        P(("groups", "rep"), "fsdp", None, None),
        P(),
        P("fsdp", None),
        P(("groups", "rep"), "fsdp", None, None),
    )
    out_specs = (
        P(("groups", "rep"), "fsdp", None, None),
        P(("groups", "rep"), "fsdp", None, None),
        P(("groups", "fsdp"), None),
        P("groups", None),
    )
    small = mesh.shape["groups"] == 2 and mesh.shape["rep"] == 4 and mesh.shape["fsdp"] == 4
    body = fused_shards if small else shards
    return jax.shard_map(body, mesh=mesh, in_specs=in_specs, out_specs=out_specs, check_vma=False)
```

```python
import functools

import jax
import jax.numpy as jnp
from jax import lax
from jax.experimental import pallas as pl
from jax.experimental.pallas import tpu as pltpu
from jax.sharding import PartitionSpec as P

GROUPS = 32
MESH = pl.DeviceIdType.MESH


def passed_along(shard, axis, by):
    size = lax.axis_size(axis)
    pairs = [(i, i + by) for i in range(size) if 0 <= i + by < size]
    return lax.ppermute(shard, axis, pairs)


def spread_taps(first, middle, last, axis):
    length = first.shape[axis]
    widths_end = [(0, 0)] * first.ndim
    widths_end[axis] = (0, 1)
    widths_start = [(0, 0)] * first.ndim
    widths_start[axis] = (1, 0)
    even = jnp.pad(first, widths_end) + jnp.pad(last, widths_start)
    odd = jnp.pad(middle, widths_end)
    merged = jnp.stack([even, odd], axis=axis + 1)
    shape = list(even.shape)
    shape[axis] = 2 * (length + 1)
    merged = merged.reshape(shape)
    return lax.slice_in_dim(merged, 0, 2 * length + 1, axis=axis)


def shards(images, gains, conv_weight, cotangent):
    batch, rows, width, chans = images.shape
    outs_ch = conv_weight.shape[1]
    n_fsdp = lax.axis_size("fsdp")
    per_group = chans // GROUPS
    x_val = images.astype(jnp.float32)
    grouped = x_val.reshape(batch, rows, width, GROUPS, per_group)
    part_one = jnp.sum(grouped, axis=(1, 2, 4))
    part_two = jnp.sum(grouped * grouped, axis=(1, 2, 4))
    full_weight = lax.all_gather(conv_weight, "fsdp", axis=0, tiled=True)
    sum_one, sum_two = lax.psum((part_one, part_two), "fsdp")
    count = rows * n_fsdp * width * per_group
    mean = sum_one / count
    rstd = 1.0 / jnp.sqrt(sum_two / count - mean * mean + 1e-05)
    normed_g = (grouped - mean[:, None, None, :, None]) * rstd[:, None, None, :, None]
    normed = normed_g.reshape(x_val.shape)
    z_val = gains[0] * normed + gains[1]
    act = (z_val * jax.nn.sigmoid(z_val)).astype(jnp.bfloat16)
    above = passed_along(act[:, rows - 1 : rows], "fsdp", 1)
    padded = jnp.concatenate([above, act], axis=1)
    kernel = full_weight.reshape(3, 3, chans, outs_ch)
    result = lax.conv_general_dilated(
        padded,
        kernel,
        (2, 2),
        ((0, 0), (1, 0)),
        dimension_numbers=("NHWC", "HWIO", "NHWC"),
        preferred_element_type=jnp.float32,
    )
    output_maps = result.astype(jnp.bfloat16)
    patch_grad = jnp.einsum(
        "bijo,ko->bijk", cotangent, full_weight, preferred_element_type=jnp.float32
    )
    half_rows, half_cols = (cotangent.shape[1], cotangent.shape[2])
    taps = patch_grad.reshape(batch, half_rows, half_cols, 3, 3, chans)
    by_row = [
        spread_taps(
            taps[:, :, :, row_tap, 0], taps[:, :, :, row_tap, 1], taps[:, :, :, row_tap, 2], 2
        )
        for row_tap in range(3)
    ]
    grid = spread_taps(by_row[0], by_row[1], by_row[2], 1)[:, :, 1:]
    from_below = passed_along(grid[:, 0:1].astype(jnp.bfloat16), "fsdp", -1).astype(jnp.float32)
    filler = jnp.zeros((batch, rows - 1, width, chans), jnp.float32)
    act_grad = grid[:, 1:] + jnp.concatenate([filler, from_below], axis=1)
    padded_cols = jnp.pad(padded, ((0, 0), (0, 0), (1, 0), (0, 0)))
    blocks = []
    for row_tap in range(3):
        for col_tap in range(3):
            window = padded_cols[:, row_tap : row_tap + rows : 2, col_tap : col_tap + width : 2]
            blocks.append(
                jnp.einsum("bijc,bijo->co", window, cotangent, preferred_element_type=jnp.float32)
            )
    total_pixels = batch * lax.axis_size("rep") * half_rows * n_fsdp * half_cols
    scale = 1.0 / jnp.sqrt(jnp.float32(total_pixels))
    weight_term = jnp.concatenate(blocks, axis=0) * scale
    sig = jax.nn.sigmoid(z_val)
    z_grad = act_grad * sig * (1.0 + z_val * (1.0 - sig))
    u_part = jnp.sum(z_grad * normed, axis=(1, 2))
    v_part = jnp.sum(z_grad, axis=(1, 2))
    u_sum, v_sum = lax.psum((u_part, v_part), "fsdp")
    gain_term = jnp.stack([jnp.sum(u_sum, axis=0), jnp.sum(v_sum, axis=0)]) * scale
    su_val = jnp.sum((gains[0] * u_sum).reshape(batch, GROUPS, per_group), axis=-1)
    sv_val = jnp.sum((gains[0] * v_sum).reshape(batch, GROUPS, per_group), axis=-1)
    scaled = (gains[0] * z_grad).reshape(grouped.shape)
    dx_val = rstd[:, None, None, :, None] * (
        scaled
        - sv_val[:, None, None, :, None] / count
        - normed_g * su_val[:, None, None, :, None] / count
    )
    input_grad = dx_val.reshape(x_val.shape).astype(jnp.bfloat16)
    owned = lax.psum_scatter(weight_term, "fsdp", scatter_dimension=0, tiled=True)
    weight_grad, gain_grad = (
        lax.psum(owned.astype(jnp.bfloat16), "rep").astype(jnp.float32),
        lax.psum(gain_term.astype(jnp.bfloat16), "rep").astype(jnp.float32),
    )
    return (output_maps, input_grad, weight_grad, gain_grad)


HIGHEST = lax.Precision.HIGHEST


def dot(lhs, rhs, contract=((1,), (0,)), precision=None):
    return lax.dot_general(
        lhs, rhs, (contract, ((), ())), precision=precision, preferred_element_type=jnp.float32
    )


def fused(
    nz,
    x_hbm,
    g_hbm,
    w_hbm,
    ct_hbm,
    out_ref,
    dx_ref,
    wg_ref,
    gg_ref,
    xv,
    gv,
    ctl,
    split,
    same,
    p_out,
    p_in,
    norm,
    dsilu,
    zgrad,
    patches,
    taps,
    edge,
    wfull,
    stat,
    stat_in,
    part,
    core_in,
    half,
    x_in,
    quarter,
    z_in,
    comb,
    final,
    rep_in,
    uv,
    uv_in,
    uv_far,
    loc_sem,
    halo_sem,
    send_sem,
    w_recv,
    y_recv,
    cd_recv,
    core_recv,
    x_recv,
    z_recv,
    rep_recv,
    uv_recv,
):
    f32, bf16 = jnp.float32, jnp.bfloat16
    rows, chans, width = x_hbm.shape[1:]
    cols = width // 2
    outs_ch, block = w_hbm.shape
    q_rows = outs_ch // 4
    h_rows = outs_ch // 2
    lanes = part.shape[3]
    pieces = part.shape[1]
    sizes = [min(lanes, block - h * lanes) for h in range(pieces)]
    w_cut = [(0, -(-q_rows // 32) * 16)]
    w_cut.append((w_cut[0][1], q_rows - w_cut[0][1]))
    count = rows * nz * width * (chans // GROUPS)
    scale = 1.0 / jnp.sqrt(f32(4 * nz * ct_hbm.shape[1] * cols))
    z = lax.axis_index("fsdp")
    rep = lax.axis_index("rep")
    yi = lax.axis_index("groups")
    xi, ci = rep // 2, rep % 2
    mine = 2 * ci + xi
    peers_z = [lax.rem(z + d, nz) for d in range(1, nz)]
    reps = [(2 * xi + 1 - ci), (2 * (1 - xi) + ci), (2 * (1 - xi) + 1 - ci)]
    core_peer, x_peer = reps[0], reps[1]
    pair = z // 2
    partner = z + 1 - 2 * (z % 2)
    inner = jnp.logical_or(z == 1, z == 2)
    outer = jnp.logical_or(z == 0, z == 3)
    order = [3 * (1 - pair), 2 - pair, partner, z]
    near_far = [partner, 2 - pair, 3 * (1 - pair)]
    one_order = [near_far[2], near_far[0], near_far[1]]
    two_order = [near_far[2], near_far[1], near_far[0]]
    others = [
        jnp.where(z == 1, one_order[k], jnp.where(z == 2, two_order[k], near_far[k]))
        for k in range(3)
    ]

    def aligned(value):
        return pl.multiple_of(value, 16)

    def remote(src, dst, send, recv, device):
        return pltpu.make_async_remote_copy(
            src_ref=src,
            dst_ref=dst,
            send_sem=send,
            recv_sem=recv,
            device_id=device,
            device_id_type=MESH,
        )

    def done(ref, sem):
        pltpu.make_async_copy(ref, ref, sem).wait()

    barrier = pltpu.get_barrier_semaphore()
    for peer in peers_z:
        pl.semaphore_signal(barrier, inc=1, device_id={"fsdp": peer}, device_id_type=MESH)
    for peer in reps:
        pl.semaphore_signal(barrier, inc=1, device_id={"rep": peer}, device_id_type=MESH)
    pl.semaphore_signal(barrier, inc=1, device_id={"groups": 1 - yi}, device_id_type=MESH)

    x_local = [pltpu.make_async_copy(x_hbm.at[0, r], xv.at[r], loc_sem.at[r]) for r in range(rows)]
    g_local = pltpu.make_async_copy(g_hbm, gv, loc_sem.at[rows])
    w_local = pltpu.make_async_copy(w_hbm, wfull.at[z], loc_sem.at[rows + 1])
    c_local = [
        pltpu.make_async_copy(
            ct_hbm.at[0, i], ctl.at[k, :, pl.ds(i * cols, cols)], loc_sem.at[rows + 2 + n]
        )
        for n, k, i in ((0, 1, 0), (0, 1, 1), (1, 0, 1))
    ]
    for cp in x_local + c_local + [w_local, g_local]:
        cp.start()

    big_i = lax.broadcasted_iota(jnp.int32, (width, width), 0)
    big_j = lax.broadcasted_iota(jnp.int32, (width, width), 1)
    inv = 1.0 / (chans // GROUPS)
    lane = lax.broadcasted_iota(jnp.int32, (chans, cols), 1)
    wide = same.shape[1] // 3
    ch_i = lax.broadcasted_iota(jnp.int32, (chans, wide), 0)
    ch_j = lax.broadcasted_iota(jnp.int32, (chans, wide), 1)
    grp_i = jnp.floor((ch_i.astype(f32) + 0.5) * inv)
    grp_j = jnp.floor((ch_j.astype(f32) + 0.5) * inv)
    same_one = jnp.where(jnp.where(ch_j < chans, grp_j, -1.0) == grp_i, 1.0, 0.0).astype(bf16)
    sums_i = lax.broadcasted_iota(jnp.int32, (8, width), 0)
    sums_j = lax.broadcasted_iota(jnp.int32, (8, width), 1)
    halves = jnp.where(jnp.where(sums_j < cols, 0, 4) == sums_i - lax.rem(sums_i, 4), 1.0, 0.0)
    halves = halves.astype(bf16)

    def three_terms(value):
        high = value.astype(bf16)
        rest = value - high.astype(f32)
        middle = rest.astype(bf16)
        low = (rest - middle.astype(f32)).astype(bf16)
        return high, middle, low

    def row_sums(first, second):
        both = jnp.concatenate([first, second], axis=1)
        terms = [dot(halves, term, ((1,), (1,))) for term in three_terms(both)]
        return terms[0] + (terms[1] + terms[2])

    def put_sums(ref, sums):
        ref[0:1] = sums[0:1]
        ref[1:2] = sums[4:5]

    def group_sums(total):
        pad = jnp.zeros((2, wide - chans), f32)
        terms = three_terms(jnp.concatenate([total, pad], axis=1))
        sums = dot(same[...], jnp.concatenate(terms, axis=1), ((1,), (1,)))
        first = jnp.broadcast_to(sums[:, 0:1], (chans, cols))
        second = jnp.broadcast_to(sums[:, 1:2], (chans, cols))
        return first, second

    @pl.when(z == nz - 1)
    def _():
        ctl[0, :, :cols] = jnp.zeros((chans, cols), bf16)

    halo_c = remote(
        ctl.at[1, :, pl.ds(0, cols)],
        ctl.at[0, :, pl.ds(0, cols)],
        halo_sem.at[0, 0],
        halo_sem.at[0, 1],
        {"fsdp": lax.rem(z + nz - 1, nz)},
    )
    p_copy = remote(
        p_out, p_in, halo_sem.at[1, 0], halo_sem.at[1, 1], {"fsdp": lax.rem(z + 1, nz)}
    )

    def w_spot(q, y_from, c):
        start, size = w_cut[c]
        return wfull.at[q, pl.ds(aligned(q_rows * (2 * ci + y_from) + start), size)]

    def own_w(to, c):
        spot = w_spot(z, yi, c)
        return remote(spot, spot, send_sem.at[0], w_recv.at[z, c], {"fsdp": to})

    def when_up(act):
        pl.when(z < nz - 1)(act)

    def when_down(act):
        pl.when(z > 0)(act)

    sum_one = jnp.zeros((chans, cols), f32)
    sum_two = jnp.zeros((chans, cols), f32)
    for r in range(rows):
        x_local[r].wait()
        even, odd = xv[r, :, :cols].astype(f32), xv[r, :, cols:].astype(f32)
        sum_one = sum_one + (even + odd)
        sum_two = sum_two + (even * even + odd * odd)
    put_sums(stat, row_sums(sum_one, sum_two))

    stat_cp = [
        remote(stat, stat_in.at[d], send_sem.at[11], uv_recv.at[2], {"fsdp": peers_z[d]})
        for d in range(nz - 1)
    ]
    pl.semaphore_wait(barrier, nz - 1 + 3 + 1)
    for d in (1, 0, 2):
        stat_cp[d].start()

    split[...] = jnp.where(
        jnp.where(big_j < cols, 2 * big_j, 2 * (big_j - cols) + 1) == big_i, 1.0, 0.0
    ).astype(bf16)
    for k in range(3):
        same[:, k * wide : (k + 1) * wide] = same_one
    done(ctl.at[1], loc_sem.at[rows + 2])
    c_local[2].wait()
    w_local.wait()

    @pl.when(z == nz - 1)
    def _():
        halo_c.start()
        for to in (1, 2):
            for c in range(2):
                own_w(to, c).start()

    for r in range(rows):
        norm[r + 1] = dot(xv[r], split[...])
    eye_i = lax.broadcasted_iota(jnp.int32, (chans, chans), 0)
    eye_j = lax.broadcasted_iota(jnp.int32, (chans, chans), 1)
    eye = jnp.where(eye_i == eye_j, 1.0, 0.0)
    g_local.wait()
    gains = dot(eye, gv[...], ((1,), (1,)), HIGHEST)
    gain = jnp.broadcast_to(gains[:, 0:1], (chans, cols))
    shift = jnp.broadcast_to(gains[:, 1:2], (chans, cols))

    def block_taps(q):
        here = pl.ds(aligned(q * block), block)
        taps[here] = dot(wfull[q], ctl[1], ((0,), (0,)))

    block_taps(z)
    done(stat_in, uv_recv.at[2])

    @pl.when(z == 0)
    def _():
        for to in (2, 1):
            for c in range(2):
                own_w(to, c).start()

    @pl.when(inner)
    def _():
        halo_c.start()
        for to in (3 * (1 - pair), partner, 3 - z):
            for c in range(2):
                own_w(to, c).start()

    total = stat[...]
    for d in range(nz - 1):
        total = total + stat_in[d]
    sum_one, sum_two = group_sums(total)
    mean = sum_one / count
    rstd = 1.0 / jnp.sqrt(sum_two / count - mean * mean + 1e-05)
    slope = gain * rstd

    def put(row_tap, col_tap, i, lo, value):
        start = (3 * row_tap + col_tap) * chans + lo
        patches[start : start + value.shape[0], i * cols : (i + 1) * cols] = value

    step = 64

    def activate(r, users):
        for lo in range(0, chans, step):
            part_of = slice(lo, lo + step)
            for odd in range(2):
                here = pl.ds(odd * cols, cols)
                x_val = norm[r, part_of, here]
                z_val = (x_val - mean[part_of]) * slope[part_of] + shift[part_of]
                sig = 0.5 * jnp.tanh(0.5 * z_val) + 0.5
                act = z_val * sig
                dsilu[r - 1, part_of, here] = sig
                rounded = act.astype(bf16)
                for t, i in users:
                    put(t, 1 + odd, i, lo, rounded)
                if odd == 1:
                    moved = pltpu.roll(act, 1, axis=1)
                    moved = jnp.where(lane[part_of] == 0, 0.0, moved).astype(bf16)
                    for t, i in users:
                        put(t, 0, i, lo, moved)

    activate(2, [(2, 0), (0, 1)])
    activate(4, [(2, 1), (0, 0)])

    pl.when(z == nz - 2)(lambda: halo_c.wait_recv())

    def relay_w(c):
        spot = w_spot(others[0], yi, c)
        return remote(spot, spot, send_sem.at[1], w_recv.at[others[0], c], {"fsdp": partner})

    def w_arrive(j, c, role=None):
        def take():
            q = others[j]
            spot = w_spot(q, yi, c)
            remote(spot, spot, send_sem.at[1], w_recv.at[q, c], {"fsdp": partner}).wait_recv()
            if j == 0 and role is not outer:
                pl.when(inner)(lambda: relay_w(c).start())
            y_forward(j, c).start()
            c_forward(j, c).start()

        if role is None:
            take()
        else:
            pl.when(role)(take)

    def y_forward(j, c):
        spot = w_spot(others[j], yi, c)
        return remote(spot, spot, send_sem.at[2], y_recv.at[j, c], {"groups": 1 - yi})

    def c_forward(j, c):
        spot = w_spot(others[j], yi, c)
        return remote(spot, spot, send_sem.at[3], cd_recv.at[j], {"rep": core_peer})

    def d_forward(j, c):
        spot = w_spot(others[j], 1 - yi, c)
        return remote(spot, spot, send_sem.at[4], cd_recv.at[j], {"rep": core_peer})

    def w_second(j, c):
        y_forward(j, c).wait_recv()
        d_forward(j, c).start()

    def w_taps(j):
        rows_in = pl.ds(aligned(h_rows * (1 - ci)), h_rows)
        done(wfull.at[others[j], rows_in], cd_recv.at[j])
        block_taps(others[j])

    def core_copy(n, h):
        return remote(
            part.at[n, h, pl.ds(aligned(h_rows * (1 - ci)), h_rows)],
            core_in.at[n, h],
            send_sem.at[5],
            core_recv.at[n, h],
            {"rep": core_peer},
        )

    def x_copy(n, h):
        return remote(
            half.at[n, h, pl.ds(aligned(q_rows * (1 - xi)), q_rows)],
            x_in.at[n, h],
            send_sem.at[6],
            x_recv.at[n, h],
            {"rep": x_peer},
        )

    def z_copy(n, h):
        return remote(
            quarter.at[n, h],
            z_in.at[n, h],
            send_sem.at[7],
            z_recv.at[n, h],
            {"fsdp": partner},
        )

    def comb_copy(n, h):
        return remote(
            comb.at[n, h],
            z_in.at[3, h],
            send_sem.at[7],
            z_recv.at[3, h],
            {"fsdp": order[n]},
        )

    def weight_step(n, h):
        q, size = order[n], sizes[h]
        rhs = patches[pl.ds(aligned(q * block + h * lanes), size)]
        lhs = ctl[jnp.where(q == 0, 0, 1)]
        part[n, h, :, :size] = dot(lhs, rhs, ((1,), (1,))).astype(bf16)
        if h == 0 and n > 0:
            taken = 3 * chans - block

            @pl.when(q == 1)
            def _():
                rhs = patches[block : block + taken]
                part[n, h, :, :taken] = dot(ctl[0], rhs, ((1,), (1,))).astype(bf16)

        core_copy(n, h).start()

    def core_step(n, h):
        core_copy(n, h).wait_recv()
        mine_rows = part[n, h, pl.ds(aligned(h_rows * ci), h_rows)]
        half[n, h] = (mine_rows.astype(f32) + core_in[n, h].astype(f32)).astype(bf16)
        x_copy(n, h).start()

    def x_step(n, h):
        x_copy(n, h).wait_recv()
        mine_rows = half[n, h, pl.ds(aligned(q_rows * xi), q_rows)]
        quarter[n, h] = (mine_rows.astype(f32) + x_in[n, h].astype(f32)).astype(bf16)
        if n == 2:
            z_copy(n, h).start()
        elif n < 2:
            pl.when(outer)(lambda: z_copy(n, h).start())

    def comb_step(n, h):
        @pl.when(inner)
        def _():
            z_copy(n, h).wait_recv()
            value = quarter[n, h].astype(f32) + z_in[n, h].astype(f32)
            comb[n, h] = value.astype(bf16)
            comb_copy(n, h).start()

    def rep_copy(m, h):
        slot = (0, 2, 1)[m]
        src = final.at[h] if m < 2 else rep_in.at[h, 2]
        to = core_peer if m == 2 else reps[m]
        recv = rep_recv.at[1 if m == 1 else 0, h]
        return remote(src, rep_in.at[h, slot], send_sem.at[8], recv, {"rep": to})

    def place(ref, k, h):
        rows_k = pl.ds(aligned(q_rows * k), q_rows)
        wg_ref[rows_k, h * lanes : h * lanes + sizes[h]] = ref[:, : sizes[h]].astype(f32)

    def final_step(h):
        z_copy(2, h).wait_recv()
        comb_copy(1, h).wait_recv()
        value = quarter[3, h].astype(f32) + z_in[2, h].astype(f32) + z_in[3, h].astype(f32)
        final[h] = (value * scale).astype(bf16)
        rep_copy(1, h).start()
        rep_copy(0, h).start()

    owners = [2 * (1 - ci) + xi, 2 * (1 - ci) + 1 - xi, 2 * ci + 1 - xi]
    def relay_step(h):
        rep_copy(1, h).wait_recv()
        rep_copy(2, h).start()

    def first_places(h):
        place(final.at[h], mine, h)
        place(rep_in.at[h, 2], owners[2], h)

    def last_places(h):
        done(rep_in.at[h, pl.ds(0, 2)], rep_recv.at[0, h])
        for m in range(2):
            place(rep_in.at[h, m], owners[m], h)

    def gain_sums():
        done(uv_far, uv_recv.at[1])
        total = uv[...]
        for d in range(nz - 1):
            total = total + uv_in[d]
        for d in range(3 * nz):
            total = total + uv_far[d]
        gg_ref[...] = total * scale


    def prepare():
        for r in range(rows):
            for odd in range(2):
                here = pl.ds(odd * cols, cols)
                normed = (norm[r + 1, :, here] - mean) * rstd
                z_val = gain * normed + shift
                sig = dsilu[r, :, here]
                norm[r + 1, :, here] = normed
                dsilu[r, :, here] = sig * (1.0 + z_val * (1.0 - sig))

    w_lane = lax.broadcasted_iota(jnp.int32, (outs_ch, block), 1)
    top = 3 * chans - block
    upto, since = -(-top // 128) * 128, top // 128 * 128

    def top_maps():
        first = jnp.where(w_lane[:, :upto] < top, wfull[1, :, :upto].astype(f32), 0.0).astype(bf16)
        value = dot(wfull[0], patches[:block]) + dot(first, patches[block : block + upto])
        p_out[...] = value[:, :cols].astype(bf16)
        when_up(lambda: p_copy.start())
        return value[:, cols:]

    def low_maps(above):
        rest = wfull[1, :, since:].astype(f32)
        rest = jnp.where(w_lane[:, since:] < top, 0.0, rest).astype(bf16)
        value = dot(rest, patches[block + since : 2 * block])
        for q in range(2, nz):
            value = value + dot(wfull[q], patches[q * block : (q + 1) * block])
        out_ref[0, 1] = (value[:, cols:] + above).astype(bf16)
        return value[:, :cols]

    def join_maps(value):
        @pl.when(z == 0)
        def _():
            p_in[...] = jnp.zeros(p_in.shape, bf16)

        when_down(lambda: p_copy.wait_recv())
        out_ref[0, 0] = (value + p_in[...].astype(f32)).astype(bf16)

    def edge_taps():
        @pl.when(z < nz - 1)
        def _():
            below = ctl[0, :, :cols]
            edge[:block] = dot(wfull[0], below, ((0,), (0,)))
            edge[block:] = dot(wfull[1, :, :top], below, ((0,), (0,)))

        @pl.when(z == nz - 1)
        def _():
            edge[...] = jnp.zeros(edge.shape, f32)

    def tap_at(row_tap, col_tap, i):
        tap = 3 * row_tap + col_tap
        here = slice(tap * chans, (tap + 1) * chans)
        if i == 2:
            return edge[here]
        return taps[here, i * cols : (i + 1) * cols]

    uv_cp = [
        remote(uv, uv_in.at[d], send_sem.at[9], uv_recv.at[0], {"fsdp": peers_z[d]})
        for d in range(nz - 1)
    ]

    far_cp = [
        remote(
            uv,
            uv_far.at[3 * d + m],
            send_sem.at[10],
            uv_recv.at[1],
            {"fsdp": lax.rem(z + d, nz), "rep": reps[m]},
        )
        for d in (2, 1, 3, 0)
        for m in range(3)
    ]

    def channel_sums():
        u_sum = jnp.zeros((chans, cols), f32)
        v_sum = jnp.zeros((chans, cols), f32)
        for r in range(rows):
            pairs = [(t, i) for i in range(3) for t in range(3) if 2 * i + t == r + 1]
            for odd in range(2):
                here = pl.ds(odd * cols, cols)
                grad = sum(tap_at(t, 1 + odd, i) for t, i in pairs)
                if odd == 1:
                    left = sum(tap_at(t, 0, i) for t, i in pairs)
                    moved = pltpu.roll(left, cols - 1, axis=1)
                    grad = grad + jnp.where(lane == cols - 1, 0.0, moved)
                value = grad * dsilu[r, :, here]
                zgrad[r, :, here] = value
                u_sum = u_sum + value * norm[r + 1, :, here]
                v_sum = v_sum + value
        put_sums(uv, row_sums(u_sum, v_sum))
        for d in (1, 0, 2):
            uv_cp[d].start()
        for cp in far_cp:
            cp.start()

    def input_grads():
        done(uv_in, uv_recv.at[0])
        total = uv[...]
        for d in range(nz - 1):
            total = total + uv_in[d]
        su_val, sv_val = group_sums(gv[0:1] * total)
        su_val, sv_val = su_val / count, sv_val / count
        merge = jnp.where(
            jnp.where(big_i < cols, 2 * big_i, 2 * (big_i - cols) + 1) == big_j, 1.0, 0.0
        ).astype(bf16)
        def grad_row(r):
            for odd in range(2):
                here = pl.ds(odd * cols, cols)
                value = rstd * (gain * zgrad[r, :, here] - sv_val - norm[r + 1, :, here] * su_val)
                patches[r * chans : (r + 1) * chans, here] = value.astype(bf16)
            dx_ref[0, r] = dot(patches[r * chans : (r + 1) * chans], merge).astype(bf16)

        grad_row(0)
        grad_row(1)
        relay_step(2)
        first_places(2)
        grad_row(2)
        grad_row(3)

    def halo_wait():
        pl.when(z < nz - 2)(lambda: halo_c.wait_recv())

    def drain():
        own = wfull.at[0, pl.ds(0, q_rows)]
        three = wfull.at[0, pl.ds(0, 3 * q_rows)]

        done(stat_in, send_sem.at[11])
        when_down(lambda: halo_c.wait_send())
        pl.when(outer)(lambda: done(wfull.at[0, pl.ds(0, 2 * q_rows)], send_sem.at[0]))

        @pl.when(inner)
        def _():
            done(three, send_sem.at[0])
            done(own, send_sem.at[1])

        for k in (2, 3, 4):
            done(three, send_sem.at[k])
        done(half, send_sem.at[5])
        done(quarter, send_sem.at[6])
        done(comb, send_sem.at[7])

    weight_step(0, 0)
    weight_step(0, 1)
    weight_step(0, 2)
    activate(1, [(1, 0)])
    activate(3, [(1, 1)])
    weight_step(1, 0)
    core_step(0, 0)
    weight_step(1, 1)
    core_step(0, 1)
    weight_step(1, 2)
    core_step(0, 2)
    core_step(1, 0)
    w_arrive(0, 0)
    core_step(1, 1)
    w_arrive(0, 1, inner)
    core_step(1, 2)
    halo_wait()
    weight_step(2, 0)
    weight_step(2, 1)
    weight_step(2, 2)
    weight_step(3, 0)
    weight_step(3, 1)
    x_step(0, 0)
    weight_step(3, 2)
    w_arrive(0, 1, outer)
    w_arrive(1, 0)
    x_step(0, 1)
    prepare()
    core_step(2, 0)
    core_step(2, 1)
    core_step(2, 2)
    x_step(0, 2)
    w_arrive(1, 1)
    w_second(0, 0)
    x_step(1, 0)
    core_step(3, 0)
    w_second(0, 1)
    core_step(3, 1)
    core_step(3, 2)
    w_arrive(2, 0)
    x_step(1, 1)
    w_arrive(2, 1)
    comb_step(0, 0)
    x_step(1, 2)
    comb_step(0, 1)
    w_second(1, 0)
    comb_step(0, 2)
    w_second(1, 1)
    x_step(2, 0)
    w_taps(0)
    comb_step(1, 0)
    x_step(2, 1)
    comb_step(1, 1)
    w_second(2, 0)
    w_taps(1)
    x_step(2, 2)
    w_second(2, 1)
    comb_step(1, 2)
    edge_taps()
    x_step(3, 0)
    x_step(3, 1)
    w_taps(2)
    final_step(0)
    x_step(3, 2)
    channel_sums()
    final_step(1)
    final_step(2)
    above = top_maps()
    low = low_maps(above)
    drain()
    relay_step(0)
    relay_step(1)
    first_places(0)
    first_places(1)
    input_grads()
    join_maps(low)

    last_places(0)
    last_places(1)
    last_places(2)
    gain_sums()

    when_up(lambda: p_copy.wait_send())
    done(uv_in, send_sem.at[9])
    done(uv_far, send_sem.at[10])
    done(rep_in, send_sem.at[8])


def write_out(*refs):
    n = len(refs) // 2
    sems = refs[-1]
    copies = [pltpu.make_async_copy(refs[i], refs[n + i], sems.at[i]) for i in range(n)]
    for cp in copies:
        cp.start()
    for cp in copies:
        cp.wait()


def in_hbm(value):
    return pltpu.with_memory_space_constraint(value, pltpu.HBM)


def fused_shards(images, gains, conv_weight, cotangent):
    batch, rows, width, chans = images.shape
    block, outs_ch = conv_weight.shape
    nz = lax.axis_size("fsdp")
    fits = (batch, rows, cotangent.shape[1]) == (1, 4, 2) and chans % 64 == 0 and width == 256
    if not fits or block % 16 or outs_ch % 64 or nz * block != 9 * chans:
        return shards(images, gains, conv_weight, cotangent)
    if not block < 3 * chans < 2 * block or 3 * chans - block > 256:
        return shards(images, gains, conv_weight, cotangent)
    cols = width // 2
    q_rows = outs_ch // 4
    lanes = 256
    pieces = -(-block // lanes)
    wide = -(-chans // 128) * 128
    f32, bf16 = jnp.float32, jnp.bfloat16
    vmem = pltpu.VMEM
    dma = pltpu.SemaphoreType.DMA
    shapes = (
        jax.ShapeDtypeStruct((batch, rows // 2, outs_ch, cols), bf16),
        jax.ShapeDtypeStruct((batch, rows, chans, width), bf16),
        jax.ShapeDtypeStruct((outs_ch, block), f32),
        jax.ShapeDtypeStruct(gains.shape, f32),
    )
    results = pl.pallas_call(
        functools.partial(fused, nz),
        out_shape=tuple(vmem(shape.shape, shape.dtype) for shape in shapes),
        in_specs=[pl.BlockSpec(memory_space=pltpu.HBM)] * 4,
        out_specs=[pl.BlockSpec(memory_space=vmem)] * 4,
        scratch_shapes=[
            vmem((rows, chans, width), bf16),
            vmem(gains.shape, f32),
            vmem((2, outs_ch, width), bf16),
            vmem((width, width), bf16),
            vmem((chans, 3 * wide), bf16),
            vmem((outs_ch, cols), bf16),
            vmem((outs_ch, cols), bf16),
            vmem((rows + 1, chans, width), f32),
            vmem((rows, chans, width), f32),
            vmem((rows, chans, width), f32),
            vmem((nz * block, width), bf16),
            vmem((nz * block, width), f32),
            vmem((3 * chans, cols), f32),
            vmem((nz, outs_ch, block), bf16),
            vmem(gains.shape, f32),
            vmem((nz - 1,) + gains.shape, f32),
            vmem((nz, pieces, outs_ch, lanes), bf16),
            vmem((nz, pieces, 2 * q_rows, lanes), bf16),
            vmem((nz, pieces, 2 * q_rows, lanes), bf16),
            vmem((nz, pieces, q_rows, lanes), bf16),
            vmem((nz, pieces, q_rows, lanes), bf16),
            vmem((4, pieces, q_rows, lanes), bf16),
            vmem((3, pieces, q_rows, lanes), bf16),
            vmem((pieces, q_rows, lanes), bf16),
            vmem((pieces, 3, q_rows, lanes), bf16),
            vmem(gains.shape, f32),
            vmem((nz - 1,) + gains.shape, f32),
            vmem((3 * nz,) + gains.shape, f32),
            dma((rows + 4,)),
            dma((2, 2)),
            dma((12,)),
            dma((nz, 2)),
            dma((3, 2)),
            dma((3,)),
            dma((nz, pieces)),
            dma((nz, pieces)),
            dma((4, pieces)),
            dma((2, pieces)),
            dma((3,)),
        ],
        compiler_params=pltpu.CompilerParams(
            collective_id=0, has_side_effects=True, vmem_limit_bytes=48 * 1024 * 1024
        ),
    )(
        in_hbm(jnp.swapaxes(images, 2, 3)),
        in_hbm(gains),
        in_hbm(conv_weight.T),
        in_hbm(jnp.swapaxes(cotangent, 2, 3)),
    )
    output_maps, input_grad, weight_grad, gain_grad = pl.pallas_call(
        write_out,
        out_shape=shapes,
        in_specs=[pl.BlockSpec(memory_space=vmem)] * 4,
        out_specs=[pl.BlockSpec(memory_space=pltpu.HBM)] * 4,
        scratch_shapes=[dma((4,))],
        compiler_params=pltpu.CompilerParams(vmem_limit_bytes=1024 * 1024),
    )(*(pltpu.with_memory_space_constraint(value, vmem) for value in results))
    return (
        jnp.swapaxes(output_maps, 2, 3),
        jnp.swapaxes(input_grad, 2, 3),
        weight_grad.T,
        gain_grad,
    )


def solution(mesh):
    in_specs = (
        P(("groups", "rep"), "fsdp", None, None),
        P(),
        P("fsdp", None),
        P(("groups", "rep"), "fsdp", None, None),
    )
    out_specs = (
        P(("groups", "rep"), "fsdp", None, None),
        P(("groups", "rep"), "fsdp", None, None),
        P(("groups", "fsdp"), None),
        P("groups", None),
    )
    small = mesh.shape["groups"] == 2 and mesh.shape["rep"] == 4 and mesh.shape["fsdp"] == 4
    body = fused_shards if small else shards
    return jax.shard_map(body, mesh=mesh, in_specs=in_specs, out_specs=out_specs, check_vma=False)
```

```python
import functools

import jax
import jax.numpy as jnp
from jax import lax
from jax.experimental import pallas as pl
from jax.experimental.pallas import tpu as pltpu
from jax.sharding import PartitionSpec as P

GROUPS = 32
MESH = pl.DeviceIdType.MESH


def passed_along(shard, axis, by):
    size = lax.axis_size(axis)
    pairs = [(i, i + by) for i in range(size) if 0 <= i + by < size]
    return lax.ppermute(shard, axis, pairs)


def spread_taps(first, middle, last, axis):
    length = first.shape[axis]
    widths_end = [(0, 0)] * first.ndim
    widths_end[axis] = (0, 1)
    widths_start = [(0, 0)] * first.ndim
    widths_start[axis] = (1, 0)
    even = jnp.pad(first, widths_end) + jnp.pad(last, widths_start)
    odd = jnp.pad(middle, widths_end)
    merged = jnp.stack([even, odd], axis=axis + 1)
    shape = list(even.shape)
    shape[axis] = 2 * (length + 1)
    merged = merged.reshape(shape)
    return lax.slice_in_dim(merged, 0, 2 * length + 1, axis=axis)


def shards(images, gains, conv_weight, cotangent):
    batch, rows, width, chans = images.shape
    outs_ch = conv_weight.shape[1]
    n_fsdp = lax.axis_size("fsdp")
    per_group = chans // GROUPS
    x_val = images.astype(jnp.float32)
    grouped = x_val.reshape(batch, rows, width, GROUPS, per_group)
    part_one = jnp.sum(grouped, axis=(1, 2, 4))
    part_two = jnp.sum(grouped * grouped, axis=(1, 2, 4))
    full_weight = lax.all_gather(conv_weight, "fsdp", axis=0, tiled=True)
    sum_one, sum_two = lax.psum((part_one, part_two), "fsdp")
    count = rows * n_fsdp * width * per_group
    mean = sum_one / count
    rstd = 1.0 / jnp.sqrt(sum_two / count - mean * mean + 1e-05)
    normed_g = (grouped - mean[:, None, None, :, None]) * rstd[:, None, None, :, None]
    normed = normed_g.reshape(x_val.shape)
    z_val = gains[0] * normed + gains[1]
    act = (z_val * jax.nn.sigmoid(z_val)).astype(jnp.bfloat16)
    above = passed_along(act[:, rows - 1 : rows], "fsdp", 1)
    padded = jnp.concatenate([above, act], axis=1)
    kernel = full_weight.reshape(3, 3, chans, outs_ch)
    result = lax.conv_general_dilated(
        padded,
        kernel,
        (2, 2),
        ((0, 0), (1, 0)),
        dimension_numbers=("NHWC", "HWIO", "NHWC"),
        preferred_element_type=jnp.float32,
    )
    output_maps = result.astype(jnp.bfloat16)
    patch_grad = jnp.einsum(
        "bijo,ko->bijk", cotangent, full_weight, preferred_element_type=jnp.float32
    )
    half_rows, half_cols = (cotangent.shape[1], cotangent.shape[2])
    taps = patch_grad.reshape(batch, half_rows, half_cols, 3, 3, chans)
    by_row = [
        spread_taps(
            taps[:, :, :, row_tap, 0], taps[:, :, :, row_tap, 1], taps[:, :, :, row_tap, 2], 2
        )
        for row_tap in range(3)
    ]
    grid = spread_taps(by_row[0], by_row[1], by_row[2], 1)[:, :, 1:]
    from_below = passed_along(grid[:, 0:1].astype(jnp.bfloat16), "fsdp", -1).astype(jnp.float32)
    filler = jnp.zeros((batch, rows - 1, width, chans), jnp.float32)
    act_grad = grid[:, 1:] + jnp.concatenate([filler, from_below], axis=1)
    padded_cols = jnp.pad(padded, ((0, 0), (0, 0), (1, 0), (0, 0)))
    blocks = []
    for row_tap in range(3):
        for col_tap in range(3):
            window = padded_cols[:, row_tap : row_tap + rows : 2, col_tap : col_tap + width : 2]
            blocks.append(
                jnp.einsum("bijc,bijo->co", window, cotangent, preferred_element_type=jnp.float32)
            )
    total_pixels = batch * lax.axis_size("rep") * half_rows * n_fsdp * half_cols
    scale = 1.0 / jnp.sqrt(jnp.float32(total_pixels))
    weight_term = jnp.concatenate(blocks, axis=0) * scale
    sig = jax.nn.sigmoid(z_val)
    z_grad = act_grad * sig * (1.0 + z_val * (1.0 - sig))
    u_part = jnp.sum(z_grad * normed, axis=(1, 2))
    v_part = jnp.sum(z_grad, axis=(1, 2))
    u_sum, v_sum = lax.psum((u_part, v_part), "fsdp")
    gain_term = jnp.stack([jnp.sum(u_sum, axis=0), jnp.sum(v_sum, axis=0)]) * scale
    su_val = jnp.sum((gains[0] * u_sum).reshape(batch, GROUPS, per_group), axis=-1)
    sv_val = jnp.sum((gains[0] * v_sum).reshape(batch, GROUPS, per_group), axis=-1)
    scaled = (gains[0] * z_grad).reshape(grouped.shape)
    dx_val = rstd[:, None, None, :, None] * (
        scaled
        - sv_val[:, None, None, :, None] / count
        - normed_g * su_val[:, None, None, :, None] / count
    )
    input_grad = dx_val.reshape(x_val.shape).astype(jnp.bfloat16)
    owned = lax.psum_scatter(weight_term, "fsdp", scatter_dimension=0, tiled=True)
    weight_grad, gain_grad = (
        lax.psum(owned.astype(jnp.bfloat16), "rep").astype(jnp.float32),
        lax.psum(gain_term.astype(jnp.bfloat16), "rep").astype(jnp.float32),
    )
    return (output_maps, input_grad, weight_grad, gain_grad)


HIGHEST = lax.Precision.HIGHEST


def dot(lhs, rhs, contract=((1,), (0,)), precision=None):
    return lax.dot_general(
        lhs, rhs, (contract, ((), ())), precision=precision, preferred_element_type=jnp.float32
    )


def fused(
    nz,
    x_hbm,
    g_hbm,
    w_hbm,
    ct_hbm,
    out_ref,
    dx_ref,
    wg_ref,
    gg_ref,
    xv,
    gv,
    ctl,
    split,
    same,
    p_out,
    p_in,
    norm,
    dsilu,
    zgrad,
    patches,
    taps,
    edge,
    wfull,
    stat,
    stat_in,
    part,
    core_in,
    half,
    x_in,
    quarter,
    z_in,
    comb,
    final,
    rep_in,
    uv,
    uv_in,
    uv_far,
    loc_sem,
    halo_sem,
    send_sem,
    w_recv,
    y_recv,
    cd_recv,
    core_recv,
    x_recv,
    z_recv,
    rep_recv,
    uv_recv,
):
    f32, bf16 = jnp.float32, jnp.bfloat16
    rows, chans, width = x_hbm.shape[1:]
    cols = width // 2
    outs_ch, block = w_hbm.shape
    q_rows = outs_ch // 4
    h_rows = outs_ch // 2
    lanes = part.shape[3]
    pieces = part.shape[1]
    sizes = [min(lanes, block - h * lanes) for h in range(pieces)]
    w_cut = [(0, -(-q_rows // 32) * 16)]
    w_cut.append((w_cut[0][1], q_rows - w_cut[0][1]))
    count = rows * nz * width * (chans // GROUPS)
    scale = 1.0 / jnp.sqrt(f32(4 * nz * ct_hbm.shape[1] * cols))
    z = lax.axis_index("fsdp")
    rep = lax.axis_index("rep")
    yi = lax.axis_index("groups")
    xi, ci = rep // 2, rep % 2
    mine = 2 * ci + xi
    peers_z = [lax.rem(z + d, nz) for d in range(1, nz)]
    reps = [(2 * xi + 1 - ci), (2 * (1 - xi) + ci), (2 * (1 - xi) + 1 - ci)]
    core_peer, x_peer = reps[0], reps[1]
    pair = z // 2
    partner = z + 1 - 2 * (z % 2)
    inner = jnp.logical_or(z == 1, z == 2)
    outer = jnp.logical_or(z == 0, z == 3)
    order = [3 * (1 - pair), 2 - pair, partner, z]
    near_far = [partner, 2 - pair, 3 * (1 - pair)]
    one_order = [near_far[2], near_far[0], near_far[1]]
    two_order = [near_far[2], near_far[1], near_far[0]]
    others = [
        jnp.where(z == 1, one_order[k], jnp.where(z == 2, two_order[k], near_far[k]))
        for k in range(3)
    ]

    def aligned(value):
        return pl.multiple_of(value, 16)

    def remote(src, dst, send, recv, device):
        return pltpu.make_async_remote_copy(
            src_ref=src,
            dst_ref=dst,
            send_sem=send,
            recv_sem=recv,
            device_id=device,
            device_id_type=MESH,
        )

    def done(ref, sem):
        pltpu.make_async_copy(ref, ref, sem).wait()

    barrier = pltpu.get_barrier_semaphore()
    for peer in peers_z:
        pl.semaphore_signal(barrier, inc=1, device_id={"fsdp": peer}, device_id_type=MESH)
    for peer in reps:
        pl.semaphore_signal(barrier, inc=1, device_id={"rep": peer}, device_id_type=MESH)
    pl.semaphore_signal(barrier, inc=1, device_id={"groups": 1 - yi}, device_id_type=MESH)

    x_local = [pltpu.make_async_copy(x_hbm.at[0, r], xv.at[r], loc_sem.at[r]) for r in range(rows)]
    g_local = pltpu.make_async_copy(g_hbm, gv, loc_sem.at[rows])
    w_local = pltpu.make_async_copy(w_hbm, wfull.at[z], loc_sem.at[rows + 1])
    c_local = [
        pltpu.make_async_copy(
            ct_hbm.at[0, i], ctl.at[k, :, pl.ds(i * cols, cols)], loc_sem.at[rows + 2 + n]
        )
        for n, k, i in ((0, 1, 0), (0, 1, 1), (1, 0, 1))
    ]
    for cp in x_local + c_local + [w_local, g_local]:
        cp.start()

    big_i = lax.broadcasted_iota(jnp.int32, (width, width), 0)
    big_j = lax.broadcasted_iota(jnp.int32, (width, width), 1)
    inv = 1.0 / (chans // GROUPS)
    lane = lax.broadcasted_iota(jnp.int32, (chans, cols), 1)
    wide = same.shape[1] // 3
    ch_i = lax.broadcasted_iota(jnp.int32, (chans, wide), 0)
    ch_j = lax.broadcasted_iota(jnp.int32, (chans, wide), 1)
    grp_i = jnp.floor((ch_i.astype(f32) + 0.5) * inv)
    grp_j = jnp.floor((ch_j.astype(f32) + 0.5) * inv)
    same_one = jnp.where(jnp.where(ch_j < chans, grp_j, -1.0) == grp_i, 1.0, 0.0).astype(bf16)
    sums_i = lax.broadcasted_iota(jnp.int32, (8, width), 0)
    sums_j = lax.broadcasted_iota(jnp.int32, (8, width), 1)
    halves = jnp.where(jnp.where(sums_j < cols, 0, 4) == sums_i - lax.rem(sums_i, 4), 1.0, 0.0)
    halves = halves.astype(bf16)

    def three_terms(value):
        high = value.astype(bf16)
        rest = value - high.astype(f32)
        middle = rest.astype(bf16)
        low = (rest - middle.astype(f32)).astype(bf16)
        return high, middle, low

    def row_sums(first, second):
        both = jnp.concatenate([first, second], axis=1)
        terms = [dot(halves, term, ((1,), (1,))) for term in three_terms(both)]
        return terms[0] + (terms[1] + terms[2])

    def put_sums(ref, sums):
        ref[0:1] = sums[0:1]
        ref[1:2] = sums[4:5]

    def group_sums(total):
        pad = jnp.zeros((2, wide - chans), f32)
        terms = three_terms(jnp.concatenate([total, pad], axis=1))
        sums = dot(same[...], jnp.concatenate(terms, axis=1), ((1,), (1,)))
        first = jnp.broadcast_to(sums[:, 0:1], (chans, cols))
        second = jnp.broadcast_to(sums[:, 1:2], (chans, cols))
        return first, second

    @pl.when(z == nz - 1)
    def _():
        ctl[0, :, :cols] = jnp.zeros((chans, cols), bf16)

    halo_c = remote(
        ctl.at[1, :, pl.ds(0, cols)],
        ctl.at[0, :, pl.ds(0, cols)],
        halo_sem.at[0, 0],
        halo_sem.at[0, 1],
        {"fsdp": lax.rem(z + nz - 1, nz)},
    )
    p_copy = remote(
        p_out, p_in, halo_sem.at[1, 0], halo_sem.at[1, 1], {"fsdp": lax.rem(z + 1, nz)}
    )

    def w_spot(q, y_from, c):
        start, size = w_cut[c]
        return wfull.at[q, pl.ds(aligned(q_rows * (2 * ci + y_from) + start), size)]

    def own_w(to, c):
        spot = w_spot(z, yi, c)
        return remote(spot, spot, send_sem.at[0], w_recv.at[z, c], {"fsdp": to})

    def when_up(act):
        pl.when(z < nz - 1)(act)

    def when_down(act):
        pl.when(z > 0)(act)

    sum_one = jnp.zeros((chans, cols), f32)
    sum_two = jnp.zeros((chans, cols), f32)
    for r in range(rows):
        x_local[r].wait()
        even, odd = xv[r, :, :cols].astype(f32), xv[r, :, cols:].astype(f32)
        sum_one = sum_one + (even + odd)
        sum_two = sum_two + (even * even + odd * odd)
    put_sums(stat, row_sums(sum_one, sum_two))

    stat_cp = [
        remote(stat, stat_in.at[d], send_sem.at[11], uv_recv.at[2], {"fsdp": peers_z[d]})
        for d in range(nz - 1)
    ]
    pl.semaphore_wait(barrier, nz - 1 + 3 + 1)
    for d in (1, 0, 2):
        stat_cp[d].start()

    split[...] = jnp.where(
        jnp.where(big_j < cols, 2 * big_j, 2 * (big_j - cols) + 1) == big_i, 1.0, 0.0
    ).astype(bf16)
    for k in range(3):
        same[:, k * wide : (k + 1) * wide] = same_one
    done(ctl.at[1], loc_sem.at[rows + 2])
    c_local[2].wait()
    w_local.wait()

    @pl.when(z == nz - 1)
    def _():
        halo_c.start()
        for to in (1, 2):
            for c in range(2):
                own_w(to, c).start()

    for r in range(rows):
        norm[r + 1] = dot(xv[r], split[...])
    eye_i = lax.broadcasted_iota(jnp.int32, (chans, chans), 0)
    eye_j = lax.broadcasted_iota(jnp.int32, (chans, chans), 1)
    eye = jnp.where(eye_i == eye_j, 1.0, 0.0)
    g_local.wait()
    gains = dot(eye, gv[...], ((1,), (1,)), HIGHEST)
    gain = jnp.broadcast_to(gains[:, 0:1], (chans, cols))
    shift = jnp.broadcast_to(gains[:, 1:2], (chans, cols))

    def block_taps(q):
        here = pl.ds(aligned(q * block), block)
        taps[here] = dot(wfull[q], ctl[1], ((0,), (0,)))

    block_taps(z)
    done(stat_in, uv_recv.at[2])

    @pl.when(z == 0)
    def _():
        for to in (2, 1):
            for c in range(2):
                own_w(to, c).start()

    @pl.when(inner)
    def _():
        halo_c.start()
        for to in (3 * (1 - pair), partner, 3 - z):
            for c in range(2):
                own_w(to, c).start()

    total = stat[...]
    for d in range(nz - 1):
        total = total + stat_in[d]
    sum_one, sum_two = group_sums(total)
    mean = sum_one / count
    rstd = 1.0 / jnp.sqrt(sum_two / count - mean * mean + 1e-05)
    slope = gain * rstd

    def put(row_tap, col_tap, i, lo, value):
        start = (3 * row_tap + col_tap) * chans + lo
        patches[start : start + value.shape[0], i * cols : (i + 1) * cols] = value

    step = 64

    def activate(r, users):
        for lo in range(0, chans, step):
            part_of = slice(lo, lo + step)
            for odd in range(2):
                here = pl.ds(odd * cols, cols)
                x_val = norm[r, part_of, here]
                z_val = (x_val - mean[part_of]) * slope[part_of] + shift[part_of]
                sig = 0.5 * jnp.tanh(0.5 * z_val) + 0.5
                act = z_val * sig
                dsilu[r - 1, part_of, here] = sig
                rounded = act.astype(bf16)
                for t, i in users:
                    put(t, 1 + odd, i, lo, rounded)
                if odd == 1:
                    moved = pltpu.roll(act, 1, axis=1)
                    moved = jnp.where(lane[part_of] == 0, 0.0, moved).astype(bf16)
                    for t, i in users:
                        put(t, 0, i, lo, moved)

    activate(2, [(2, 0), (0, 1)])
    activate(4, [(2, 1), (0, 0)])

    pl.when(z == nz - 2)(lambda: halo_c.wait_recv())

    def relay_w(c):
        spot = w_spot(others[0], yi, c)
        return remote(spot, spot, send_sem.at[1], w_recv.at[others[0], c], {"fsdp": partner})

    def w_arrive(j, c, role=None):
        def take():
            q = others[j]
            spot = w_spot(q, yi, c)
            remote(spot, spot, send_sem.at[1], w_recv.at[q, c], {"fsdp": partner}).wait_recv()
            if j == 0 and role is not outer:
                pl.when(inner)(lambda: relay_w(c).start())
            y_forward(j, c).start()
            c_forward(j, c).start()

        if role is None:
            take()
        else:
            pl.when(role)(take)

    def y_forward(j, c):
        spot = w_spot(others[j], yi, c)
        return remote(spot, spot, send_sem.at[2], y_recv.at[j, c], {"groups": 1 - yi})

    def c_forward(j, c):
        spot = w_spot(others[j], yi, c)
        return remote(spot, spot, send_sem.at[3], cd_recv.at[j], {"rep": core_peer})

    def d_forward(j, c):
        spot = w_spot(others[j], 1 - yi, c)
        return remote(spot, spot, send_sem.at[4], cd_recv.at[j], {"rep": core_peer})

    def w_second(j, c):
        y_forward(j, c).wait_recv()
        d_forward(j, c).start()

    def w_taps(j):
        rows_in = pl.ds(aligned(h_rows * (1 - ci)), h_rows)
        done(wfull.at[others[j], rows_in], cd_recv.at[j])
        block_taps(others[j])

    def core_copy(n, h):
        return remote(
            part.at[n, h, pl.ds(aligned(h_rows * (1 - ci)), h_rows)],
            core_in.at[n, h],
            send_sem.at[5],
            core_recv.at[n, h],
            {"rep": core_peer},
        )

    def x_copy(n, h):
        return remote(
            half.at[n, h, pl.ds(aligned(q_rows * (1 - xi)), q_rows)],
            x_in.at[n, h],
            send_sem.at[6],
            x_recv.at[n, h],
            {"rep": x_peer},
        )

    def z_copy(n, h):
        return remote(
            quarter.at[n, h],
            z_in.at[n, h],
            send_sem.at[7],
            z_recv.at[n, h],
            {"fsdp": partner},
        )

    def comb_copy(n, h):
        return remote(
            comb.at[n, h],
            z_in.at[3, h],
            send_sem.at[7],
            z_recv.at[3, h],
            {"fsdp": order[n]},
        )

    def weight_step(n, h):
        q, size = order[n], sizes[h]
        rhs = patches[pl.ds(aligned(q * block + h * lanes), size)]
        lhs = ctl[jnp.where(q == 0, 0, 1)]
        part[n, h, :, :size] = dot(lhs, rhs, ((1,), (1,))).astype(bf16)
        if h == 0 and n > 0:
            taken = 3 * chans - block

            @pl.when(q == 1)
            def _():
                rhs = patches[block : block + taken]
                part[n, h, :, :taken] = dot(ctl[0], rhs, ((1,), (1,))).astype(bf16)

        core_copy(n, h).start()

    def core_step(n, h):
        core_copy(n, h).wait_recv()
        mine_rows = part[n, h, pl.ds(aligned(h_rows * ci), h_rows)]
        half[n, h] = (mine_rows.astype(f32) + core_in[n, h].astype(f32)).astype(bf16)
        x_copy(n, h).start()

    def x_step(n, h):
        x_copy(n, h).wait_recv()
        mine_rows = half[n, h, pl.ds(aligned(q_rows * xi), q_rows)]
        quarter[n, h] = (mine_rows.astype(f32) + x_in[n, h].astype(f32)).astype(bf16)
        if n == 2:
            z_copy(n, h).start()
        elif n < 2:
            pl.when(outer)(lambda: z_copy(n, h).start())

    def comb_step(n, h):
        @pl.when(inner)
        def _():
            z_copy(n, h).wait_recv()
            value = quarter[n, h].astype(f32) + z_in[n, h].astype(f32)
            comb[n, h] = value.astype(bf16)
            comb_copy(n, h).start()

    def rep_copy(m, h):
        slot = (0, 2, 1)[m]
        src = final.at[h] if m < 2 else rep_in.at[h, 2]
        to = core_peer if m == 2 else reps[m]
        recv = rep_recv.at[1 if m == 1 else 0, h]
        return remote(src, rep_in.at[h, slot], send_sem.at[8], recv, {"rep": to})

    def place(ref, k, h):
        rows_k = pl.ds(aligned(q_rows * k), q_rows)
        wg_ref[rows_k, h * lanes : h * lanes + sizes[h]] = ref[:, : sizes[h]].astype(f32)

    def final_step(h):
        z_copy(2, h).wait_recv()
        comb_copy(1, h).wait_recv()
        value = quarter[3, h].astype(f32) + z_in[2, h].astype(f32) + z_in[3, h].astype(f32)
        final[h] = (value * scale).astype(bf16)
        rep_copy(1, h).start()
        rep_copy(0, h).start()

    owners = [2 * (1 - ci) + xi, 2 * (1 - ci) + 1 - xi, 2 * ci + 1 - xi]
    def relay_step(h):
        rep_copy(1, h).wait_recv()
        rep_copy(2, h).start()

    def first_places(h):
        place(final.at[h], mine, h)
        place(rep_in.at[h, 2], owners[2], h)

    def last_places(h):
        done(rep_in.at[h, pl.ds(0, 2)], rep_recv.at[0, h])
        for m in range(2):
            place(rep_in.at[h, m], owners[m], h)

    def gain_sums():
        done(uv_far, uv_recv.at[1])
        total = uv[...]
        for d in range(nz - 1):
            total = total + uv_in[d]
        for d in range(3 * nz):
            total = total + uv_far[d]
        gg_ref[...] = total * scale


    def prepare():
        for r in range(rows):
            for odd in range(2):
                here = pl.ds(odd * cols, cols)
                normed = (norm[r + 1, :, here] - mean) * rstd
                z_val = gain * normed + shift
                sig = dsilu[r, :, here]
                norm[r + 1, :, here] = normed
                dsilu[r, :, here] = sig * (1.0 + z_val * (1.0 - sig))

    w_lane = lax.broadcasted_iota(jnp.int32, (outs_ch, block), 1)
    top = 3 * chans - block
    upto, since = -(-top // 128) * 128, top // 128 * 128

    def top_maps():
        first = jnp.where(w_lane[:, :upto] < top, wfull[1, :, :upto].astype(f32), 0.0).astype(bf16)
        value = dot(wfull[0], patches[:block]) + dot(first, patches[block : block + upto])
        p_out[...] = value[:, :cols].astype(bf16)
        when_up(lambda: p_copy.start())
        return value[:, cols:]

    def low_maps(above):
        rest = wfull[1, :, since:].astype(f32)
        rest = jnp.where(w_lane[:, since:] < top, 0.0, rest).astype(bf16)
        value = dot(rest, patches[block + since : 2 * block])
        for q in range(2, nz):
            value = value + dot(wfull[q], patches[q * block : (q + 1) * block])
        out_ref[0, 1] = (value[:, cols:] + above).astype(bf16)
        return value[:, :cols]

    def join_maps(value):
        @pl.when(z == 0)
        def _():
            p_in[...] = jnp.zeros(p_in.shape, bf16)

        when_down(lambda: p_copy.wait_recv())
        out_ref[0, 0] = (value + p_in[...].astype(f32)).astype(bf16)

    def edge_taps():
        @pl.when(z < nz - 1)
        def _():
            below = ctl[0, :, :cols]
            edge[:block] = dot(wfull[0], below, ((0,), (0,)))
            edge[block:] = dot(wfull[1, :, :top], below, ((0,), (0,)))

        @pl.when(z == nz - 1)
        def _():
            edge[...] = jnp.zeros(edge.shape, f32)

    def tap_at(row_tap, col_tap, i):
        tap = 3 * row_tap + col_tap
        here = slice(tap * chans, (tap + 1) * chans)
        if i == 2:
            return edge[here]
        return taps[here, i * cols : (i + 1) * cols]

    uv_cp = [
        remote(uv, uv_in.at[d], send_sem.at[9], uv_recv.at[0], {"fsdp": peers_z[d]})
        for d in range(nz - 1)
    ]

    far_cp = [
        remote(
            uv,
            uv_far.at[3 * d + m],
            send_sem.at[10],
            uv_recv.at[1],
            {"fsdp": lax.rem(z + d, nz), "rep": reps[m]},
        )
        for d in (2, 1, 3, 0)
        for m in range(3)
    ]

    def channel_sums():
        u_sum = jnp.zeros((chans, cols), f32)
        v_sum = jnp.zeros((chans, cols), f32)
        for r in range(rows):
            pairs = [(t, i) for i in range(3) for t in range(3) if 2 * i + t == r + 1]
            for odd in range(2):
                here = pl.ds(odd * cols, cols)
                grad = sum(tap_at(t, 1 + odd, i) for t, i in pairs)
                if odd == 1:
                    left = sum(tap_at(t, 0, i) for t, i in pairs)
                    moved = pltpu.roll(left, cols - 1, axis=1)
                    grad = grad + jnp.where(lane == cols - 1, 0.0, moved)
                value = grad * dsilu[r, :, here]
                zgrad[r, :, here] = value
                u_sum = u_sum + value * norm[r + 1, :, here]
                v_sum = v_sum + value
        put_sums(uv, row_sums(u_sum, v_sum))
        for d in (1, 0, 2):
            uv_cp[d].start()

    def input_grads():
        done(uv_in, uv_recv.at[0])
        total = uv[...]
        for d in range(nz - 1):
            total = total + uv_in[d]
        su_val, sv_val = group_sums(gv[0:1] * total)
        su_val, sv_val = su_val / count, sv_val / count
        merge = jnp.where(
            jnp.where(big_i < cols, 2 * big_i, 2 * (big_i - cols) + 1) == big_j, 1.0, 0.0
        ).astype(bf16)
        def grad_row(r):
            for odd in range(2):
                here = pl.ds(odd * cols, cols)
                value = rstd * (gain * zgrad[r, :, here] - sv_val - norm[r + 1, :, here] * su_val)
                patches[r * chans : (r + 1) * chans, here] = value.astype(bf16)
            dx_ref[0, r] = dot(patches[r * chans : (r + 1) * chans], merge).astype(bf16)

        relay_step(2)
        first_places(2)
        grad_row(0)
        grad_row(1)
        grad_row(2)
        grad_row(3)

    def halo_wait():
        pl.when(z < nz - 2)(lambda: halo_c.wait_recv())

    def drain():
        own = wfull.at[0, pl.ds(0, q_rows)]
        three = wfull.at[0, pl.ds(0, 3 * q_rows)]

        done(stat_in, send_sem.at[11])
        when_down(lambda: halo_c.wait_send())
        pl.when(outer)(lambda: done(wfull.at[0, pl.ds(0, 2 * q_rows)], send_sem.at[0]))

        @pl.when(inner)
        def _():
            done(three, send_sem.at[0])
            done(own, send_sem.at[1])

        for k in (2, 3, 4):
            done(three, send_sem.at[k])
        done(half, send_sem.at[5])
        done(quarter, send_sem.at[6])
        done(comb, send_sem.at[7])

    weight_step(0, 0)
    weight_step(0, 1)
    weight_step(0, 2)
    activate(1, [(1, 0)])
    activate(3, [(1, 1)])
    weight_step(1, 0)
    core_step(0, 0)
    weight_step(1, 1)
    core_step(0, 1)
    weight_step(1, 2)
    core_step(0, 2)
    core_step(1, 0)
    w_arrive(0, 0)
    core_step(1, 1)
    w_arrive(0, 1, inner)
    halo_wait()
    weight_step(2, 0)
    core_step(1, 2)
    weight_step(2, 1)
    weight_step(2, 2)
    weight_step(3, 0)
    weight_step(3, 1)
    x_step(0, 0)
    weight_step(3, 2)
    w_arrive(0, 1, outer)
    w_arrive(1, 0)
    x_step(0, 1)
    prepare()
    core_step(2, 0)
    core_step(2, 1)
    core_step(2, 2)
    x_step(0, 2)
    w_arrive(1, 1)
    w_second(0, 0)
    x_step(1, 0)
    core_step(3, 0)
    w_second(0, 1)
    core_step(3, 1)
    core_step(3, 2)
    w_arrive(2, 0)
    x_step(1, 1)
    w_arrive(2, 1)
    comb_step(0, 0)
    x_step(1, 2)
    comb_step(0, 1)
    w_second(1, 0)
    comb_step(0, 2)
    w_second(1, 1)
    x_step(2, 0)
    w_taps(0)
    comb_step(1, 0)
    x_step(2, 1)
    w_second(2, 0)
    comb_step(1, 1)
    w_taps(1)
    w_second(2, 1)
    x_step(2, 2)
    edge_taps()
    x_step(3, 0)
    comb_step(1, 2)
    x_step(3, 1)
    w_taps(2)
    final_step(0)
    x_step(3, 2)
    channel_sums()
    final_step(1)
    final_step(2)
    for cp in far_cp:
        cp.start()
    above = top_maps()
    low = low_maps(above)
    drain()
    relay_step(0)
    relay_step(1)
    first_places(0)
    first_places(1)
    input_grads()
    join_maps(low)

    last_places(0)
    last_places(1)
    last_places(2)
    gain_sums()

    when_up(lambda: p_copy.wait_send())
    done(uv_in, send_sem.at[9])
    done(uv_far, send_sem.at[10])
    done(rep_in, send_sem.at[8])


def write_out(*refs):
    n = len(refs) // 2
    sems = refs[-1]
    copies = [pltpu.make_async_copy(refs[i], refs[n + i], sems.at[i]) for i in range(n)]
    for cp in copies:
        cp.start()
    for cp in copies:
        cp.wait()


def in_hbm(value):
    return pltpu.with_memory_space_constraint(value, pltpu.HBM)


def fused_shards(images, gains, conv_weight, cotangent):
    batch, rows, width, chans = images.shape
    block, outs_ch = conv_weight.shape
    nz = lax.axis_size("fsdp")
    fits = (batch, rows, cotangent.shape[1]) == (1, 4, 2) and chans % 64 == 0 and width == 256
    if not fits or block % 16 or outs_ch % 64 or nz * block != 9 * chans:
        return shards(images, gains, conv_weight, cotangent)
    if not block < 3 * chans < 2 * block or 3 * chans - block > 256:
        return shards(images, gains, conv_weight, cotangent)
    cols = width // 2
    q_rows = outs_ch // 4
    lanes = 256
    pieces = -(-block // lanes)
    wide = -(-chans // 128) * 128
    f32, bf16 = jnp.float32, jnp.bfloat16
    vmem = pltpu.VMEM
    dma = pltpu.SemaphoreType.DMA
    shapes = (
        jax.ShapeDtypeStruct((batch, rows // 2, outs_ch, cols), bf16),
        jax.ShapeDtypeStruct((batch, rows, chans, width), bf16),
        jax.ShapeDtypeStruct((outs_ch, block), f32),
        jax.ShapeDtypeStruct(gains.shape, f32),
    )
    results = pl.pallas_call(
        functools.partial(fused, nz),
        out_shape=tuple(vmem(shape.shape, shape.dtype) for shape in shapes),
        in_specs=[pl.BlockSpec(memory_space=pltpu.HBM)] * 4,
        out_specs=[pl.BlockSpec(memory_space=vmem)] * 4,
        scratch_shapes=[
            vmem((rows, chans, width), bf16),
            vmem(gains.shape, f32),
            vmem((2, outs_ch, width), bf16),
            vmem((width, width), bf16),
            vmem((chans, 3 * wide), bf16),
            vmem((outs_ch, cols), bf16),
            vmem((outs_ch, cols), bf16),
            vmem((rows + 1, chans, width), f32),
            vmem((rows, chans, width), f32),
            vmem((rows, chans, width), f32),
            vmem((nz * block, width), bf16),
            vmem((nz * block, width), f32),
            vmem((3 * chans, cols), f32),
            vmem((nz, outs_ch, block), bf16),
            vmem(gains.shape, f32),
            vmem((nz - 1,) + gains.shape, f32),
            vmem((nz, pieces, outs_ch, lanes), bf16),
            vmem((nz, pieces, 2 * q_rows, lanes), bf16),
            vmem((nz, pieces, 2 * q_rows, lanes), bf16),
            vmem((nz, pieces, q_rows, lanes), bf16),
            vmem((nz, pieces, q_rows, lanes), bf16),
            vmem((4, pieces, q_rows, lanes), bf16),
            vmem((3, pieces, q_rows, lanes), bf16),
            vmem((pieces, q_rows, lanes), bf16),
            vmem((pieces, 3, q_rows, lanes), bf16),
            vmem(gains.shape, f32),
            vmem((nz - 1,) + gains.shape, f32),
            vmem((3 * nz,) + gains.shape, f32),
            dma((rows + 4,)),
            dma((2, 2)),
            dma((12,)),
            dma((nz, 2)),
            dma((3, 2)),
            dma((3,)),
            dma((nz, pieces)),
            dma((nz, pieces)),
            dma((4, pieces)),
            dma((2, pieces)),
            dma((3,)),
        ],
        compiler_params=pltpu.CompilerParams(
            collective_id=0, has_side_effects=True, vmem_limit_bytes=48 * 1024 * 1024
        ),
    )(
        in_hbm(jnp.swapaxes(images, 2, 3)),
        in_hbm(gains),
        in_hbm(conv_weight.T),
        in_hbm(jnp.swapaxes(cotangent, 2, 3)),
    )
    output_maps, input_grad, weight_grad, gain_grad = pl.pallas_call(
        write_out,
        out_shape=shapes,
        in_specs=[pl.BlockSpec(memory_space=vmem)] * 4,
        out_specs=[pl.BlockSpec(memory_space=pltpu.HBM)] * 4,
        scratch_shapes=[dma((4,))],
        compiler_params=pltpu.CompilerParams(vmem_limit_bytes=1024 * 1024),
    )(*(pltpu.with_memory_space_constraint(value, vmem) for value in results))
    return (
        jnp.swapaxes(output_maps, 2, 3),
        jnp.swapaxes(input_grad, 2, 3),
        weight_grad.T,
        gain_grad,
    )


def solution(mesh):
    in_specs = (
        P(("groups", "rep"), "fsdp", None, None),
        P(),
        P("fsdp", None),
        P(("groups", "rep"), "fsdp", None, None),
    )
    out_specs = (
        P(("groups", "rep"), "fsdp", None, None),
        P(("groups", "rep"), "fsdp", None, None),
        P(("groups", "fsdp"), None),
        P("groups", None),
    )
    small = mesh.shape["groups"] == 2 and mesh.shape["rep"] == 4 and mesh.shape["fsdp"] == 4
    body = fused_shards if small else shards
    return jax.shard_map(body, mesh=mesh, in_specs=in_specs, out_specs=out_specs, check_vma=False)
```

```python
import functools

import jax
import jax.numpy as jnp
from jax import lax
from jax.experimental import pallas as pl
from jax.experimental.pallas import tpu as pltpu
from jax.sharding import PartitionSpec as P

GROUPS = 32
MESH = pl.DeviceIdType.MESH


def passed_along(shard, axis, by):
    size = lax.axis_size(axis)
    pairs = [(i, i + by) for i in range(size) if 0 <= i + by < size]
    return lax.ppermute(shard, axis, pairs)


def spread_taps(first, middle, last, axis):
    length = first.shape[axis]
    widths_end = [(0, 0)] * first.ndim
    widths_end[axis] = (0, 1)
    widths_start = [(0, 0)] * first.ndim
    widths_start[axis] = (1, 0)
    even = jnp.pad(first, widths_end) + jnp.pad(last, widths_start)
    odd = jnp.pad(middle, widths_end)
    merged = jnp.stack([even, odd], axis=axis + 1)
    shape = list(even.shape)
    shape[axis] = 2 * (length + 1)
    merged = merged.reshape(shape)
    return lax.slice_in_dim(merged, 0, 2 * length + 1, axis=axis)


def shards(images, gains, conv_weight, cotangent):
    batch, rows, width, chans = images.shape
    outs_ch = conv_weight.shape[1]
    n_fsdp = lax.axis_size("fsdp")
    per_group = chans // GROUPS
    x_val = images.astype(jnp.float32)
    grouped = x_val.reshape(batch, rows, width, GROUPS, per_group)
    part_one = jnp.sum(grouped, axis=(1, 2, 4))
    part_two = jnp.sum(grouped * grouped, axis=(1, 2, 4))
    full_weight = lax.all_gather(conv_weight, "fsdp", axis=0, tiled=True)
    sum_one, sum_two = lax.psum((part_one, part_two), "fsdp")
    count = rows * n_fsdp * width * per_group
    mean = sum_one / count
    rstd = 1.0 / jnp.sqrt(sum_two / count - mean * mean + 1e-05)
    normed_g = (grouped - mean[:, None, None, :, None]) * rstd[:, None, None, :, None]
    normed = normed_g.reshape(x_val.shape)
    z_val = gains[0] * normed + gains[1]
    act = (z_val * jax.nn.sigmoid(z_val)).astype(jnp.bfloat16)
    above = passed_along(act[:, rows - 1 : rows], "fsdp", 1)
    padded = jnp.concatenate([above, act], axis=1)
    kernel = full_weight.reshape(3, 3, chans, outs_ch)
    result = lax.conv_general_dilated(
        padded,
        kernel,
        (2, 2),
        ((0, 0), (1, 0)),
        dimension_numbers=("NHWC", "HWIO", "NHWC"),
        preferred_element_type=jnp.float32,
    )
    output_maps = result.astype(jnp.bfloat16)
    patch_grad = jnp.einsum(
        "bijo,ko->bijk", cotangent, full_weight, preferred_element_type=jnp.float32
    )
    half_rows, half_cols = (cotangent.shape[1], cotangent.shape[2])
    taps = patch_grad.reshape(batch, half_rows, half_cols, 3, 3, chans)
    by_row = [
        spread_taps(
            taps[:, :, :, row_tap, 0], taps[:, :, :, row_tap, 1], taps[:, :, :, row_tap, 2], 2
        )
        for row_tap in range(3)
    ]
    grid = spread_taps(by_row[0], by_row[1], by_row[2], 1)[:, :, 1:]
    from_below = passed_along(grid[:, 0:1].astype(jnp.bfloat16), "fsdp", -1).astype(jnp.float32)
    filler = jnp.zeros((batch, rows - 1, width, chans), jnp.float32)
    act_grad = grid[:, 1:] + jnp.concatenate([filler, from_below], axis=1)
    padded_cols = jnp.pad(padded, ((0, 0), (0, 0), (1, 0), (0, 0)))
    blocks = []
    for row_tap in range(3):
        for col_tap in range(3):
            window = padded_cols[:, row_tap : row_tap + rows : 2, col_tap : col_tap + width : 2]
            blocks.append(
                jnp.einsum("bijc,bijo->co", window, cotangent, preferred_element_type=jnp.float32)
            )
    total_pixels = batch * lax.axis_size("rep") * half_rows * n_fsdp * half_cols
    scale = 1.0 / jnp.sqrt(jnp.float32(total_pixels))
    weight_term = jnp.concatenate(blocks, axis=0) * scale
    sig = jax.nn.sigmoid(z_val)
    z_grad = act_grad * sig * (1.0 + z_val * (1.0 - sig))
    u_part = jnp.sum(z_grad * normed, axis=(1, 2))
    v_part = jnp.sum(z_grad, axis=(1, 2))
    u_sum, v_sum = lax.psum((u_part, v_part), "fsdp")
    gain_term = jnp.stack([jnp.sum(u_sum, axis=0), jnp.sum(v_sum, axis=0)]) * scale
    su_val = jnp.sum((gains[0] * u_sum).reshape(batch, GROUPS, per_group), axis=-1)
    sv_val = jnp.sum((gains[0] * v_sum).reshape(batch, GROUPS, per_group), axis=-1)
    scaled = (gains[0] * z_grad).reshape(grouped.shape)
    dx_val = rstd[:, None, None, :, None] * (
        scaled
        - sv_val[:, None, None, :, None] / count
        - normed_g * su_val[:, None, None, :, None] / count
    )
    input_grad = dx_val.reshape(x_val.shape).astype(jnp.bfloat16)
    owned = lax.psum_scatter(weight_term, "fsdp", scatter_dimension=0, tiled=True)
    weight_grad, gain_grad = (
        lax.psum(owned.astype(jnp.bfloat16), "rep").astype(jnp.float32),
        lax.psum(gain_term.astype(jnp.bfloat16), "rep").astype(jnp.float32),
    )
    return (output_maps, input_grad, weight_grad, gain_grad)


HIGHEST = lax.Precision.HIGHEST


def dot(lhs, rhs, contract=((1,), (0,)), precision=None):
    return lax.dot_general(
        lhs, rhs, (contract, ((), ())), precision=precision, preferred_element_type=jnp.float32
    )


def fused(
    nz,
    x_hbm,
    g_hbm,
    w_hbm,
    ct_hbm,
    out_ref,
    dx_ref,
    wg_ref,
    gg_ref,
    xv,
    gv,
    ctl,
    split,
    same,
    p_out,
    p_in,
    norm,
    dsilu,
    zgrad,
    patches,
    taps,
    edge,
    wfull,
    stat,
    stat_in,
    part,
    core_in,
    half,
    x_in,
    quarter,
    z_in,
    comb,
    final,
    rep_in,
    uv,
    uv_in,
    uv_far,
    loc_sem,
    halo_sem,
    send_sem,
    w_recv,
    y_recv,
    cd_recv,
    core_recv,
    x_recv,
    z_recv,
    rep_recv,
    uv_recv,
):
    f32, bf16 = jnp.float32, jnp.bfloat16
    rows, chans, width = x_hbm.shape[1:]
    cols = width // 2
    outs_ch, block = w_hbm.shape
    q_rows = outs_ch // 4
    h_rows = outs_ch // 2
    lanes = part.shape[3]
    pieces = part.shape[1]
    sizes = [min(lanes, block - h * lanes) for h in range(pieces)]
    w_cut = [(0, -(-q_rows // 32) * 16)]
    w_cut.append((w_cut[0][1], q_rows - w_cut[0][1]))
    count = rows * nz * width * (chans // GROUPS)
    scale = 1.0 / jnp.sqrt(f32(4 * nz * ct_hbm.shape[1] * cols))
    z = lax.axis_index("fsdp")
    rep = lax.axis_index("rep")
    yi = lax.axis_index("groups")
    xi, ci = rep // 2, rep % 2
    mine = 2 * ci + xi
    peers_z = [lax.rem(z + d, nz) for d in range(1, nz)]
    reps = [(2 * xi + 1 - ci), (2 * (1 - xi) + ci), (2 * (1 - xi) + 1 - ci)]
    core_peer, x_peer = reps[0], reps[1]
    pair = z // 2
    partner = z + 1 - 2 * (z % 2)
    inner = jnp.logical_or(z == 1, z == 2)
    outer = jnp.logical_or(z == 0, z == 3)
    order = [3 * (1 - pair), 2 - pair, partner, z]
    near_far = [partner, 2 - pair, 3 * (1 - pair)]
    one_order = [near_far[2], near_far[0], near_far[1]]
    two_order = [near_far[2], near_far[1], near_far[0]]
    others = [
        jnp.where(z == 1, one_order[k], jnp.where(z == 2, two_order[k], near_far[k]))
        for k in range(3)
    ]

    def aligned(value):
        return pl.multiple_of(value, 16)

    def remote(src, dst, send, recv, device):
        return pltpu.make_async_remote_copy(
            src_ref=src,
            dst_ref=dst,
            send_sem=send,
            recv_sem=recv,
            device_id=device,
            device_id_type=MESH,
        )

    def done(ref, sem):
        pltpu.make_async_copy(ref, ref, sem).wait()

    barrier = pltpu.get_barrier_semaphore()
    for peer in peers_z:
        pl.semaphore_signal(barrier, inc=1, device_id={"fsdp": peer}, device_id_type=MESH)
    for peer in reps:
        pl.semaphore_signal(barrier, inc=1, device_id={"rep": peer}, device_id_type=MESH)
    pl.semaphore_signal(barrier, inc=1, device_id={"groups": 1 - yi}, device_id_type=MESH)

    x_local = [pltpu.make_async_copy(x_hbm.at[0, r], xv.at[r], loc_sem.at[r]) for r in range(rows)]
    g_local = pltpu.make_async_copy(g_hbm, gv, loc_sem.at[rows])
    w_local = pltpu.make_async_copy(w_hbm, wfull.at[z], loc_sem.at[rows + 1])
    c_local = [
        pltpu.make_async_copy(
            ct_hbm.at[0, i], ctl.at[k, :, pl.ds(i * cols, cols)], loc_sem.at[rows + 2 + n]
        )
        for n, k, i in ((0, 1, 0), (0, 1, 1), (1, 0, 1))
    ]
    for cp in x_local + c_local + [w_local, g_local]:
        cp.start()

    big_i = lax.broadcasted_iota(jnp.int32, (width, width), 0)
    big_j = lax.broadcasted_iota(jnp.int32, (width, width), 1)
    inv = 1.0 / (chans // GROUPS)
    lane = lax.broadcasted_iota(jnp.int32, (chans, cols), 1)
    wide = same.shape[1] // 3
    ch_i = lax.broadcasted_iota(jnp.int32, (chans, wide), 0)
    ch_j = lax.broadcasted_iota(jnp.int32, (chans, wide), 1)
    grp_i = jnp.floor((ch_i.astype(f32) + 0.5) * inv)
    grp_j = jnp.floor((ch_j.astype(f32) + 0.5) * inv)
    same_one = jnp.where(jnp.where(ch_j < chans, grp_j, -1.0) == grp_i, 1.0, 0.0).astype(bf16)
    sums_i = lax.broadcasted_iota(jnp.int32, (8, width), 0)
    sums_j = lax.broadcasted_iota(jnp.int32, (8, width), 1)
    halves = jnp.where(jnp.where(sums_j < cols, 0, 4) == sums_i - lax.rem(sums_i, 4), 1.0, 0.0)
    halves = halves.astype(bf16)

    def three_terms(value):
        high = value.astype(bf16)
        rest = value - high.astype(f32)
        middle = rest.astype(bf16)
        low = (rest - middle.astype(f32)).astype(bf16)
        return high, middle, low

    def row_sums(first, second):
        both = jnp.concatenate([first, second], axis=1)
        terms = [dot(halves, term, ((1,), (1,))) for term in three_terms(both)]
        return terms[0] + (terms[1] + terms[2])

    def put_sums(ref, sums):
        ref[0:1] = sums[0:1]
        ref[1:2] = sums[4:5]

    def group_sums(total):
        pad = jnp.zeros((2, wide - chans), f32)
        terms = three_terms(jnp.concatenate([total, pad], axis=1))
        sums = dot(same[...], jnp.concatenate(terms, axis=1), ((1,), (1,)))
        first = jnp.broadcast_to(sums[:, 0:1], (chans, cols))
        second = jnp.broadcast_to(sums[:, 1:2], (chans, cols))
        return first, second

    @pl.when(z == nz - 1)
    def _():
        ctl[0, :, :cols] = jnp.zeros((chans, cols), bf16)

    halo_c = remote(
        ctl.at[1, :, pl.ds(0, cols)],
        ctl.at[0, :, pl.ds(0, cols)],
        halo_sem.at[0, 0],
        halo_sem.at[0, 1],
        {"fsdp": lax.rem(z + nz - 1, nz)},
    )
    p_copy = remote(
        p_out, p_in, halo_sem.at[1, 0], halo_sem.at[1, 1], {"fsdp": lax.rem(z + 1, nz)}
    )

    def w_spot(q, y_from, c):
        start, size = w_cut[c]
        return wfull.at[q, pl.ds(aligned(q_rows * (2 * ci + y_from) + start), size)]

    def own_w(to, c):
        spot = w_spot(z, yi, c)
        return remote(spot, spot, send_sem.at[0], w_recv.at[z, c], {"fsdp": to})

    def when_up(act):
        pl.when(z < nz - 1)(act)

    def when_down(act):
        pl.when(z > 0)(act)

    sum_one = jnp.zeros((chans, cols), f32)
    sum_two = jnp.zeros((chans, cols), f32)
    for r in range(rows):
        x_local[r].wait()
        even, odd = xv[r, :, :cols].astype(f32), xv[r, :, cols:].astype(f32)
        sum_one = sum_one + (even + odd)
        sum_two = sum_two + (even * even + odd * odd)
    put_sums(stat, row_sums(sum_one, sum_two))

    stat_cp = [
        remote(stat, stat_in.at[d], send_sem.at[11], uv_recv.at[2], {"fsdp": peers_z[d]})
        for d in range(nz - 1)
    ]
    pl.semaphore_wait(barrier, nz - 1 + 3 + 1)
    for d in (1, 0, 2):
        stat_cp[d].start()

    split[...] = jnp.where(
        jnp.where(big_j < cols, 2 * big_j, 2 * (big_j - cols) + 1) == big_i, 1.0, 0.0
    ).astype(bf16)
    for k in range(3):
        same[:, k * wide : (k + 1) * wide] = same_one
    done(ctl.at[1], loc_sem.at[rows + 2])
    c_local[2].wait()
    w_local.wait()

    @pl.when(z == nz - 1)
    def _():
        halo_c.start()
        for to in (1, 2):
            for c in range(2):
                own_w(to, c).start()

    for r in range(rows):
        norm[r + 1] = dot(xv[r], split[...])
    eye_i = lax.broadcasted_iota(jnp.int32, (chans, chans), 0)
    eye_j = lax.broadcasted_iota(jnp.int32, (chans, chans), 1)
    eye = jnp.where(eye_i == eye_j, 1.0, 0.0)
    g_local.wait()
    gains = dot(eye, gv[...], ((1,), (1,)), HIGHEST)
    gain = jnp.broadcast_to(gains[:, 0:1], (chans, cols))
    shift = jnp.broadcast_to(gains[:, 1:2], (chans, cols))

    def block_taps(q):
        here = pl.ds(aligned(q * block), block)
        taps[here] = dot(wfull[q], ctl[1], ((0,), (0,)))

    block_taps(z)
    done(stat_in, uv_recv.at[2])

    @pl.when(z == 0)
    def _():
        for to in (2, 1):
            for c in range(2):
                own_w(to, c).start()

    @pl.when(inner)
    def _():
        halo_c.start()
        for to in (3 * (1 - pair), 3 - z, partner):
            for c in range(2):
                own_w(to, c).start()

    total = stat[...]
    for d in range(nz - 1):
        total = total + stat_in[d]
    sum_one, sum_two = group_sums(total)
    mean = sum_one / count
    rstd = 1.0 / jnp.sqrt(sum_two / count - mean * mean + 1e-05)
    slope = gain * rstd

    def put(row_tap, col_tap, i, lo, value):
        start = (3 * row_tap + col_tap) * chans + lo
        patches[start : start + value.shape[0], i * cols : (i + 1) * cols] = value

    step = 64

    def activate(r, users):
        for lo in range(0, chans, step):
            part_of = slice(lo, lo + step)
            for odd in range(2):
                here = pl.ds(odd * cols, cols)
                x_val = norm[r, part_of, here]
                z_val = (x_val - mean[part_of]) * slope[part_of] + shift[part_of]
                sig = 0.5 * jnp.tanh(0.5 * z_val) + 0.5
                act = z_val * sig
                dsilu[r - 1, part_of, here] = sig
                rounded = act.astype(bf16)
                for t, i in users:
                    put(t, 1 + odd, i, lo, rounded)
                if odd == 1:
                    moved = pltpu.roll(act, 1, axis=1)
                    moved = jnp.where(lane[part_of] == 0, 0.0, moved).astype(bf16)
                    for t, i in users:
                        put(t, 0, i, lo, moved)

    activate(2, [(2, 0), (0, 1)])
    activate(4, [(2, 1), (0, 0)])

    pl.when(z == nz - 2)(lambda: halo_c.wait_recv())

    def relay_w(c):
        spot = w_spot(others[0], yi, c)
        return remote(spot, spot, send_sem.at[1], w_recv.at[others[0], c], {"fsdp": partner})

    def w_arrive(j, c, role=None):
        def take():
            q = others[j]
            spot = w_spot(q, yi, c)
            remote(spot, spot, send_sem.at[1], w_recv.at[q, c], {"fsdp": partner}).wait_recv()
            if j == 0 and role is not outer:
                pl.when(inner)(lambda: relay_w(c).start())
            y_forward(j, c).start()
            c_forward(j, c).start()

        if role is None:
            take()
        else:
            pl.when(role)(take)

    def y_forward(j, c):
        spot = w_spot(others[j], yi, c)
        return remote(spot, spot, send_sem.at[2], y_recv.at[j, c], {"groups": 1 - yi})

    def c_forward(j, c):
        spot = w_spot(others[j], yi, c)
        return remote(spot, spot, send_sem.at[3], cd_recv.at[j], {"rep": core_peer})

    def d_forward(j, c):
        spot = w_spot(others[j], 1 - yi, c)
        return remote(spot, spot, send_sem.at[4], cd_recv.at[j], {"rep": core_peer})

    def w_second(j, c):
        y_forward(j, c).wait_recv()
        d_forward(j, c).start()

    def w_taps(j):
        rows_in = pl.ds(aligned(h_rows * (1 - ci)), h_rows)
        done(wfull.at[others[j], rows_in], cd_recv.at[j])
        block_taps(others[j])

    def core_copy(n, h):
        return remote(
            part.at[n, h, pl.ds(aligned(h_rows * (1 - ci)), h_rows)],
            core_in.at[n, h],
            send_sem.at[5],
            core_recv.at[n, h],
            {"rep": core_peer},
        )

    def x_copy(n, h):
        return remote(
            half.at[n, h, pl.ds(aligned(q_rows * (1 - xi)), q_rows)],
            x_in.at[n, h],
            send_sem.at[6],
            x_recv.at[n, h],
            {"rep": x_peer},
        )

    def z_copy(n, h):
        return remote(
            quarter.at[n, h],
            z_in.at[n, h],
            send_sem.at[7],
            z_recv.at[n, h],
            {"fsdp": partner},
        )

    def comb_copy(n, h):
        return remote(
            comb.at[n, h],
            z_in.at[3, h],
            send_sem.at[7],
            z_recv.at[3, h],
            {"fsdp": order[n]},
        )

    def weight_step(n, h):
        q, size = order[n], sizes[h]
        rhs = patches[pl.ds(aligned(q * block + h * lanes), size)]
        lhs = ctl[jnp.where(q == 0, 0, 1)]
        part[n, h, :, :size] = dot(lhs, rhs, ((1,), (1,))).astype(bf16)
        if h == 0 and n > 0:
            taken = 3 * chans - block

            @pl.when(q == 1)
            def _():
                rhs = patches[block : block + taken]
                part[n, h, :, :taken] = dot(ctl[0], rhs, ((1,), (1,))).astype(bf16)

        core_copy(n, h).start()

    def core_step(n, h):
        core_copy(n, h).wait_recv()
        mine_rows = part[n, h, pl.ds(aligned(h_rows * ci), h_rows)]
        half[n, h] = (mine_rows.astype(f32) + core_in[n, h].astype(f32)).astype(bf16)
        x_copy(n, h).start()

    def x_step(n, h):
        x_copy(n, h).wait_recv()
        mine_rows = half[n, h, pl.ds(aligned(q_rows * xi), q_rows)]
        quarter[n, h] = (mine_rows.astype(f32) + x_in[n, h].astype(f32)).astype(bf16)
        if n == 2:
            z_copy(n, h).start()
        elif n < 2:
            pl.when(outer)(lambda: z_copy(n, h).start())

    def comb_step(n, h):
        @pl.when(inner)
        def _():
            z_copy(n, h).wait_recv()
            value = quarter[n, h].astype(f32) + z_in[n, h].astype(f32)
            comb[n, h] = value.astype(bf16)
            comb_copy(n, h).start()

    def rep_copy(m, h):
        slot = (0, 2, 1)[m]
        src = final.at[h] if m < 2 else rep_in.at[h, 2]
        to = core_peer if m == 2 else reps[m]
        recv = rep_recv.at[1 if m == 1 else 0, h]
        return remote(src, rep_in.at[h, slot], send_sem.at[8], recv, {"rep": to})

    def place(ref, k, h):
        rows_k = pl.ds(aligned(q_rows * k), q_rows)
        wg_ref[rows_k, h * lanes : h * lanes + sizes[h]] = ref[:, : sizes[h]].astype(f32)

    def final_step(h):
        z_copy(2, h).wait_recv()
        comb_copy(1, h).wait_recv()
        value = quarter[3, h].astype(f32) + z_in[2, h].astype(f32) + z_in[3, h].astype(f32)
        final[h] = (value * scale).astype(bf16)
        rep_copy(1, h).start()
        rep_copy(0, h).start()

    owners = [2 * (1 - ci) + xi, 2 * (1 - ci) + 1 - xi, 2 * ci + 1 - xi]
    def relay_step(h):
        rep_copy(1, h).wait_recv()
        rep_copy(2, h).start()

    def first_places(h):
        place(final.at[h], mine, h)
        place(rep_in.at[h, 2], owners[2], h)

    def last_places(h):
        done(rep_in.at[h, pl.ds(0, 2)], rep_recv.at[0, h])
        for m in range(2):
            place(rep_in.at[h, m], owners[m], h)

    def gain_sums():
        done(uv_far, uv_recv.at[1])
        total = uv[...]
        for d in range(nz - 1):
            total = total + uv_in[d]
        for d in range(3 * nz):
            total = total + uv_far[d]
        gg_ref[...] = total * scale


    def prepare():
        for r in range(rows):
            for odd in range(2):
                here = pl.ds(odd * cols, cols)
                normed = (norm[r + 1, :, here] - mean) * rstd
                z_val = gain * normed + shift
                sig = dsilu[r, :, here]
                norm[r + 1, :, here] = normed
                dsilu[r, :, here] = sig * (1.0 + z_val * (1.0 - sig))

    w_lane = lax.broadcasted_iota(jnp.int32, (outs_ch, block), 1)
    top = 3 * chans - block
    upto, since = -(-top // 128) * 128, top // 128 * 128

    def top_maps():
        first = jnp.where(w_lane[:, :upto] < top, wfull[1, :, :upto].astype(f32), 0.0).astype(bf16)
        value = dot(wfull[0], patches[:block]) + dot(first, patches[block : block + upto])
        p_out[...] = value[:, :cols].astype(bf16)
        when_up(lambda: p_copy.start())
        return value[:, cols:]

    def low_maps(above):
        rest = wfull[1, :, since:].astype(f32)
        rest = jnp.where(w_lane[:, since:] < top, 0.0, rest).astype(bf16)
        value = dot(rest, patches[block + since : 2 * block])
        for q in range(2, nz):
            value = value + dot(wfull[q], patches[q * block : (q + 1) * block])
        out_ref[0, 1] = (value[:, cols:] + above).astype(bf16)
        return value[:, :cols]

    def join_maps(value):
        @pl.when(z == 0)
        def _():
            p_in[...] = jnp.zeros(p_in.shape, bf16)

        when_down(lambda: p_copy.wait_recv())
        out_ref[0, 0] = (value + p_in[...].astype(f32)).astype(bf16)

    def edge_taps():
        @pl.when(z < nz - 1)
        def _():
            below = ctl[0, :, :cols]
            edge[:block] = dot(wfull[0], below, ((0,), (0,)))
            edge[block:] = dot(wfull[1, :, :top], below, ((0,), (0,)))

        @pl.when(z == nz - 1)
        def _():
            edge[...] = jnp.zeros(edge.shape, f32)

    def tap_at(row_tap, col_tap, i):
        tap = 3 * row_tap + col_tap
        here = slice(tap * chans, (tap + 1) * chans)
        if i == 2:
            return edge[here]
        return taps[here, i * cols : (i + 1) * cols]

    uv_cp = [
        remote(uv, uv_in.at[d], send_sem.at[9], uv_recv.at[0], {"fsdp": peers_z[d]})
        for d in range(nz - 1)
    ]

    far_cp = [
        remote(
            uv,
            uv_far.at[3 * d + m],
            send_sem.at[10],
            uv_recv.at[1],
            {"fsdp": lax.rem(z + d, nz), "rep": reps[m]},
        )
        for d in (2, 1, 3, 0)
        for m in range(3)
    ]

    def channel_sums():
        u_sum = jnp.zeros((chans, cols), f32)
        v_sum = jnp.zeros((chans, cols), f32)
        for r in range(rows):
            pairs = [(t, i) for i in range(3) for t in range(3) if 2 * i + t == r + 1]
            for odd in range(2):
                here = pl.ds(odd * cols, cols)
                grad = sum(tap_at(t, 1 + odd, i) for t, i in pairs)
                if odd == 1:
                    left = sum(tap_at(t, 0, i) for t, i in pairs)
                    moved = pltpu.roll(left, cols - 1, axis=1)
                    grad = grad + jnp.where(lane == cols - 1, 0.0, moved)
                value = grad * dsilu[r, :, here]
                zgrad[r, :, here] = value
                u_sum = u_sum + value * norm[r + 1, :, here]
                v_sum = v_sum + value
        put_sums(uv, row_sums(u_sum, v_sum))
        for d in (1, 0, 2):
            uv_cp[d].start()

    def input_grads():
        done(uv_in, uv_recv.at[0])
        total = uv[...]
        for d in range(nz - 1):
            total = total + uv_in[d]
        su_val, sv_val = group_sums(gv[0:1] * total)
        su_val, sv_val = su_val / count, sv_val / count
        merge = jnp.where(
            jnp.where(big_i < cols, 2 * big_i, 2 * (big_i - cols) + 1) == big_j, 1.0, 0.0
        ).astype(bf16)
        def grad_row(r):
            for odd in range(2):
                here = pl.ds(odd * cols, cols)
                value = rstd * (gain * zgrad[r, :, here] - sv_val - norm[r + 1, :, here] * su_val)
                patches[r * chans : (r + 1) * chans, here] = value.astype(bf16)
            dx_ref[0, r] = dot(patches[r * chans : (r + 1) * chans], merge).astype(bf16)

        relay_step(2)
        first_places(2)
        grad_row(0)
        grad_row(1)
        grad_row(2)
        grad_row(3)

    def halo_wait():
        pl.when(z < nz - 2)(lambda: halo_c.wait_recv())

    def drain():
        own = wfull.at[0, pl.ds(0, q_rows)]
        three = wfull.at[0, pl.ds(0, 3 * q_rows)]

        done(stat_in, send_sem.at[11])
        when_down(lambda: halo_c.wait_send())
        pl.when(outer)(lambda: done(wfull.at[0, pl.ds(0, 2 * q_rows)], send_sem.at[0]))

        @pl.when(inner)
        def _():
            done(three, send_sem.at[0])
            done(own, send_sem.at[1])

        for k in (2, 3, 4):
            done(three, send_sem.at[k])
        done(half, send_sem.at[5])
        done(quarter, send_sem.at[6])
        done(comb, send_sem.at[7])

    weight_step(0, 0)
    weight_step(0, 1)
    weight_step(0, 2)
    activate(1, [(1, 0)])
    activate(3, [(1, 1)])
    weight_step(1, 0)
    core_step(0, 0)
    weight_step(1, 1)
    core_step(0, 1)
    weight_step(1, 2)
    core_step(0, 2)
    core_step(1, 0)
    w_arrive(0, 0)
    core_step(1, 1)
    w_arrive(0, 1, inner)
    halo_wait()
    weight_step(2, 0)
    core_step(1, 2)
    weight_step(2, 1)
    weight_step(2, 2)
    weight_step(3, 0)
    weight_step(3, 1)
    x_step(0, 0)
    weight_step(3, 2)
    w_arrive(0, 1, outer)
    w_arrive(1, 0)
    x_step(0, 1)
    prepare()
    core_step(2, 0)
    core_step(2, 1)
    core_step(2, 2)
    x_step(0, 2)
    w_arrive(1, 1)
    w_second(0, 0)
    x_step(1, 0)
    core_step(3, 0)
    w_second(0, 1)
    core_step(3, 1)
    core_step(3, 2)
    w_arrive(2, 0)
    x_step(1, 1)
    w_arrive(2, 1)
    comb_step(0, 0)
    x_step(1, 2)
    comb_step(0, 1)
    w_second(1, 0)
    comb_step(0, 2)
    w_second(1, 1)
    x_step(2, 0)
    w_taps(0)
    comb_step(1, 0)
    x_step(2, 1)
    w_second(2, 0)
    comb_step(1, 1)
    w_taps(1)
    w_second(2, 1)
    x_step(2, 2)
    edge_taps()
    x_step(3, 0)
    comb_step(1, 2)
    x_step(3, 1)
    w_taps(2)
    final_step(0)
    x_step(3, 2)
    channel_sums()
    final_step(1)
    final_step(2)
    for cp in far_cp:
        cp.start()
    above = top_maps()
    low = low_maps(above)
    drain()
    relay_step(0)
    relay_step(1)
    first_places(0)
    first_places(1)
    input_grads()
    join_maps(low)

    last_places(0)
    last_places(1)
    last_places(2)
    gain_sums()

    when_up(lambda: p_copy.wait_send())
    done(uv_in, send_sem.at[9])
    done(uv_far, send_sem.at[10])
    done(rep_in, send_sem.at[8])


def write_out(*refs):
    n = len(refs) // 2
    sems = refs[-1]
    copies = [pltpu.make_async_copy(refs[i], refs[n + i], sems.at[i]) for i in range(n)]
    for cp in copies:
        cp.start()
    for cp in copies:
        cp.wait()


def in_hbm(value):
    return pltpu.with_memory_space_constraint(value, pltpu.HBM)


def fused_shards(images, gains, conv_weight, cotangent):
    batch, rows, width, chans = images.shape
    block, outs_ch = conv_weight.shape
    nz = lax.axis_size("fsdp")
    fits = (batch, rows, cotangent.shape[1]) == (1, 4, 2) and chans % 64 == 0 and width == 256
    if not fits or block % 16 or outs_ch % 64 or nz * block != 9 * chans:
        return shards(images, gains, conv_weight, cotangent)
    if not block < 3 * chans < 2 * block or 3 * chans - block > 256:
        return shards(images, gains, conv_weight, cotangent)
    cols = width // 2
    q_rows = outs_ch // 4
    lanes = 256
    pieces = -(-block // lanes)
    wide = -(-chans // 128) * 128
    f32, bf16 = jnp.float32, jnp.bfloat16
    vmem = pltpu.VMEM
    dma = pltpu.SemaphoreType.DMA
    shapes = (
        jax.ShapeDtypeStruct((batch, rows // 2, outs_ch, cols), bf16),
        jax.ShapeDtypeStruct((batch, rows, chans, width), bf16),
        jax.ShapeDtypeStruct((outs_ch, block), f32),
        jax.ShapeDtypeStruct(gains.shape, f32),
    )
    results = pl.pallas_call(
        functools.partial(fused, nz),
        out_shape=tuple(vmem(shape.shape, shape.dtype) for shape in shapes),
        in_specs=[pl.BlockSpec(memory_space=pltpu.HBM)] * 4,
        out_specs=[pl.BlockSpec(memory_space=vmem)] * 4,
        scratch_shapes=[
            vmem((rows, chans, width), bf16),
            vmem(gains.shape, f32),
            vmem((2, outs_ch, width), bf16),
            vmem((width, width), bf16),
            vmem((chans, 3 * wide), bf16),
            vmem((outs_ch, cols), bf16),
            vmem((outs_ch, cols), bf16),
            vmem((rows + 1, chans, width), f32),
            vmem((rows, chans, width), f32),
            vmem((rows, chans, width), f32),
            vmem((nz * block, width), bf16),
            vmem((nz * block, width), f32),
            vmem((3 * chans, cols), f32),
            vmem((nz, outs_ch, block), bf16),
            vmem(gains.shape, f32),
            vmem((nz - 1,) + gains.shape, f32),
            vmem((nz, pieces, outs_ch, lanes), bf16),
            vmem((nz, pieces, 2 * q_rows, lanes), bf16),
            vmem((nz, pieces, 2 * q_rows, lanes), bf16),
            vmem((nz, pieces, q_rows, lanes), bf16),
            vmem((nz, pieces, q_rows, lanes), bf16),
            vmem((4, pieces, q_rows, lanes), bf16),
            vmem((3, pieces, q_rows, lanes), bf16),
            vmem((pieces, q_rows, lanes), bf16),
            vmem((pieces, 3, q_rows, lanes), bf16),
            vmem(gains.shape, f32),
            vmem((nz - 1,) + gains.shape, f32),
            vmem((3 * nz,) + gains.shape, f32),
            dma((rows + 4,)),
            dma((2, 2)),
            dma((12,)),
            dma((nz, 2)),
            dma((3, 2)),
            dma((3,)),
            dma((nz, pieces)),
            dma((nz, pieces)),
            dma((4, pieces)),
            dma((2, pieces)),
            dma((3,)),
        ],
        compiler_params=pltpu.CompilerParams(
            collective_id=0, has_side_effects=True, vmem_limit_bytes=48 * 1024 * 1024
        ),
    )(
        in_hbm(jnp.swapaxes(images, 2, 3)),
        in_hbm(gains),
        in_hbm(conv_weight.T),
        in_hbm(jnp.swapaxes(cotangent, 2, 3)),
    )
    output_maps, input_grad, weight_grad, gain_grad = pl.pallas_call(
        write_out,
        out_shape=shapes,
        in_specs=[pl.BlockSpec(memory_space=vmem)] * 4,
        out_specs=[pl.BlockSpec(memory_space=pltpu.HBM)] * 4,
        scratch_shapes=[dma((4,))],
        compiler_params=pltpu.CompilerParams(vmem_limit_bytes=1024 * 1024),
    )(*(pltpu.with_memory_space_constraint(value, vmem) for value in results))
    return (
        jnp.swapaxes(output_maps, 2, 3),
        jnp.swapaxes(input_grad, 2, 3),
        weight_grad.T,
        gain_grad,
    )


def solution(mesh):
    in_specs = (
        P(("groups", "rep"), "fsdp", None, None),
        P(),
        P("fsdp", None),
        P(("groups", "rep"), "fsdp", None, None),
    )
    out_specs = (
        P(("groups", "rep"), "fsdp", None, None),
        P(("groups", "rep"), "fsdp", None, None),
        P(("groups", "fsdp"), None),
        P("groups", None),
    )
    small = mesh.shape["groups"] == 2 and mesh.shape["rep"] == 4 and mesh.shape["fsdp"] == 4
    body = fused_shards if small else shards
    return jax.shard_map(body, mesh=mesh, in_specs=in_specs, out_specs=out_specs, check_vma=False)
```
